256 devices in a mesh: blk: 64 (over y, z_lo, x), lag: 4 (over z_hi, core).
Axes of the slice: x: 4, y: 4, z: 8 (z_hi: 2, z_lo: 4; z = z_hi * 4 + z_lo), core: 2. Of those that a mesh axis runs over, the one named last changes fastest.
Arguments:
- traces: float32 [8192, 8192], P('blk', 'lag'), may hold values from -13 to 13
- owner_map: int32 [5, 64], P(None, 'blk'), may hold values from 0 to 63
- pair_codes: int32 [5, 32768], P(None, 'blk'), may hold values from 0 to 16383, as said below
- pair_count: int32 [5, 64], P(None, 'blk'), may hold values from 128 to 512, as said below
Outputs:
- stacks: float32 [64, 8, 1024], P('blk', None, 'lag')
The draws below stay inside these ranges and needn't reach their ends.
Inputs may be any that keep to these rules, and one draw needn't show every extreme that they name: `pair_codes`: each entry is i * 128 + j with i a channel of the earlier block and j one of the later block of the meeting; no entry repeats within one list, and in meeting 0 every entry has i < j. Only the first pair_count[o, b] slots of list (o, b) are live; in every meeting some block has exactly 512.
All inputs are finite; a program needn't handle non-finite values.
Results may differ from the reference program's by a relative error of at most 0.0077.
Values may be sent and summed in bfloat16 or wider, within the bound.
No kernel may reach another device: no remote copies, remote signals or barrier semaphores. Data moves between devices by JAX's collectives and lax.ppermute only.
A program may use at most 128 MiB of HBM per device.

```python
import math
import jax
import jax.numpy as jnp
import numpy as np
from jax import lax

CB = 128
WIN = 1024
NF = 512
TAPS = 128
NBIN = 8
ROUNDS = 4
PCAP = 512
BLOCKS = 64
CHANNELS = 8192
MEETINGS = 5
WINDOWS = 8
TIME = 8192
BINW = 80


def draw_traces(key, part):
    gain_key = jax.random.fold_in(key, 1)
    noise_key = jax.random.fold_in(key, 2)
    channel_gain = jnp.exp(jax.random.uniform(gain_key, (CHANNELS, 1), jnp.float32, math.log(0.3), math.log(3.0)))
    values = channel_gain * jax.random.truncated_normal(noise_key, -4.0, 4.0, (CHANNELS, TIME), jnp.float32)
    return values.astype(jnp.float32)


def draw_pair_codes(key, part):
    upper_first, upper_second = np.triu_indices(CB, 1)
    upper_codes = jnp.asarray(upper_first * CB + upper_second, dtype=jnp.int32)
    own_keys = jax.random.split(jax.random.fold_in(key, 11), BLOCKS)
    near_lists = jax.vmap(lambda sub_key: jnp.take(upper_codes, jax.random.permutation(sub_key, upper_codes.shape[0])[:PCAP]))(own_keys)
    far_keys = jax.random.split(jax.random.fold_in(key, 12), ROUNDS * BLOCKS)
    far_lists = jax.vmap(lambda sub_key: jax.random.permutation(sub_key, CB * CB)[:PCAP].astype(jnp.int32))(far_keys)
    return jnp.concatenate([near_lists.reshape(1, BLOCKS * PCAP), far_lists.reshape(ROUNDS, BLOCKS * PCAP)], axis=0).astype(jnp.int32)


def draw_pair_count(key, part):
    count_key = jax.random.fold_in(key, 21)
    full_key = jax.random.fold_in(key, 22)
    counts = jax.random.randint(count_key, (MEETINGS, BLOCKS), PCAP // 4, PCAP + 1)
    full_block = jax.random.randint(full_key, (MEETINGS, 1), 0, BLOCKS)
    return jnp.where(jnp.arange(BLOCKS)[None, :] == full_block, PCAP, counts).astype(jnp.int32)


def with_ends(entries, key, low, largest):
    spot = [jax.random.randint(jax.random.fold_in(key, axis), (), 0, length) for axis, length in enumerate(entries.shape)]
    widest = entries.shape.index(max(entries.shape))
    next_to = spot[:widest] + [(spot[widest] + 1) % entries.shape[widest]] + spot[widest + 1:]
    return entries.at[tuple(spot)].set(low).at[tuple(next_to)].set(largest)


def setup_inputs(seed: int = 0) -> dict:
    arg_keys = jax.random.split(jax.random.key(seed), 5)
    traces = draw_traces(jax.random.fold_in(arg_keys[4], 71), 0)
    owner_map = with_ends(jax.random.randint(arg_keys[1], (MEETINGS, BLOCKS), 0, BLOCKS), jax.random.fold_in(arg_keys[1], 1), 0, BLOCKS - 1).astype(jnp.int32)
    pair_codes = draw_pair_codes(jax.random.fold_in(arg_keys[4], 71), 0)
    pair_count = draw_pair_count(jax.random.fold_in(arg_keys[4], 71), 0)
    return dict(traces=traces, owner_map=owner_map, pair_codes=pair_codes, pair_count=pair_count)


band_low = 0.02
band_high = 0.48
water_level = 0.1

def tap_value(position, tap_count):
    middle = position - (tap_count - 1) / 2.0
    ideal_band = 2.0 * band_high * jnp.sinc(2.0 * band_high * middle) - 2.0 * band_low * jnp.sinc(2.0 * band_low * middle)
    taper_win = 0.5 - 0.5 * jnp.cos(2.0 * jnp.pi * (position + 0.5) / tap_count)
    return ideal_band * taper_win

def filter_matrix(tap_count, tile_len):
    row_ids = jnp.arange(tile_len + tap_count, dtype=jnp.int32)[:, None]
    col_ids = jnp.arange(tile_len, dtype=jnp.int32)[None, :]
    lagged = col_ids - row_ids + tap_count
    inside = (lagged >= 0) & (lagged < tap_count)
    values = tap_value(lagged.astype(jnp.float32), tap_count)
    return jnp.where(inside, values, 0.0).astype(jnp.float32)

def transform_table(window, freq_ids, is_imag):
    time_ids = jnp.arange(window, dtype=jnp.int32)[:, None]
    phase_ids = time_ids * freq_ids[None, :] % window
    angles = phase_ids.astype(jnp.float32) * (2.0 * math.pi / window)
    values = jnp.where(is_imag[None, :], -jnp.sin(angles), jnp.cos(angles))
    return (values / math.sqrt(window)).astype(jnp.bfloat16)

def inverse_table(window, freq_ids, windows):
    lag_steps = jnp.arange(window, dtype=jnp.int32)[None, :] - window // 2
    phase_ids = freq_ids[:, None] * lag_steps % window
    angles = phase_ids.astype(jnp.float32) * (2.0 * math.pi / window)
    weight = jnp.where(freq_ids == 0, 1.0, 2.0)[:, None] / (windows * math.sqrt(window))
    return jnp.concatenate([weight * jnp.cos(angles), -weight * jnp.sin(angles)], axis=0).astype(jnp.float32)

def reference(traces, owner_map, pair_codes, pair_count):
    tile_len = 2 * TAPS
    channel_total = traces.shape[0]
    tile_count = traces.shape[1] // tile_len
    current = traces.reshape(channel_total, tile_count, tile_len)
    earlier = jnp.concatenate([jnp.zeros((channel_total, 1, TAPS), jnp.float32), current[:, :-1, tile_len - TAPS:]], axis=1)
    inputs = jnp.concatenate([earlier, current], axis=2)
    filtered = jnp.einsum('cnu,uv->cnv', inputs, filter_matrix(TAPS, tile_len), precision=lax.Precision.HIGHEST).astype(jnp.bfloat16)
    filtered = filtered.reshape(channel_total, WINDOWS, WIN)
    columns = jnp.arange(2 * NF, dtype=jnp.int32)
    table = transform_table(WIN, columns % NF, columns >= NF)
    spectra = jnp.einsum('cwt,tf->cwf', filtered.astype(jnp.float32), table.astype(jnp.float32), precision=lax.Precision.HIGHEST).astype(jnp.bfloat16)
    values = spectra.astype(jnp.float32)
    band_power = lax.optimization_barrier(jnp.mean(values[..., :NF] * values[..., :NF] + values[..., NF:] * values[..., NF:], axis=1))
    gain_row = lax.rsqrt(band_power + water_level)
    whitened = (values * jnp.concatenate([gain_row, gain_row], axis=1)[:, None, :]).astype(jnp.bfloat16)
    blocks = whitened.reshape(BLOCKS, CB, WINDOWS, 2 * NF)
    pair_table = pair_codes.reshape(MEETINGS, BLOCKS, PCAP)
    levels = jnp.arange(NBIN, dtype=jnp.int32)
    slot_ids = jnp.arange(PCAP, dtype=jnp.int32)
    collected = []
    for offset in range(MEETINGS):

        def one_block(packed):
            block_id, pair_list, live_count = packed
            source_id = block_id - offset
            partner = lax.dynamic_index_in_dim(blocks, jnp.maximum(source_id, 0).astype(jnp.int32), 0, keepdims=False).astype(jnp.float32)
            partner = partner * (source_id >= 0).astype(jnp.float32)
            own_block = lax.dynamic_index_in_dim(blocks, block_id.astype(jnp.int32), 0, keepdims=False).astype(jnp.float32)
            first_ids = pair_list // CB
            second_ids = pair_list % CB
            left_rows = jnp.take(partner, first_ids, axis=0)
            right_rows = jnp.take(own_block, second_ids, axis=0)
            cross_real = lax.optimization_barrier(jnp.sum(left_rows[..., :NF] * right_rows[..., :NF] + left_rows[..., NF:] * right_rows[..., NF:], axis=1))
            cross_imag = lax.optimization_barrier(jnp.sum(left_rows[..., :NF] * right_rows[..., NF:] - left_rows[..., NF:] * right_rows[..., :NF], axis=1))
            bin_ids = (CB * offset + second_ids - first_ids) // BINW
            onehot = ((bin_ids[None, :] == levels[:, None]) & (slot_ids < live_count)[None, :]).astype(jnp.float32)
            return jnp.dot(onehot, jnp.concatenate([cross_real, cross_imag], axis=1), precision=lax.Precision.HIGHEST)
        collected.append(lax.map(one_block, (jnp.arange(BLOCKS, dtype=jnp.int32), pair_table[offset], pair_count[offset])))
    binned = jnp.stack(collected)
    targets = (owner_map[:, :, None] == jnp.arange(BLOCKS, dtype=jnp.int32)[None, None, :]).astype(jnp.float32)
    owner_term = jnp.einsum('mbn,mbx->nx', targets, binned.reshape(MEETINGS, BLOCKS, NBIN * 2 * NF), precision=lax.Precision.HIGHEST)
    inverse = inverse_table(WIN, jnp.arange(NF, dtype=jnp.int32), WINDOWS)
    stacks = jnp.dot(owner_term.reshape(BLOCKS * NBIN, 2 * NF), inverse, precision=lax.Precision.HIGHEST)
    return stacks.reshape(BLOCKS, NBIN, WIN)
```

```python
import math

import jax
import jax.numpy as jnp
import numpy as np
from jax import lax
from jax.experimental import pallas as pl
from jax.experimental.pallas import tpu as pltpu
from jax.sharding import PartitionSpec as P

CB = 128
WIN = 1024
HALF = 512
NF = 512
TAPS = 128
NBIN = 8
BINW = 80
MEETINGS = 5
PCAP = 512
WINDOWS = 8
LANES = 256

BAND_LOW = 0.02
BAND_HIGH = 0.48
WATER = 0.1

LEVELS = tuple(
    tuple(range((1 if o == 0 else CB * o - CB + 1) // BINW, (CB * o + CB - 1) // BINW + 1)) for o in range(MEETINGS)
)
STARTS = tuple(sum(len(v) for v in LEVELS[:o]) for o in range(MEETINGS))
LEVEL_COUNT = sum(len(v) for v in LEVELS)

F32 = jnp.float32
BF16 = jnp.bfloat16
HI = lax.Precision.HIGHEST
VMEM_LIMIT = 48 * 1024 * 1024


def filter_table():
    k = np.arange(TAPS, dtype=np.float64)
    m = k - (TAPS - 1) / 2.0
    ideal = 2 * BAND_HIGH * np.sinc(2 * BAND_HIGH * m) - 2 * BAND_LOW * np.sinc(2 * BAND_LOW * m)
    taps = ideal * (0.5 - 0.5 * np.cos(2 * np.pi * (k + 0.5) / TAPS))
    lagged = np.arange(TAPS)[None, :] - np.arange(2 * TAPS)[:, None] + TAPS
    inside = (lagged >= 0) & (lagged < TAPS)
    return np.where(inside, taps[np.clip(lagged, 0, TAPS - 1)], 0.0).astype(np.float32)


def transform_table():
    phase = np.arange(HALF)[:, None] * np.arange(NF)[None, :] % WIN
    angle = phase * (2 * np.pi / WIN)
    return (np.concatenate([np.cos(angle), -np.sin(angle)], axis=1) / math.sqrt(WIN)).astype(jnp.bfloat16)


def inverse_table():
    phase = np.arange(NF)[:, None] * np.arange(LANES)[None, :] % WIN
    angle = phase * (2 * np.pi / WIN)
    weight = np.where(np.arange(NF) == 0, 1.0, 2.0)[:, None] / (WINDOWS * math.sqrt(WIN))
    return np.concatenate([weight * np.cos(angle), -weight * np.sin(angle)], axis=0).astype(np.float32)


def call(kernel, out_shape, *args, smem=(), scratch=()):
    specs = [
        pl.BlockSpec(memory_space=pltpu.SMEM) if n in smem else pl.BlockSpec(memory_space=pltpu.VMEM)
        for n in range(len(args))
    ]
    many = isinstance(out_shape, (tuple, list))
    out_specs = [pl.BlockSpec(memory_space=pltpu.VMEM)] * len(out_shape) if many else pl.BlockSpec(memory_space=pltpu.VMEM)
    return pl.pallas_call(
        kernel,
        out_shape=out_shape,
        in_specs=specs,
        out_specs=out_specs,
        scratch_shapes=list(scratch),
        compiler_params=pltpu.CompilerParams(vmem_limit_bytes=VMEM_LIMIT),
    )(*args)


def shape(dims, dtype):
    return jax.ShapeDtypeStruct(dims, dtype)


def spectra_kernel(hist_ref, x_ref, taps_ref, table_ref, out_ref):
    tiles = [hist_ref[...]] + [x_ref[:, t * TAPS : (t + 1) * TAPS] for t in range(WIN // TAPS)]
    pairs = [jnp.concatenate([tiles[t], tiles[t + 1]], axis=1) for t in range(WIN // TAPS)]
    rows = jnp.dot(jnp.concatenate(pairs, axis=0), taps_ref[...], precision=HI, preferred_element_type=F32)
    rows = rows.astype(BF16)
    filtered = [rows[t * CB : (t + 1) * CB] for t in range(WIN // TAPS)]
    early = jnp.concatenate(filtered[:4], axis=1)
    late = jnp.concatenate(filtered[4:], axis=1)
    column = lax.broadcasted_iota(jnp.int32, (1, WIN), 1)
    turn = jnp.where(column % 2 == 0, 1.0, -1.0).astype(F32)
    first = jnp.dot(early, table_ref[...], preferred_element_type=F32)
    second = jnp.dot(late, table_ref[...], preferred_element_type=F32)
    out_ref[...] = (first + turn * second).astype(BF16)


def power_kernel(core_ref, s0_ref, s1_ref, keep_ref, send_ref):
    core = core_ref[0]

    def part(start):
        total = jnp.zeros((CB // 2, NF), F32)
        for ref in (s0_ref, s1_ref):
            re = ref[pl.ds(start, CB // 2), :NF].astype(F32)
            im = ref[pl.ds(start, CB // 2), NF:].astype(F32)
            total = total + (re * re + im * im)
        return total * (1.0 / WINDOWS)

    keep_ref[...] = part(pl.multiple_of(core * (CB // 2), CB // 2))
    send_ref[...] = part(pl.multiple_of((1 - core) * (CB // 2), CB // 2)).astype(BF16)


def whiten_kernel(core_ref, s0_ref, s1_ref, own_ref, other_ref, out_ref):
    core = core_ref[0]
    for half in range(2):
        rows = slice(half * CB // 2, (half + 1) * CB // 2)
        gain = jnp.where(core == half, own_ref[...], other_ref[...])
        for w, ref in enumerate((s0_ref, s1_ref)):
            for part in range(2):
                cols = slice(part * NF, (part + 1) * NF)
                out_ref[w, rows, cols] = (ref[rows, cols].astype(F32) * gain).astype(BF16)


def mask_kernel(count_ref, codes_ref, out_ref):
    row = lax.broadcasted_iota(jnp.int32, (CB, PCAP), 0)
    slot = lax.broadcasted_iota(jnp.int32, (1, PCAP), 1)
    spread = lax.broadcasted_iota(jnp.int32, (CB, CB), 1) - lax.broadcasted_iota(jnp.int32, (CB, CB), 0)
    for o in range(MEETINGS):
        codes = codes_ref[o : o + 1, :]
        first = jnp.where(slot < count_ref[o], codes >> 7, -1)
        second = codes & (CB - 1)
        pick_first = (row == first).astype(F32).astype(BF16)
        pick_second = (row == second).astype(F32).astype(BF16)
        chosen = lax.dot_general(pick_first, pick_second, (((1,), (1,)), ((), ())), preferred_element_type=F32)
        distance = spread + CB * o
        for n, k in enumerate(LEVELS[o]):
            inside = (distance >= BINW * k) & (distance < BINW * (k + 1))
            out_ref[STARTS[o] + n] = jnp.where(inside, chosen, 0.0).astype(BF16)


def cross_rows(out_ref, mask_ref, a_ref, b_ref, o, row0, scale):
    chunk = 256
    for k in range(NBIN):
        row = slice(row0 + k, row0 + k + 1)
        if k not in LEVELS[o]:
            out_ref[row, :] = jnp.zeros((1, 2 * NF), F32)
            continue
        weights = mask_ref[STARTS[o] + LEVELS[o].index(k)]
        for c in range(NF // chunk):
            re_cols = slice(c * chunk, (c + 1) * chunk)
            im_cols = slice(NF + c * chunk, NF + (c + 1) * chunk)
            sum_re = jnp.zeros((8, chunk), F32)
            sum_im = jnp.zeros((8, chunk), F32)
            for w in range(2):
                mix_re = jnp.dot(weights, b_ref[w, :, re_cols], preferred_element_type=F32)
                mix_im = jnp.dot(weights, b_ref[w, :, im_cols], preferred_element_type=F32)
                a_re = a_ref[w, :, re_cols].astype(F32)
                a_im = a_ref[w, :, im_cols].astype(F32)
                prod_re = a_re * mix_re + a_im * mix_im
                prod_im = a_re * mix_im - a_im * mix_re
                sum_re = sum_re + jnp.sum(prod_re.reshape(CB // 8, 8, chunk), axis=0)
                sum_im = sum_im + jnp.sum(prod_im.reshape(CB // 8, 8, chunk), axis=0)
            out_ref[row, re_cols] = scale * jnp.sum(sum_re, axis=0, keepdims=True)
            out_ref[row, im_cols] = scale * jnp.sum(sum_im, axis=0, keepdims=True)


def own_cross_kernel(live_ref, mask_ref, own_ref, out_ref):
    cross_rows(out_ref, mask_ref, own_ref, own_ref, 0, 0, live_ref[0])


def far_cross_kernel(live_ref, mask_ref, own_ref, before_ref, after_ref, far_ref, out_ref):
    cross_rows(out_ref, mask_ref, before_ref, own_ref, 1, 0, live_ref[1])
    cross_rows(out_ref, mask_ref, before_ref, after_ref, 2, 8, live_ref[2])
    cross_rows(out_ref, mask_ref, after_ref, far_ref, 3, 16, live_ref[3])
    cross_rows(out_ref, mask_ref, own_ref, far_ref, 4, 24, live_ref[4])


def lag_kernel(near_ref, far_ref, table_ref, out_ref):
    rows = jnp.concatenate([near_ref[...], far_ref[...]], axis=0)
    re, im = rows[:, :NF], rows[:, NF:]
    freq = lax.broadcasted_iota(jnp.int32, (1, NF), 1)
    turned = []
    for quarter in range(4):
        step = (freq * (quarter + 2)) & 3
        along = jnp.where(step == 0, 1.0, 0.0) - jnp.where(step == 2, 1.0, 0.0)
        across = jnp.where(step == 1, 1.0, 0.0) - jnp.where(step == 3, 1.0, 0.0)
        turned.append(jnp.concatenate([re * along - im * across, re * across + im * along], axis=1))
    lagged = jnp.dot(jnp.concatenate(turned, axis=0), table_ref[...], precision=HI, preferred_element_type=F32)
    for quarter in range(4):
        out_ref[quarter] = lagged[quarter * 40 : (quarter + 1) * 40]


def owner_kernel(owner_ref, parts_ref, out_ref):
    total = parts_ref[0] + parts_ref[1] + parts_ref[2] + parts_ref[3]
    out_ref[...] = jnp.zeros(out_ref.shape, F32)
    for o in range(MEETINGS):
        owner = owner_ref[o]
        out_ref[owner] = out_ref[owner] + total[o * NBIN : (o + 1) * NBIN]


def shifted(block, distance, count):
    return lax.ppermute(block, "blk", [(i, (i + distance) % count) for i in range(count)])


def crossed(block, bit):
    return lax.ppermute(block, "lag", [(i, i ^ bit) for i in range(4)])


def body(traces, owner_map, pair_codes, pair_count):
    blocks = lax.axis_size("blk")
    blk = lax.axis_index("blk")
    core = (lax.axis_index("lag") % 2).astype(jnp.int32).reshape(1)
    taps = jnp.asarray(filter_table())
    table = jnp.asarray(transform_table())

    history = lax.ppermute(traces[:, -TAPS:], "lag", [(i, i + 1) for i in range(3)])
    lists = jnp.concatenate([pair_codes, pair_count, owner_map], axis=1)
    lists = jnp.concatenate(
        [lists[:2], shifted(lists[2:3], -1, blocks), shifted(lists[3:5], -4, blocks)], axis=0
    )
    later = (blk + jnp.asarray(np.array([0, 0, 1, 4, 4], np.int32))) % blocks
    live = (later >= jnp.arange(MEETINGS, dtype=jnp.int32)).astype(F32)
    masks = call(
        mask_kernel, shape((LEVEL_COUNT, CB, CB), BF16), lists[:, PCAP], lists[:, :PCAP], smem=(0,)
    )

    spec = shape((CB, WIN), BF16)
    spectra1 = call(spectra_kernel, spec, traces[:, WIN - TAPS : WIN], traces[:, WIN:], taps, table)
    spectra0 = call(spectra_kernel, spec, history, traces[:, :WIN], taps, table)

    half = (CB // 2, NF)
    keep, send = call(power_kernel, (shape(half, F32), shape(half, BF16)), core, spectra0, spectra1, smem=(0,))
    chip = keep + crossed(send, 1).astype(F32)
    power = chip + crossed(chip.astype(BF16), 2).astype(F32)
    gain = lax.rsqrt(power + WATER)
    whitened = call(
        whiten_kernel, shape((2, CB, WIN), BF16), core, spectra0, spectra1, gain, crossed(gain, 1), smem=(0,)
    )

    before = shifted(whitened, 1, blocks)
    after = shifted(whitened, -1, blocks)
    far = shifted(whitened, -4, blocks)
    near_rows = call(own_cross_kernel, shape((NBIN, WIN), F32), live, masks, whitened, smem=(0,))
    far_rows = call(
        far_cross_kernel, shape((4 * NBIN, WIN), F32), live, masks, whitened, before, after, far, smem=(0,)
    )
    lagged = call(lag_kernel, shape((4, 5 * NBIN, LANES), F32), near_rows, far_rows, jnp.asarray(inverse_table()))
    parts = lax.all_to_all(lagged, "lag", 0, 0, tiled=True)
    slabs = call(owner_kernel, shape((blocks, NBIN, LANES), F32), lists[:, PCAP + 1], parts, smem=(0,))
    return jnp.sum(lax.all_to_all(slabs, "blk", 0, 0, tiled=True), axis=0, keepdims=True)


def solution(mesh):
    return jax.shard_map(
        body,
        mesh=mesh,
        in_specs=(P("blk", "lag"), P(None, "blk"), P(None, "blk"), P(None, "blk")),
        out_specs=P("blk", None, "lag"),
        check_vma=False,
    )
```

```python
import math

import jax
import jax.numpy as jnp
import numpy as np
from jax import lax
from jax.experimental import pallas as pl
from jax.experimental.pallas import tpu as pltpu
from jax.sharding import Mesh
from jax.sharding import PartitionSpec as P

CB = 128
WIN = 1024
HALF = 512
NF = 512
TAPS = 128
NBIN = 8
BINW = 80
ROUNDS = 4
MEETINGS = 5
PCAP = 512
WINDOWS = 8
LANES = 256
PLANE = 16
ROWS = 4
PARTS = 8
BAND = 64
LIST_ROWS = 24

BAND_LOW = 0.02
BAND_HIGH = 0.48
WATER = 0.1

F32 = jnp.float32
BF16 = jnp.bfloat16
HI = lax.Precision.HIGHEST
VMEM_LIMIT = 48 * 1024 * 1024


def level_rows(o):
    found = []
    for k in range(NBIN):
        pairs = [
            i
            for i in range(CB)
            for j in range(CB)
            if (o > 0 or i < j) and (CB * o + j - i) // BINW == k
        ]
        if pairs:
            found.append((k, min(pairs) // 16 * 16, max(pairs) // 16 * 16 + 16))
    return tuple(found)


LEVELS = tuple(level_rows(o) for o in range(MEETINGS))
STARTS = tuple(sum(len(v) for v in LEVELS[:o]) for o in range(MEETINGS))
LEVEL_COUNT = sum(len(v) for v in LEVELS)


def filter_table():
    k = np.arange(TAPS, dtype=np.float64)
    m = k - (TAPS - 1) / 2.0
    ideal = 2 * BAND_HIGH * np.sinc(2 * BAND_HIGH * m) - 2 * BAND_LOW * np.sinc(2 * BAND_LOW * m)
    taps = ideal * (0.5 - 0.5 * np.cos(2 * np.pi * (k + 0.5) / TAPS))
    lagged = np.arange(TAPS)[None, :] - np.arange(2 * TAPS)[:, None] + TAPS
    inside = (lagged >= 0) & (lagged < TAPS)
    return np.where(inside, taps[np.clip(lagged, 0, TAPS - 1)], 0.0).astype(np.float32)


def column_order():
    column = np.arange(WIN)
    return column // (2 * BAND) * BAND + column % BAND, column // BAND % 2 == 1


def transform_table():
    freq, is_imag = column_order()
    angle = (np.arange(HALF)[:, None] * freq[None, :] % WIN) * (2 * np.pi / WIN)
    return (np.where(is_imag[None, :], -np.sin(angle), np.cos(angle)) / math.sqrt(WIN)).astype(jnp.bfloat16)


def inverse_table():
    freq, is_imag = column_order()
    angle = (freq[:, None] * np.arange(LANES)[None, :] % WIN) * (2 * np.pi / WIN)
    weight = np.where(freq == 0, 1.0, 2.0)[:, None] / (WINDOWS * math.sqrt(WIN))
    return (weight * np.where(is_imag[:, None], -np.sin(angle), np.cos(angle))).astype(np.float32)


def bin_table():
    spread = np.arange(CB)[None, :] - np.arange(CB)[:, None]
    tables = [
        ((CB * o + spread) // BINW == k).astype(jnp.bfloat16) for o in range(MEETINGS) for k, _, _ in LEVELS[o]
    ]
    return np.stack(tables)


def call(kernel, out_shape, *args, smem=(), aliases=None):
    specs = [
        pl.BlockSpec(memory_space=pltpu.SMEM) if n in smem else pl.BlockSpec(memory_space=pltpu.VMEM)
        for n in range(len(args))
    ]
    many = isinstance(out_shape, (tuple, list))
    out_specs = [pl.BlockSpec(memory_space=pltpu.VMEM)] * len(out_shape) if many else pl.BlockSpec(memory_space=pltpu.VMEM)
    return pl.pallas_call(
        kernel,
        out_shape=out_shape,
        in_specs=specs,
        out_specs=out_specs,
        input_output_aliases=aliases or {},
        compiler_params=pltpu.CompilerParams(vmem_limit_bytes=VMEM_LIMIT),
    )(*args)


def shape(dims, dtype):
    return jax.ShapeDtypeStruct(dims, dtype)


def low_lanes(width=2 * BAND):
    return lax.broadcasted_iota(jnp.int32, (1, width), 1) < BAND


def spectra_kernel(hist_ref, x_ref, taps_ref, table_ref, out_ref):
    tiles = [hist_ref[...]] + [x_ref[:, t * TAPS : (t + 1) * TAPS] for t in range(WIN // TAPS)]
    pairs = [jnp.concatenate([tiles[t], tiles[t + 1]], axis=1) for t in range(WIN // TAPS)]
    rows = jnp.dot(jnp.concatenate(pairs, axis=0), taps_ref[...], precision=HI, preferred_element_type=F32)
    rows = rows.astype(BF16)
    filtered = [rows[t * CB : (t + 1) * CB] for t in range(WIN // TAPS)]
    early = jnp.concatenate(filtered[:4], axis=1)
    late = jnp.concatenate(filtered[4:], axis=1)
    column = lax.broadcasted_iota(jnp.int32, (1, WIN), 1)
    turn = jnp.where(column % 2 == 0, 1.0, -1.0).astype(F32)
    first = jnp.dot(early, table_ref[...], preferred_element_type=F32)
    second = jnp.dot(late, table_ref[...], preferred_element_type=F32)
    out_ref[...] = (first + turn * second).astype(BF16)


def power_kernel(core_ref, s0_ref, s1_ref, keep_ref, send_ref):
    core = core_ref[0]
    low = low_lanes()

    def part(start, ref):
        for pair in range(PARTS // 2):
            both = []
            for q in (2 * pair, 2 * pair + 1):
                cols = slice(q * 2 * BAND, (q + 1) * 2 * BAND)
                square = jnp.zeros((CB // 2, 2 * BAND), F32)
                for source in (s0_ref, s1_ref):
                    values = source[pl.ds(start, CB // 2), cols].astype(F32)
                    square = square + values * values
                both.append(square + pltpu.roll(square, BAND, 1))
            merged = jnp.where(low, both[0], both[1]) * (1.0 / WINDOWS)
            ref[:, pair * 2 * BAND : (pair + 1) * 2 * BAND] = merged.astype(ref.dtype)

    part(pl.multiple_of(core * (CB // 2), CB // 2), keep_ref)
    part(pl.multiple_of((1 - core) * (CB // 2), CB // 2), send_ref)


def whiten_kernel(core_ref, s0_ref, s1_ref, own_ref, other_ref, out_ref):
    core = core_ref[0]
    low = low_lanes()
    for half in range(2):
        rows = slice(half * CB // 2, (half + 1) * CB // 2)
        for pair in range(PARTS // 2):
            cols = slice(pair * 2 * BAND, (pair + 1) * 2 * BAND)
            gain = jnp.where(core == half, own_ref[:, cols], other_ref[:, cols])
            turned = pltpu.roll(gain, BAND, 1)
            for q, spread in ((2 * pair, jnp.where(low, gain, turned)), (2 * pair + 1, jnp.where(low, turned, gain))):
                for w, ref in enumerate((s0_ref, s1_ref)):
                    values = ref[rows, q * 2 * BAND : (q + 1) * 2 * BAND].astype(F32)
                    out_ref[2 * q + w, rows, :] = (values * spread).astype(BF16)


def list_kernel(blk_ref, count_ref, owner_ref, codes_ref, out_ref):
    lane = lax.broadcasted_iota(jnp.int32, (1, CB), 1)
    rows = []
    owners = jnp.zeros((1, CB), jnp.int32)
    for o in range(MEETINGS):
        live = jnp.where(blk_ref[0] >= o, count_ref[o, 0], 0)
        for n in range(4):
            rows.append(jnp.where(lane + n * CB < live, codes_ref[o : o + 1, n * CB : (n + 1) * CB], -1))
        owners = jnp.where(lane == o, owner_ref[o, 0], owners)
    rows = rows + [owners] + [jnp.zeros((1, CB), jnp.int32)] * (LIST_ROWS - len(rows) - 1)
    block = jnp.concatenate(rows, axis=0)
    for p in range(PLANE):
        out_ref[p] = block


def chosen_kernel(lists_ref, out_ref):
    row = lax.broadcasted_iota(jnp.int32, (CB, PCAP), 0)

    def one(p, carry):
        for o in range(MEETINGS):
            pieces = [lists_ref[p, o * 4 + n : o * 4 + n + 1, :] for n in range(4)]
            codes = jnp.concatenate(pieces, axis=1)
            pick_first = jnp.where(row == (codes >> 7), 1.0, 0.0).astype(BF16)
            pick_second = jnp.where(row == (codes & (CB - 1)), 1.0, 0.0).astype(BF16)
            chosen = lax.dot_general(pick_first, pick_second, (((1,), (1,)), ((), ())), preferred_element_type=F32)
            out_ref[p, o] = chosen.astype(BF16)
        return carry

    lax.fori_loop(0, PLANE, one, 0)


def meet(out_ref, bins_ref, chosen, a_block, b_block, o, owner):
    low = low_lanes()
    sign = jnp.where(low, -1.0, 1.0)
    weights = jnp.concatenate(
        [chosen[lo:hi] * bins_ref[STARTS[o] + n, lo:hi, :] for n, (_, lo, hi) in enumerate(LEVELS[o])], axis=0
    )
    mixed = jnp.dot(weights, b_block, preferred_element_type=F32)
    straight = a_block.astype(F32)
    swapped = pltpu.roll(straight, BAND, 1) * sign
    row_id = lax.broadcasted_iota(jnp.int32, (NBIN, 2 * BAND), 0)
    real = jnp.zeros((NBIN, 2 * BAND), F32)
    imag = jnp.zeros((NBIN, 2 * BAND), F32)
    at = 0
    for k, lo, hi in LEVELS[o]:
        part = mixed[at : at + hi - lo]
        at += hi - lo
        dims = ((hi - lo) // 8, 8, 2 * BAND)
        along = jnp.sum(jnp.sum((straight[lo:hi] * part).reshape(dims), axis=0), axis=0, keepdims=True)
        across = jnp.sum(jnp.sum((swapped[lo:hi] * part).reshape(dims), axis=0), axis=0, keepdims=True)
        real = jnp.where(row_id == k, along, real)
        imag = jnp.where(row_id == k, across, imag)
    terms = jnp.where(low, real + pltpu.roll(real, BAND, 1), imag + pltpu.roll(imag, BAND, 1))
    spot = (owner % PLANE) * ROWS + owner // PLANE
    out_ref[spot] = out_ref[spot] + terms


def plane_kernel(owner_ref, bins_ref, chosen_ref, group_ref, out_ref):
    out_ref[...] = jnp.zeros(out_ref.shape, F32)
    for o in range(MEETINGS):

        def one(p, carry, o=o):
            meet(out_ref, bins_ref, chosen_ref[p, o], group_ref[p - o], group_ref[p], o, owner_ref[p, o])
            return carry

        lax.fori_loop(o, PLANE, one, 0)


def below_kernel(owner_ref, bins_ref, chosen_ref, group_ref, below_ref, sums_ref, out_ref):
    out_ref[...] = sums_ref[...]
    for o in range(1, MEETINGS):

        def one(p, carry, o=o):
            meet(out_ref, bins_ref, chosen_ref[p, o], below_ref[p - o + ROUNDS], group_ref[p], o, owner_ref[p, o])
            return carry

        lax.fori_loop(0, o, one, 0)


def lag_kernel(parts_ref, table_ref, out_ref):
    lane = lax.broadcasted_iota(jnp.int32, (1, 2 * BAND), 1)
    sign = jnp.where(lane < BAND, -1.0, 1.0)
    merged = [parts_ref[2 * q] + parts_ref[2 * q + 1] for q in range(PARTS)]
    swapped = [pltpu.roll(value, BAND, 1) for value in merged]
    turned = []
    for quarter in range(4):
        step = (lane * (quarter + 2)) & 3
        along = jnp.where(step == 0, 1.0, 0.0) - jnp.where(step == 2, 1.0, 0.0)
        across = sign * (jnp.where(step == 1, 1.0, 0.0) - jnp.where(step == 3, 1.0, 0.0))
        turned.append(jnp.concatenate([x * along + y * across for x, y in zip(merged, swapped)], axis=1))
    lagged = jnp.dot(jnp.concatenate(turned, axis=0), table_ref[...], precision=HI, preferred_element_type=F32)
    for quarter in range(4):
        for y in range(ROWS):
            at = quarter * ROWS * NBIN + y * NBIN
            out_ref[y * 4 + quarter] = lagged[at : at + NBIN]


def crossed(block, bit):
    return lax.ppermute(block, "lag", [(i, i ^ bit) for i in range(4)])


def body(traces, owner_map, pair_codes, pair_count):
    blk = lax.axis_index("row") * PLANE + lax.axis_index("plane")
    core = (lax.axis_index("lag") % 2).astype(jnp.int32).reshape(1)
    taps = jnp.asarray(filter_table())
    table = jnp.asarray(transform_table())

    history = lax.ppermute(traces[:, -TAPS:], "lag", [(i, i + 1) for i in range(3)])

    lists = call(
        list_kernel,
        shape((PLANE, LIST_ROWS, CB), jnp.int32),
        blk.astype(jnp.int32).reshape(1),
        pair_count,
        owner_map,
        pair_codes,
        smem=(0, 1, 2),
    )
    lists = lax.all_to_all(lists, "plane", 0, 0, tiled=True)

    spec = shape((CB, WIN), BF16)
    spectra1 = call(spectra_kernel, spec, traces[:, WIN - TAPS : WIN], traces[:, WIN:], taps, table)
    spectra0 = call(spectra_kernel, spec, history, traces[:, :WIN], taps, table)

    half = (CB // 2, NF)
    keep, send = call(power_kernel, (shape(half, F32), shape(half, BF16)), core, spectra0, spectra1, smem=(0,))
    send, lists = lax.optimization_barrier((send, lists))
    owners = lists[:, 4 * MEETINGS, :MEETINGS]
    chosen = call(chosen_kernel, shape((PLANE, MEETINGS, CB, CB), BF16), lists)
    chip = keep + crossed(send, 1).astype(F32)
    power = chip + crossed(chip.astype(BF16), 2).astype(F32)
    gain = lax.rsqrt(power + WATER)
    slabs = call(
        whiten_kernel, shape((PLANE, CB, CB), BF16), core, spectra0, spectra1, gain, crossed(gain, 1), smem=(0,)
    )
    group = lax.all_to_all(slabs, "plane", 0, 0, tiled=True)
    last, chosen = lax.optimization_barrier((group[PLANE - ROUNDS :], chosen))
    below = lax.ppermute(last, "row", [(i, i + 1) for i in range(ROWS - 1)])

    bins = jnp.asarray(bin_table())
    sums_shape = shape((ROWS * PLANE, NBIN, 2 * BAND), F32)
    sums = call(plane_kernel, sums_shape, owners, bins, chosen, group, smem=(0,))
    sums = call(below_kernel, sums_shape, owners, bins, chosen, group, below, sums, smem=(0,), aliases={5: 0})
    parts = lax.all_to_all(sums.reshape(PLANE, ROWS * NBIN, 2 * BAND), "plane", 0, 0, tiled=True)
    lagged = call(lag_kernel, shape((ROWS * 4, NBIN, LANES), F32), parts, jnp.asarray(inverse_table()))
    return jnp.sum(lax.all_to_all(lagged, ("row", "lag"), 0, 0, tiled=True), axis=0, keepdims=True)


def solution(mesh):
    split = Mesh(mesh.devices.reshape(ROWS, PLANE, 4), ("row", "plane", "lag"))
    owned = ("row", "plane")
    return jax.shard_map(
        body,
        mesh=split,
        in_specs=(P(owned, "lag"), P(None, owned), P(None, owned), P(None, owned)),
        out_specs=P(owned, None, "lag"),
        check_vma=False,
    )
```

```python
import math

import jax
import jax.numpy as jnp
import numpy as np
from jax import lax
from jax.experimental import pallas as pl
from jax.experimental.pallas import tpu as pltpu
from jax.sharding import Mesh
from jax.sharding import PartitionSpec as P

CB = 128
WIN = 1024
HALF = 512
NF = 512
TAPS = 128
NBIN = 8
BINW = 80
ROUNDS = 4
MEETINGS = 5
PCAP = 512
WINDOWS = 8
LANES = 256
PLANE = 16
ROWS = 4
PARTS = 8
BAND = 64
LIST_ROWS = 24

BAND_LOW = 0.02
BAND_HIGH = 0.48
WATER = 0.1

F32 = jnp.float32
BF16 = jnp.bfloat16
HI = lax.Precision.HIGHEST
VMEM_LIMIT = 16 * 1024 * 1024


def level_rows(o):
    found = []
    for k in range(NBIN):
        pairs = [
            i
            for i in range(CB)
            for j in range(CB)
            if (o > 0 or i < j) and (CB * o + j - i) // BINW == k
        ]
        if pairs:
            found.append((k, min(pairs) // 16 * 16, max(pairs) // 16 * 16 + 16))
    return tuple(found)


LEVELS = tuple(level_rows(o) for o in range(MEETINGS))
SPANS = tuple((o, k, lo, hi) for o in range(MEETINGS) for k, lo, hi in LEVELS[o])
SPAN_ROWS = sum(hi - lo for _, _, lo, hi in SPANS)


def filter_table():
    k = np.arange(TAPS, dtype=np.float64)
    m = k - (TAPS - 1) / 2.0
    ideal = 2 * BAND_HIGH * np.sinc(2 * BAND_HIGH * m) - 2 * BAND_LOW * np.sinc(2 * BAND_LOW * m)
    taps = ideal * (0.5 - 0.5 * np.cos(2 * np.pi * (k + 0.5) / TAPS))
    lagged = np.arange(TAPS)[None, :] - np.arange(2 * TAPS)[:, None] + TAPS
    inside = (lagged >= 0) & (lagged < TAPS)
    return np.where(inside, taps[np.clip(lagged, 0, TAPS - 1)], 0.0).astype(np.float32)


def column_order():
    column = np.arange(WIN)
    return column // (2 * BAND) * BAND + column % BAND, column // BAND % 2 == 1


def transform_table():
    freq, is_imag = column_order()
    angle = (np.arange(HALF)[:, None] * freq[None, :] % WIN) * (2 * np.pi / WIN)
    return (np.where(is_imag[None, :], -np.sin(angle), np.cos(angle)) / math.sqrt(WIN)).astype(jnp.bfloat16)


def inverse_table():
    freq, is_imag = column_order()
    angle = (freq[:, None] * np.arange(LANES)[None, :] % WIN) * (2 * np.pi / WIN)
    weight = np.where(freq == 0, 1.0, 2.0)[:, None] / (WINDOWS * math.sqrt(WIN))
    return (weight * np.where(is_imag[:, None], -np.sin(angle), np.cos(angle))).astype(np.float32)


def call(kernel, out_shape, *args, smem=(), aliases=None, scratch=()):
    specs = [
        pl.BlockSpec(memory_space=pltpu.SMEM) if n in smem else pl.BlockSpec(memory_space=pltpu.VMEM)
        for n in range(len(args))
    ]
    many = isinstance(out_shape, (tuple, list))
    out_specs = [pl.BlockSpec(memory_space=pltpu.VMEM)] * len(out_shape) if many else pl.BlockSpec(memory_space=pltpu.VMEM)
    return pl.pallas_call(
        kernel,
        out_shape=out_shape,
        in_specs=specs,
        out_specs=out_specs,
        input_output_aliases=aliases or {},
        scratch_shapes=list(scratch),
        compiler_params=pltpu.CompilerParams(vmem_limit_bytes=VMEM_LIMIT),
    )(*args)


def shape(dims, dtype):
    return jax.ShapeDtypeStruct(dims, dtype)


def low_lanes(width=2 * BAND):
    return lax.broadcasted_iota(jnp.int32, (1, width), 1) < BAND


def spectra_kernel(hist_ref, x_ref, taps_ref, table_ref, out_ref):
    tiles = [hist_ref[...]] + [x_ref[:, t * TAPS : (t + 1) * TAPS] for t in range(WIN // TAPS)]
    pairs = [jnp.concatenate([tiles[t], tiles[t + 1]], axis=1) for t in range(WIN // TAPS)]
    rows = jnp.dot(jnp.concatenate(pairs, axis=0), taps_ref[...], precision=HI, preferred_element_type=F32)
    rows = rows.astype(BF16)
    filtered = [rows[t * CB : (t + 1) * CB] for t in range(WIN // TAPS)]
    early = jnp.concatenate(filtered[:4], axis=1)
    late = jnp.concatenate(filtered[4:], axis=1)
    column = lax.broadcasted_iota(jnp.int32, (1, WIN), 1)
    turn = jnp.where(column % 2 == 0, 1.0, -1.0).astype(F32)
    first = jnp.dot(early, table_ref[...], preferred_element_type=F32)
    second = jnp.dot(late, table_ref[...], preferred_element_type=F32)
    out_ref[...] = (first + turn * second).astype(BF16)


def power_kernel(core_ref, s0_ref, s1_ref, keep_ref, send_ref):
    core = core_ref[0]
    low = low_lanes()

    def part(start, ref):
        for pair in range(PARTS // 2):
            both = []
            for q in (2 * pair, 2 * pair + 1):
                cols = slice(q * 2 * BAND, (q + 1) * 2 * BAND)
                square = jnp.zeros((CB // 2, 2 * BAND), F32)
                for source in (s0_ref, s1_ref):
                    values = source[pl.ds(start, CB // 2), cols].astype(F32)
                    square = square + values * values
                both.append(square + pltpu.roll(square, BAND, 1))
            merged = jnp.where(low, both[0], both[1]) * (1.0 / WINDOWS)
            ref[:, pair * 2 * BAND : (pair + 1) * 2 * BAND] = merged.astype(ref.dtype)

    part(pl.multiple_of(core * (CB // 2), CB // 2), keep_ref)
    part(pl.multiple_of((1 - core) * (CB // 2), CB // 2), send_ref)


def whiten_kernel(core_ref, s0_ref, s1_ref, own_ref, other_ref, out_ref):
    core = core_ref[0]
    low = low_lanes()
    for half in range(2):
        rows = slice(half * CB // 2, (half + 1) * CB // 2)
        for pair in range(PARTS // 2):
            cols = slice(pair * 2 * BAND, (pair + 1) * 2 * BAND)
            gain = jnp.where(core == half, own_ref[:, cols], other_ref[:, cols])
            turned = pltpu.roll(gain, BAND, 1)
            for q, spread in ((2 * pair, jnp.where(low, gain, turned)), (2 * pair + 1, jnp.where(low, turned, gain))):
                for w, ref in enumerate((s0_ref, s1_ref)):
                    values = ref[rows, q * 2 * BAND : (q + 1) * 2 * BAND].astype(F32)
                    out_ref[2 * q + w, rows, :] = (values * spread).astype(BF16)


def list_kernel(blk_ref, count_ref, owner_ref, codes_ref, out_ref):
    lane = lax.broadcasted_iota(jnp.int32, (1, CB), 1)
    rows = []
    owners = jnp.zeros((1, CB), jnp.int32)
    for o in range(MEETINGS):
        live = jnp.where(blk_ref[0] >= o, count_ref[o, 0], 0)
        for n in range(4):
            rows.append(jnp.where(lane + n * CB < live, codes_ref[o : o + 1, n * CB : (n + 1) * CB], -1))
        owners = jnp.where(lane == o, owner_ref[o, 0], owners)
    rows = rows + [owners] + [jnp.zeros((1, CB), jnp.int32)] * (LIST_ROWS - len(rows) - 1)
    block = jnp.concatenate(rows, axis=0)
    for p in range(PLANE):
        out_ref[p] = block


def chosen_kernel(lists_ref, low_ref, high_ref):
    row = lax.broadcasted_iota(jnp.int32, (CB, PCAP), 0)

    def fill(p, ref, at):
        for o in range(MEETINGS):
            pieces = [lists_ref[p, o * 4 + n : o * 4 + n + 1, :] for n in range(4)]
            codes = jnp.concatenate(pieces, axis=1)
            pick_first = jnp.where(row == (codes >> 7), 1.0, 0.0).astype(BF16)
            pick_second = jnp.where(row == (codes & (CB - 1)), 1.0, 0.0).astype(BF16)
            chosen = lax.dot_general(pick_first, pick_second, (((1,), (1,)), ((), ())), preferred_element_type=F32)
            ref[at, o] = chosen.astype(BF16)

    for p in range(ROUNDS):
        fill(p, low_ref, p)

    def one(p, carry):
        fill(p, high_ref, p - ROUNDS)
        return carry

    lax.fori_loop(ROUNDS, PLANE, one, 0)


def fill_bins(bins_ref):
    spread = lax.broadcasted_iota(jnp.int32, (CB, CB), 1) - lax.broadcasted_iota(jnp.int32, (CB, CB), 0)
    at = 0
    for o, k, lo, hi in SPANS:
        distance = spread[lo:hi] + CB * o
        inside = (distance >= BINW * k) & (distance < BINW * (k + 1))
        bins_ref[at : at + hi - lo, :] = jnp.where(inside, 1.0, 0.0).astype(BF16)
        at += hi - lo


def meet(out_ref, owner_ref, bins_ref, chosen_ref, at_block, block, partners, p):
    low = low_lanes()
    sign = jnp.where(low, -1.0, 1.0)
    row_id = lax.broadcasted_iota(jnp.int32, (NBIN, 2 * BAND), 0)
    at = 0
    pieces = []
    for o, _, lo, hi in SPANS:
        pieces.append(chosen_ref[at_block, o, lo:hi, :] * bins_ref[at : at + hi - lo, :])
        at += hi - lo
    mixed = jnp.dot(jnp.concatenate(pieces, axis=0), block, preferred_element_type=F32)
    at = 0
    found = []
    for o in range(MEETINGS):
        straight = partners[o].astype(F32)
        swapped = pltpu.roll(straight, BAND, 1) * sign
        real = jnp.zeros((NBIN, 2 * BAND), F32)
        imag = jnp.zeros((NBIN, 2 * BAND), F32)
        for k, lo, hi in LEVELS[o]:
            part = mixed[at : at + hi - lo]
            at += hi - lo
            dims = ((hi - lo) // 8, 8, 2 * BAND)
            along = jnp.sum(jnp.sum((straight[lo:hi] * part).reshape(dims), axis=0), axis=0, keepdims=True)
            across = jnp.sum(jnp.sum((swapped[lo:hi] * part).reshape(dims), axis=0), axis=0, keepdims=True)
            real = jnp.where(row_id == k, along, real)
            imag = jnp.where(row_id == k, across, imag)
        found.append(jnp.where(low, real + pltpu.roll(real, BAND, 1), imag + pltpu.roll(imag, BAND, 1)))
    for o in range(MEETINGS):
        owner = owner_ref[p, o]
        spot = (owner % PLANE) * ROWS + owner // PLANE
        out_ref[spot] = out_ref[spot] + found[o]


def plane_kernel(owner_ref, chosen_ref, group_ref, out_ref, bins_ref):
    out_ref[...] = jnp.zeros(out_ref.shape, F32)
    fill_bins(bins_ref)

    def one(p, carry):
        partners = [group_ref[p - o] for o in range(MEETINGS)]
        meet(out_ref, owner_ref, bins_ref, chosen_ref, p - ROUNDS, group_ref[p], partners, p)
        return carry

    lax.fori_loop(ROUNDS, PLANE, one, 0)


def below_kernel(owner_ref, chosen_ref, group_ref, below_ref, sums_ref, out_ref, bins_ref):
    out_ref[...] = sums_ref[...]
    fill_bins(bins_ref)
    for p in range(ROUNDS):
        partners = [group_ref[p - o] if p >= o else below_ref[p - o + ROUNDS] for o in range(MEETINGS)]
        meet(out_ref, owner_ref, bins_ref, chosen_ref, p, group_ref[p], partners, p)


def lag_kernel(parts_ref, table_ref, out_ref):
    lane = lax.broadcasted_iota(jnp.int32, (1, 2 * BAND), 1)
    sign = jnp.where(lane < BAND, -1.0, 1.0)
    merged = [parts_ref[2 * q] + parts_ref[2 * q + 1] for q in range(PARTS)]
    swapped = [pltpu.roll(value, BAND, 1) for value in merged]
    turned = []
    for quarter in range(4):
        step = (lane * (quarter + 2)) & 3
        along = jnp.where(step == 0, 1.0, 0.0) - jnp.where(step == 2, 1.0, 0.0)
        across = sign * (jnp.where(step == 1, 1.0, 0.0) - jnp.where(step == 3, 1.0, 0.0))
        turned.append(jnp.concatenate([x * along + y * across for x, y in zip(merged, swapped)], axis=1))
    lagged = jnp.dot(jnp.concatenate(turned, axis=0), table_ref[...], precision=HI, preferred_element_type=F32)
    for quarter in range(4):
        for y in range(ROWS):
            at = quarter * ROWS * NBIN + y * NBIN
            out_ref[y * 4 + quarter] = lagged[at : at + NBIN]


def crossed(block, bit):
    return lax.ppermute(block, "lag", [(i, i ^ bit) for i in range(4)])


def body(traces, owner_map, pair_codes, pair_count):
    blk = lax.axis_index("row") * PLANE + lax.axis_index("plane")
    core = (lax.axis_index("lag") % 2).astype(jnp.int32).reshape(1)
    taps = jnp.asarray(filter_table())
    table = jnp.asarray(transform_table())

    history = lax.ppermute(traces[:, -TAPS:], "lag", [(i, i + 1) for i in range(3)])

    spec = shape((CB, WIN), BF16)
    spectra1 = call(spectra_kernel, spec, traces[:, WIN - TAPS : WIN], traces[:, WIN:], taps, table)
    spectra0 = call(spectra_kernel, spec, history, traces[:, :WIN], taps, table)

    half = (CB // 2, NF)
    keep, send = call(power_kernel, (shape(half, F32), shape(half, BF16)), core, spectra0, spectra1, smem=(0,))
    chip = keep + crossed(send, 1).astype(F32)
    chip, place = lax.optimization_barrier((chip, blk.astype(jnp.int32).reshape(1)))
    lists = call(
        list_kernel,
        shape((PLANE, LIST_ROWS, CB), jnp.int32),
        place,
        pair_count,
        owner_map,
        pair_codes,
        smem=(0, 1, 2),
    )
    lists = lax.all_to_all(lists, "plane", 0, 0, tiled=True)
    power = chip + crossed(chip.astype(BF16), 2).astype(F32)
    gain = lax.rsqrt(power + WATER)
    slabs = call(
        whiten_kernel, shape((PLANE, CB, CB), BF16), core, spectra0, spectra1, gain, crossed(gain, 1), smem=(0,)
    )
    slabs, lists = lax.optimization_barrier((slabs, lists))
    owners = lists[:, 4 * MEETINGS, :MEETINGS]
    halves = tuple(shape((n, MEETINGS, CB, CB), BF16) for n in (ROUNDS, PLANE - ROUNDS))
    chosen_low, chosen_high = call(chosen_kernel, halves, lists)
    group = lax.all_to_all(slabs, "plane", 0, 0, tiled=True)
    last, chosen_low, chosen_high = lax.optimization_barrier((group[PLANE - ROUNDS :], chosen_low, chosen_high))
    below = lax.ppermute(last, "row", [(i, i + 1) for i in range(ROWS - 1)])

    sums_shape = shape((ROWS * PLANE, NBIN, 2 * BAND), F32)
    bins = pltpu.VMEM((SPAN_ROWS, CB), BF16)
    sums = call(plane_kernel, sums_shape, owners, chosen_high, group, smem=(0,), scratch=(bins,))
    sums = call(
        below_kernel,
        sums_shape,
        owners,
        chosen_low,
        group,
        below,
        sums,
        smem=(0,),
        aliases={4: 0},
        scratch=(bins,),
    )
    parts = lax.all_to_all(sums.reshape(PLANE, ROWS * NBIN, 2 * BAND), "plane", 0, 0, tiled=True)
    lagged = call(lag_kernel, shape((ROWS * 4, NBIN, LANES), F32), parts, jnp.asarray(inverse_table()))
    return jnp.sum(lax.all_to_all(lagged, ("row", "lag"), 0, 0, tiled=True), axis=0, keepdims=True)


def solution(mesh):
    split = Mesh(mesh.devices.reshape(ROWS, PLANE, 4), ("row", "plane", "lag"))
    owned = ("row", "plane")
    return jax.shard_map(
        body,
        mesh=split,
        in_specs=(P(owned, "lag"), P(None, owned), P(None, owned), P(None, owned)),
        out_specs=P(owned, None, "lag"),
        check_vma=False,
    )
```

```python
import math

import jax
import jax.numpy as jnp
import numpy as np
from jax import lax
from jax.experimental import pallas as pl
from jax.experimental.pallas import tpu as pltpu
from jax.sharding import Mesh
from jax.sharding import PartitionSpec as P

CB = 128
WIN = 1024
HALF = 512
NF = 512
TAPS = 128
NBIN = 8
BINW = 80
ROUNDS = 4
MEETINGS = 5
PCAP = 512
WINDOWS = 8
LANES = 256
PLANE = 16
ROWS = 4
LAGS = 4
WIDE = 128
BAND = 8
LIST_ROWS = 24

BAND_LOW = 0.02
BAND_HIGH = 0.48
WATER = 0.1

F32 = jnp.float32
BF16 = jnp.bfloat16
HI = lax.Precision.HIGHEST
VMEM_LIMIT = 16 * 1024 * 1024


def level_rows(o):
    found = []
    for k in range(NBIN):
        pairs = [
            i
            for i in range(CB)
            for j in range(CB)
            if (o > 0 or i < j) and (CB * o + j - i) // BINW == k
        ]
        if pairs:
            found.append((k, min(pairs) // 16 * 16, max(pairs) // 16 * 16 + 16))
    return tuple(found)


LEVELS = tuple(level_rows(o) for o in range(MEETINGS))
SPANS = tuple((o, k, lo, hi) for o in range(MEETINGS) for k, lo, hi in LEVELS[o])
SPAN_ROWS = sum(hi - lo for _, _, lo, hi in SPANS)


def filter_table():
    k = np.arange(TAPS, dtype=np.float64)
    m = k - (TAPS - 1) / 2.0
    ideal = 2 * BAND_HIGH * np.sinc(2 * BAND_HIGH * m) - 2 * BAND_LOW * np.sinc(2 * BAND_LOW * m)
    taps = ideal * (0.5 - 0.5 * np.cos(2 * np.pi * (k + 0.5) / TAPS))
    lagged = np.arange(TAPS)[None, :] - np.arange(2 * TAPS)[:, None] + TAPS
    inside = (lagged >= 0) & (lagged < TAPS)
    return np.where(inside, taps[np.clip(lagged, 0, TAPS - 1)], 0.0).astype(np.float32)


def column_order():
    column = np.arange(WIN)
    return column // (2 * BAND) * BAND + column % BAND, column // BAND % 2 == 1


def transform_table():
    freq, is_imag = column_order()
    angle = (np.arange(HALF)[:, None] * freq[None, :] % WIN) * (2 * np.pi / WIN)
    return (np.where(is_imag[None, :], -np.sin(angle), np.cos(angle)) / math.sqrt(WIN)).astype(jnp.bfloat16)


def inverse_table():
    freq, is_imag = column_order()
    angle = (freq[:, None] * np.arange(LANES)[None, :] % WIN) * (2 * np.pi / WIN)
    weight = np.where(freq == 0, 1.0, 2.0)[:, None] / (WINDOWS * math.sqrt(WIN))
    table = (weight * np.where(is_imag[:, None], -np.sin(angle), np.cos(angle))).astype(np.float32)
    table = table.reshape(PLANE, LAGS, 2 * BAND, LANES).transpose(1, 0, 2, 3)
    return table.reshape(LAGS, PLANE * 2 * BAND, LANES)


def call(kernel, out_shape, *args, smem=(), aliases=None, scratch=()):
    specs = [
        pl.BlockSpec(memory_space=pltpu.SMEM) if n in smem else pl.BlockSpec(memory_space=pltpu.VMEM)
        for n in range(len(args))
    ]
    many = isinstance(out_shape, (tuple, list))
    out_specs = [pl.BlockSpec(memory_space=pltpu.VMEM)] * len(out_shape) if many else pl.BlockSpec(memory_space=pltpu.VMEM)
    return pl.pallas_call(
        kernel,
        out_shape=out_shape,
        in_specs=specs,
        out_specs=out_specs,
        input_output_aliases=aliases or {},
        scratch_shapes=list(scratch),
        compiler_params=pltpu.CompilerParams(vmem_limit_bytes=VMEM_LIMIT),
    )(*args)


def shape(dims, dtype):
    return jax.ShapeDtypeStruct(dims, dtype)


def lanes():
    return lax.broadcasted_iota(jnp.int32, (1, WIDE), 1)


def real_lanes():
    return (lanes() & BAND) == 0


def swap_parts(values):
    return jnp.where(real_lanes(), pltpu.roll(values, WIDE - BAND, 1), pltpu.roll(values, BAND, 1))


def fold(values):
    for step in (BAND, 2 * BAND, 4 * BAND, 8 * BAND):
        values = values + pltpu.roll(values, step, 1)
    return values


def transpose_pieces(arrays, width):
    bit = 1
    while bit < len(arrays):
        upper = (lanes() & (bit * width)) != 0
        out = list(arrays)
        for q in range(len(arrays)):
            if q & bit:
                continue
            a, b = arrays[q], arrays[q | bit]
            out[q] = jnp.where(upper, pltpu.roll(b, bit * width, 1), a)
            out[q | bit] = jnp.where(upper, b, pltpu.roll(a, WIDE - bit * width, 1))
        arrays = out
        bit *= 2
    return arrays


def spectra_kernel(hist_ref, x_ref, taps_ref, table_ref, out_ref):
    tiles = [hist_ref[...]] + [x_ref[:, t * TAPS : (t + 1) * TAPS] for t in range(WIN // TAPS)]
    pairs = [jnp.concatenate([tiles[t], tiles[t + 1]], axis=1) for t in range(WIN // TAPS)]
    rows = jnp.dot(jnp.concatenate(pairs, axis=0), taps_ref[...], precision=HI, preferred_element_type=F32)
    rows = rows.astype(BF16)
    filtered = [rows[t * CB : (t + 1) * CB] for t in range(WIN // TAPS)]
    early = jnp.concatenate(filtered[:4], axis=1)
    late = jnp.concatenate(filtered[4:], axis=1)
    column = lax.broadcasted_iota(jnp.int32, (1, WIN), 1)
    turn = jnp.where(column % 2 == 0, 1.0, -1.0).astype(F32)
    first = jnp.dot(early, table_ref[...], preferred_element_type=F32)
    second = jnp.dot(late, table_ref[...], preferred_element_type=F32)
    out_ref[...] = (first + turn * second).astype(BF16)


def pack_kernel(s0_ref, s1_ref, out_ref):
    for c in range(WIN // WIDE):
        cols = slice(c * WIDE, (c + 1) * WIDE)
        pieces = []
        for g in range(4):
            for ref in (s0_ref, s1_ref):
                pieces.append(ref[g * 32 : (g + 1) * 32, cols].astype(F32))
        for e, value in enumerate(transpose_pieces(pieces, 2 * BAND)):
            out_ref[c * 8 + e] = value.astype(BF16)


def whiten_kernel(slab_ref, out_ref):
    def one(p, carry):
        pieces = [slab_ref[p * LAGS + n].astype(F32) for n in range(LAGS)]
        for g, value in enumerate(transpose_pieces(pieces, 4 * BAND)):
            gain = lax.rsqrt(fold(value * value) * (1.0 / WINDOWS) + WATER)
            out_ref[p, g * 32 : (g + 1) * 32, :] = (value * gain).astype(BF16)
        return carry

    lax.fori_loop(0, PLANE, one, 0, unroll=2)


def list_kernel(blk_ref, count_ref, owner_ref, codes_ref, out_ref):
    lane = lax.broadcasted_iota(jnp.int32, (1, CB), 1)
    rows = []
    owners = jnp.zeros((1, CB), jnp.int32)
    for o in range(MEETINGS):
        live = jnp.where(blk_ref[0] >= o, count_ref[:, o : o + 1], 0)
        for n in range(4):
            rows.append(jnp.where(lane + n * CB < live, codes_ref[o : o + 1, n * CB : (n + 1) * CB], -1))
        owners = jnp.where(lane == o, owner_ref[:, o : o + 1], owners)
    rows = rows + [owners] + [jnp.zeros((1, CB), jnp.int32)] * (LIST_ROWS - len(rows) - 1)
    block = jnp.concatenate(rows, axis=0)
    for p in range(PLANE):
        out_ref[p] = block


def chosen_kernel(lists_ref, low_ref, high_ref):
    row = lax.broadcasted_iota(jnp.int32, (CB, PCAP), 0)

    def fill(p, ref, at):
        for o in range(MEETINGS):
            pieces = [lists_ref[p, o * 4 + n : o * 4 + n + 1, :] for n in range(4)]
            codes = jnp.concatenate(pieces, axis=1)
            pick_first = jnp.where(row == (codes >> 7), 1.0, 0.0).astype(BF16)
            pick_second = jnp.where(row == (codes & (CB - 1)), 1.0, 0.0).astype(BF16)
            chosen = lax.dot_general(pick_first, pick_second, (((1,), (1,)), ((), ())), preferred_element_type=F32)
            ref[at, o] = chosen.astype(BF16)

    for p in range(ROUNDS):
        fill(p, low_ref, p)

    def one(p, carry):
        fill(p, high_ref, p - ROUNDS)
        return carry

    lax.fori_loop(ROUNDS, PLANE, one, 0)


def fill_bins(bins_ref):
    spread = lax.broadcasted_iota(jnp.int32, (CB, CB), 1) - lax.broadcasted_iota(jnp.int32, (CB, CB), 0)
    at = 0
    for o, k, lo, hi in SPANS:
        distance = spread[lo:hi] + CB * o
        inside = (distance >= BINW * k) & (distance < BINW * (k + 1))
        bins_ref[at : at + hi - lo, :] = jnp.where(inside, 1.0, 0.0).astype(BF16)
        at += hi - lo


def spread(straight_ref, swapped_ref, at, block):
    values = block.astype(F32)
    straight_ref[at] = values
    swapped_ref[at] = jnp.where(real_lanes(), -1.0, 1.0) * swap_parts(values)


def meet(out_ref, owner_ref, bins_ref, chosen_ref, at_block, block, straight_ref, swapped_ref, places, p):
    row_id = lax.broadcasted_iota(jnp.int32, (NBIN, WIDE), 0)
    at = 0
    pieces = []
    for o, _, lo, hi in SPANS:
        pieces.append(chosen_ref[at_block, o, lo:hi, :] * bins_ref[at : at + hi - lo, :])
        at += hi - lo
    mixed = jnp.dot(jnp.concatenate(pieces, axis=0), block, preferred_element_type=F32)
    at = 0
    found = []
    for o in range(MEETINGS):
        real = jnp.zeros((NBIN, WIDE), F32)
        imag = jnp.zeros((NBIN, WIDE), F32)
        for k, lo, hi in LEVELS[o]:
            part = mixed[at : at + hi - lo]
            at += hi - lo
            dims = ((hi - lo) // 8, 8, WIDE)
            straight = straight_ref[places[o], lo:hi, :]
            swapped = swapped_ref[places[o], lo:hi, :]
            along = jnp.sum(jnp.sum((straight * part).reshape(dims), axis=0), axis=0, keepdims=True)
            across = jnp.sum(jnp.sum((swapped * part).reshape(dims), axis=0), axis=0, keepdims=True)
            real = jnp.where(row_id == k, along, real)
            imag = jnp.where(row_id == k, across, imag)
        found.append(jnp.where(real_lanes(), fold(real), fold(imag)))
    for o in range(MEETINGS):
        owner = owner_ref[p, o]
        spot = (owner % PLANE) * ROWS + owner // PLANE
        out_ref[spot] = out_ref[spot] + found[o]


def plane_kernel(owner_ref, chosen_ref, group_ref, out_ref, bins_ref, straight_ref, swapped_ref):
    out_ref[...] = jnp.zeros(out_ref.shape, F32)
    fill_bins(bins_ref)
    for p in range(ROUNDS):
        spread(straight_ref, swapped_ref, p, group_ref[p])

    def one(p, carry):
        spread(straight_ref, swapped_ref, p, group_ref[p])
        places = [p - o for o in range(MEETINGS)]
        meet(
            out_ref, owner_ref, bins_ref, chosen_ref, p - ROUNDS, group_ref[p], straight_ref, swapped_ref, places, p
        )
        return carry

    lax.fori_loop(ROUNDS, PLANE, one, 0)


def below_kernel(
    owner_ref, chosen_ref, group_ref, below_ref, sums_ref, out_ref, bins_ref, straight_ref, swapped_ref
):
    out_ref[...] = sums_ref[...]
    fill_bins(bins_ref)
    for p in range(ROUNDS):
        spread(straight_ref, swapped_ref, p, below_ref[p])
        spread(straight_ref, swapped_ref, p + ROUNDS, group_ref[p])
    for p in range(ROUNDS):
        places = [p + ROUNDS - o for o in range(MEETINGS)]
        meet(out_ref, owner_ref, bins_ref, chosen_ref, p, group_ref[p], straight_ref, swapped_ref, places, p)


def lag_kernel(lag_ref, parts_ref, table_ref, out_ref):
    lane = lanes()
    sign = jnp.where(real_lanes(), -1.0, 1.0)
    merged = []
    for side in range(2):
        value = jnp.zeros((ROWS * NBIN, WIDE), F32)
        for n in range(8):
            value = jnp.where((lane >> 4) == n, parts_ref[side * 8 + n], value)
        merged.append(value)
    swapped = [swap_parts(value) for value in merged]
    turned = []
    for quarter in range(4):
        step = (lane * (quarter + 2)) & 3
        along = jnp.where(step == 0, 1.0, 0.0) - jnp.where(step == 2, 1.0, 0.0)
        across = sign * (jnp.where(step == 1, 1.0, 0.0) - jnp.where(step == 3, 1.0, 0.0))
        turned.append(jnp.concatenate([x * along + y * across for x, y in zip(merged, swapped)], axis=1))
    table = table_ref[lag_ref[0]]
    lagged = jnp.dot(jnp.concatenate(turned, axis=0), table, precision=HI, preferred_element_type=F32)
    for quarter in range(4):
        for y in range(ROWS):
            at = quarter * ROWS * NBIN + y * NBIN
            out_ref[y * 4 + quarter] = lagged[at : at + NBIN]


def windows(before, before_at, traces, at, taps, table):
    return pl.pallas_call(
        spectra_kernel,
        out_shape=shape((CB, WIN), BF16),
        grid=(1,),
        in_specs=[
            pl.BlockSpec((CB, TAPS), lambda n: (0, before_at)),
            pl.BlockSpec((CB, WIN), lambda n: (0, at)),
            pl.BlockSpec((2 * TAPS, TAPS), lambda n: (0, 0)),
            pl.BlockSpec((HALF, WIN), lambda n: (0, 0)),
        ],
        out_specs=pl.BlockSpec((CB, WIN), lambda n: (0, 0)),
        compiler_params=pltpu.CompilerParams(vmem_limit_bytes=VMEM_LIMIT),
    )(before, traces, taps, table)


def body(traces, owner_map, pair_codes, pair_count):
    blk = (lax.axis_index("row") * PLANE + lax.axis_index("plane")).astype(jnp.int32).reshape(1)
    lag = lax.axis_index("lag").astype(jnp.int32).reshape(1)
    taps = jnp.asarray(filter_table())
    table = jnp.asarray(transform_table())

    history = lax.ppermute(traces[:, -TAPS:], "lag", [(i, i + 1) for i in range(3)])

    spectra1 = windows(traces, WIN // TAPS - 1, traces, 1, taps, table)
    lists_shape = shape((PLANE, LIST_ROWS, CB), jnp.int32)
    lists = call(
        list_kernel,
        lists_shape,
        blk,
        pair_count.reshape(1, MEETINGS),
        owner_map.reshape(1, MEETINGS),
        pair_codes,
        smem=(0,),
    )
    lists, history, spectra1 = lax.optimization_barrier((lists, history, spectra1))
    lists = lax.all_to_all(lists, "plane", 0, 0, tiled=True)
    spectra0 = windows(history, 0, traces, 0, taps, table)
    slabs = call(pack_kernel, shape((PLANE * LAGS, 32, WIDE), BF16), spectra0, spectra1)
    slabs, lists = lax.optimization_barrier((slabs, lists))
    owners = lists[:, 4 * MEETINGS, :MEETINGS]
    halves = tuple(shape((n, MEETINGS, CB, CB), BF16) for n in (ROUNDS, PLANE - ROUNDS))
    chosen_low, chosen_high = call(chosen_kernel, halves, lists)

    slabs = lax.all_to_all(slabs, ("plane", "lag"), 0, 0, tiled=True)
    group = call(whiten_kernel, shape((PLANE, CB, WIDE), BF16), slabs)
    last, chosen_low, chosen_high = lax.optimization_barrier((group[PLANE - ROUNDS :], chosen_low, chosen_high))
    below = lax.ppermute(last, "row", [(i, i + 1) for i in range(ROWS - 1)])

    sums_shape = shape((ROWS * PLANE, NBIN, WIDE), F32)
    bins = pltpu.VMEM((SPAN_ROWS, CB), BF16)
    spare = pltpu.VMEM((PLANE, CB, WIDE), F32)
    few = pltpu.VMEM((2 * ROUNDS, CB, WIDE), F32)
    sums = call(plane_kernel, sums_shape, owners, chosen_high, group, smem=(0,), scratch=(bins, spare, spare))
    sums = call(
        below_kernel,
        sums_shape,
        owners,
        chosen_low,
        group,
        below,
        sums,
        smem=(0,),
        aliases={4: 0},
        scratch=(bins, few, few),
    )
    parts = lax.all_to_all(sums.reshape(PLANE, ROWS * NBIN, WIDE), "plane", 0, 0, tiled=True)
    table = jnp.asarray(inverse_table())
    lagged = call(lag_kernel, shape((ROWS * LAGS, NBIN, LANES), F32), lag, parts, table, smem=(0,))
    return jnp.sum(lax.all_to_all(lagged, ("row", "lag"), 0, 0, tiled=True), axis=0, keepdims=True)


def solution(mesh):
    split = Mesh(mesh.devices.reshape(ROWS, PLANE, 4), ("row", "plane", "lag"))
    owned = ("row", "plane")
    return jax.shard_map(
        body,
        mesh=split,
        in_specs=(P(owned, "lag"), P(None, owned), P(None, owned), P(None, owned)),
        out_specs=P(owned, None, "lag"),
        check_vma=False,
    )
```

```python
import math

import jax
import jax.numpy as jnp
import numpy as np
from jax import lax
from jax.experimental import pallas as pl
from jax.experimental.pallas import tpu as pltpu
from jax.sharding import Mesh
from jax.sharding import PartitionSpec as P

CB = 128
WIN = 1024
HALF = 512
NF = 512
TAPS = 128
NBIN = 8
BINW = 80
ROUNDS = 4
MEETINGS = 5
PCAP = 512
WINDOWS = 8
LANES = 256
PLANE = 16
ROWS = 4
LAGS = 4
WIDE = 128
BAND = 8
LIST_ROWS = 24

BAND_LOW = 0.02
BAND_HIGH = 0.48
WATER = 0.1

F32 = jnp.float32
BF16 = jnp.bfloat16
HI = lax.Precision.HIGHEST
VMEM_LIMIT = 16 * 1024 * 1024


def level_rows(o):
    found = []
    for k in range(NBIN):
        pairs = [
            i
            for i in range(CB)
            for j in range(CB)
            if (o > 0 or i < j) and (CB * o + j - i) // BINW == k
        ]
        if pairs:
            found.append((k, min(pairs) // 16 * 16, max(pairs) // 16 * 16 + 16))
    return tuple(found)


LEVELS = tuple(level_rows(o) for o in range(MEETINGS))
SPANS = tuple((o, k, lo, hi) for o in range(MEETINGS) for k, lo, hi in LEVELS[o])
SPAN_ROWS = sum(hi - lo for _, _, lo, hi in SPANS)


def filter_table():
    k = np.arange(TAPS, dtype=np.float64)
    m = k - (TAPS - 1) / 2.0
    ideal = 2 * BAND_HIGH * np.sinc(2 * BAND_HIGH * m) - 2 * BAND_LOW * np.sinc(2 * BAND_LOW * m)
    taps = ideal * (0.5 - 0.5 * np.cos(2 * np.pi * (k + 0.5) / TAPS))
    lagged = np.arange(TAPS)[None, :] - np.arange(2 * TAPS)[:, None] + TAPS
    inside = (lagged >= 0) & (lagged < TAPS)
    return np.where(inside, taps[np.clip(lagged, 0, TAPS - 1)], 0.0).astype(np.float32)


def column_order():
    column = np.arange(WIN)
    return column // (2 * BAND) * BAND + column % BAND, column // BAND % 2 == 1


def transform_table():
    freq, is_imag = column_order()
    angle = (np.arange(HALF)[:, None] * freq[None, :] % WIN) * (2 * np.pi / WIN)
    return (np.where(is_imag[None, :], -np.sin(angle), np.cos(angle)) / math.sqrt(WIN)).astype(jnp.bfloat16)


def inverse_table():
    freq, is_imag = column_order()
    angle = (freq[:, None] * np.arange(LANES)[None, :] % WIN) * (2 * np.pi / WIN)
    weight = np.where(freq == 0, 1.0, 2.0)[:, None] / (WINDOWS * math.sqrt(WIN))
    return (weight * np.where(is_imag[:, None], -np.sin(angle), np.cos(angle))).astype(np.float32)


def call(kernel, out_shape, *args, smem=(), aliases=None, scratch=()):
    specs = [
        pl.BlockSpec(memory_space=pltpu.SMEM) if n in smem else pl.BlockSpec(memory_space=pltpu.VMEM)
        for n in range(len(args))
    ]
    many = isinstance(out_shape, (tuple, list))
    out_specs = [pl.BlockSpec(memory_space=pltpu.VMEM)] * len(out_shape) if many else pl.BlockSpec(memory_space=pltpu.VMEM)
    return pl.pallas_call(
        kernel,
        out_shape=out_shape,
        in_specs=specs,
        out_specs=out_specs,
        input_output_aliases=aliases or {},
        scratch_shapes=list(scratch),
        compiler_params=pltpu.CompilerParams(vmem_limit_bytes=VMEM_LIMIT),
    )(*args)


def shape(dims, dtype):
    return jax.ShapeDtypeStruct(dims, dtype)


def lanes():
    return lax.broadcasted_iota(jnp.int32, (1, WIDE), 1)


def real_lanes():
    return (lanes() & BAND) == 0


def fold(values):
    for step in (BAND, 2 * BAND, 4 * BAND, 8 * BAND):
        values = values + pltpu.roll(values, step, 1)
    return values


def fold_table(real, imag):
    row = lax.broadcasted_iota(jnp.int32, (WIDE, WIDE), 0)
    column = lax.broadcasted_iota(jnp.int32, (WIDE, WIDE), 1)
    same = ((row ^ column) & (BAND - 1)) == 0
    asked = jnp.where((column & BAND) == 0, real, imag)
    return jnp.where(same, asked, 0.0).astype(BF16)


def swap_table():
    row = lax.broadcasted_iota(jnp.int32, (WIDE, WIDE), 0)
    column = lax.broadcasted_iota(jnp.int32, (WIDE, WIDE), 1)
    value = jnp.where((column & BAND) == 0, -1.0, 1.0)
    return jnp.where(row == (column ^ BAND), value, 0.0).astype(BF16)


def order_table():
    row = lax.broadcasted_iota(jnp.int32, (4 * WIDE, 1), 0)
    goal = ((row >> 5) & 3) * WIDE + (row >> 7) * 32 + (row & 31)
    column = lax.broadcasted_iota(jnp.int32, (4 * WIDE, 4 * WIDE), 1)
    return jnp.where(column == goal, 1.0, 0.0).astype(BF16)


def halves_of(values):
    high = values.astype(BF16)
    return high, (values - high.astype(F32)).astype(BF16)


def transpose_pieces(arrays, width):
    bit = 1
    while bit < len(arrays):
        upper = (lanes() & (bit * width)) != 0
        out = list(arrays)
        for q in range(len(arrays)):
            if q & bit:
                continue
            a, b = arrays[q], arrays[q | bit]
            out[q] = jnp.where(upper, pltpu.roll(b, bit * width, 1), a)
            out[q | bit] = jnp.where(upper, b, pltpu.roll(a, WIDE - bit * width, 1))
        arrays = out
        bit *= 2
    return arrays


def spectra_kernel(hist_ref, x_ref, taps_ref, table_ref, out_ref):
    tiles = [hist_ref[...]] + [x_ref[:, t * TAPS : (t + 1) * TAPS] for t in range(WIN // TAPS)]
    pairs = [jnp.concatenate([tiles[t], tiles[t + 1]], axis=1) for t in range(WIN // TAPS)]
    rows = jnp.dot(jnp.concatenate(pairs, axis=0), taps_ref[...], precision=HI, preferred_element_type=F32)
    rows = rows.astype(BF16)
    filtered = [rows[t * CB : (t + 1) * CB] for t in range(WIN // TAPS)]
    early = jnp.concatenate(filtered[:4], axis=1)
    late = jnp.concatenate(filtered[4:], axis=1)
    column = lax.broadcasted_iota(jnp.int32, (1, WIN), 1)
    turn = jnp.where(column % 2 == 0, 1.0, -1.0).astype(F32)
    first = jnp.dot(early, table_ref[...], preferred_element_type=F32)
    second = jnp.dot(late, table_ref[...], preferred_element_type=F32)
    out_ref[...] = (first + turn * second).astype(BF16)


def pack_kernel(s0_ref, s1_ref, out_ref):
    for c in range(WIN // WIDE):
        cols = slice(c * WIDE, (c + 1) * WIDE)
        pieces = []
        for g in range(4):
            for ref in (s0_ref, s1_ref):
                pieces.append(ref[g * 32 : (g + 1) * 32, cols].astype(F32))
        for e, value in enumerate(transpose_pieces(pieces, 2 * BAND)):
            out_ref[c * 8 + e] = value.astype(BF16)


def whiten_kernel(slab_ref, low_ref, high_ref, low_swapped_ref, high_swapped_ref):
    order = order_table()
    both = fold_table(1.0, 1.0)
    both = jnp.concatenate([both, both], axis=0)
    swap = swap_table()
    batch = 4
    for first in range(0, PLANE, batch):
        rows = []
        for p in range(first, first + batch):
            rows.append(jnp.concatenate([slab_ref[p * LAGS + n] for n in range(LAGS)], axis=1))
        values = jnp.dot(jnp.concatenate(rows, axis=0), order, preferred_element_type=F32)
        values = jnp.concatenate([values[:, g * WIDE : (g + 1) * WIDE] for g in range(4)], axis=0)
        high, low = halves_of(values * values)
        power = jnp.dot(jnp.concatenate([high, low], axis=1), both, preferred_element_type=F32)
        whitened = (values * lax.rsqrt(power * (1.0 / WINDOWS) + WATER)).astype(BF16)
        turned = jnp.dot(whitened, swap, preferred_element_type=F32).astype(BF16)
        for n in range(batch):
            at_block = first + n if first < ROUNDS else first + n - ROUNDS
            out_ref = low_ref if first < ROUNDS else high_ref
            swapped_ref = low_swapped_ref if first < ROUNDS else high_swapped_ref
            for g in range(4):
                at = (g * batch + n) * 32
                out_ref[at_block, g * 32 : (g + 1) * 32, :] = whitened[at : at + 32]
                swapped_ref[at_block, g * 32 : (g + 1) * 32, :] = turned[at : at + 32]


def list_kernel(blk_ref, count_ref, owner_ref, codes_ref, out_ref):
    lane = lax.broadcasted_iota(jnp.int32, (1, CB), 1)
    rows = []
    owners = jnp.zeros((1, CB), jnp.int32)
    for o in range(MEETINGS):
        live = jnp.where(blk_ref[0] >= o, count_ref[:, o : o + 1], 0)
        for n in range(4):
            rows.append(jnp.where(lane + n * CB < live, codes_ref[o : o + 1, n * CB : (n + 1) * CB], -1))
        owner = owner_ref[:, o : o + 1]
        owners = jnp.where(lane == o, (owner & (PLANE - 1)) * ROWS + (owner >> 4), owners)
    rows = rows + [owners] + [jnp.zeros((1, CB), jnp.int32)] * (LIST_ROWS - len(rows) - 1)
    block = jnp.concatenate(rows, axis=0)
    for p in range(PLANE):
        out_ref[p] = block


def chosen_kernel(lists_ref, low_ref, high_ref):
    row = lax.broadcasted_iota(jnp.int32, (CB, PCAP), 0)

    def fill(p, ref, at):
        for o in range(MEETINGS):
            pieces = [lists_ref[p, o * 4 + n : o * 4 + n + 1, :] for n in range(4)]
            codes = jnp.concatenate(pieces, axis=1)
            pick_first = jnp.where(row == (codes >> 7), 1.0, 0.0).astype(BF16)
            pick_second = jnp.where(row == (codes & (CB - 1)), 1.0, 0.0).astype(BF16)
            chosen = lax.dot_general(pick_first, pick_second, (((1,), (1,)), ((), ())), preferred_element_type=F32)
            ref[at, o] = chosen.astype(BF16)

    for p in range(ROUNDS):
        fill(p, low_ref, p)

    def one(p, carry):
        fill(p, high_ref, p - ROUNDS)
        return carry

    lax.fori_loop(ROUNDS, PLANE, one, 0, unroll=4)


def fill_bins(bins_ref):
    spread = lax.broadcasted_iota(jnp.int32, (CB, CB), 1) - lax.broadcasted_iota(jnp.int32, (CB, CB), 0)
    at = 0
    for o, k, lo, hi in SPANS:
        distance = spread[lo:hi] + CB * o
        inside = (distance >= BINW * k) & (distance < BINW * (k + 1))
        bins_ref[at : at + hi - lo, :] = jnp.where(inside, 1.0, 0.0).astype(BF16)
        at += hi - lo


def meet(out_ref, owner_ref, bins_ref, chosen_ref, at_block, block, partners, p):
    row_id = lax.broadcasted_iota(jnp.int32, (NBIN, WIDE), 0)
    at = 0
    pieces = []
    for o, _, lo, hi in SPANS:
        pieces.append(chosen_ref[at_block, o, lo:hi, :] * bins_ref[at : at + hi - lo, :])
        at += hi - lo
    mixed = jnp.dot(jnp.concatenate(pieces, axis=0), block, preferred_element_type=F32)
    at = 0
    real, imag = [], []
    for o in range(MEETINGS):
        straight = partners[o][0].astype(F32)
        swapped = partners[o][1].astype(F32)
        for k, lo, hi in LEVELS[o]:
            part = mixed[at : at + hi - lo]
            at += hi - lo
            dims = ((hi - lo) // 8, 8, WIDE)
            real.append(jnp.sum((straight[lo:hi] * part).reshape(dims), axis=0))
            imag.append(jnp.sum((swapped[lo:hi] * part).reshape(dims), axis=0))
    at = 0
    for o in range(MEETINGS):
        re = jnp.zeros((NBIN, WIDE), F32)
        im = jnp.zeros((NBIN, WIDE), F32)
        for k, _, _ in LEVELS[o]:
            re = jnp.where(row_id == k, jnp.sum(real[at], axis=0, keepdims=True), re)
            im = jnp.where(row_id == k, jnp.sum(imag[at], axis=0, keepdims=True), im)
            at += 1
        found = jnp.where(real_lanes(), fold(re), fold(im))
        spot = owner_ref[p, o]
        out_ref[spot] = out_ref[spot] + found


def plane_kernel(
    owner_ref, chosen_ref, low_ref, high_ref, low_swapped_ref, high_swapped_ref, out_ref, bins_ref, group_ref, swapped_ref
):
    out_ref[...] = jnp.zeros(out_ref.shape, F32)
    fill_bins(bins_ref)
    group_ref[:ROUNDS] = low_ref[...]
    group_ref[ROUNDS:] = high_ref[...]
    swapped_ref[:ROUNDS] = low_swapped_ref[...]
    swapped_ref[ROUNDS:] = high_swapped_ref[...]

    def one(p, carry):
        partners = [(group_ref[p - o], swapped_ref[p - o]) for o in range(MEETINGS)]
        meet(out_ref, owner_ref, bins_ref, chosen_ref, p - ROUNDS, group_ref[p], partners, p)
        return carry

    lax.fori_loop(ROUNDS, PLANE, one, 0, unroll=4)


def below_kernel(owner_ref, chosen_ref, group_ref, swapped_ref, below_ref, sums_ref, out_ref, bins_ref, total_ref):
    total_ref[...] = sums_ref[...]
    fill_bins(bins_ref)
    swap = swap_table()
    under = []
    for n in range(ROUNDS):
        block = below_ref[n]
        under.append((block, jnp.dot(block, swap, preferred_element_type=F32).astype(BF16)))
    for p in range(ROUNDS):
        partners = [
            (group_ref[p - o], swapped_ref[p - o]) if p >= o else under[p - o + ROUNDS] for o in range(MEETINGS)
        ]
        meet(total_ref, owner_ref, bins_ref, chosen_ref, p, group_ref[p], partners, p)
    row_id = lax.broadcasted_iota(jnp.int32, (NBIN, WIDE), 0)
    own_piece = (lanes() >> 4) == row_id
    for n in range(PLANE):
        rows = jnp.zeros((NBIN, WIDE), F32)
        for y in range(ROWS):
            value = jnp.where(own_piece, total_ref[n * ROWS + y], 0.0)
            rows = jnp.where(row_id == y, jnp.sum(value, axis=0, keepdims=True), rows)
        for lag in range(LAGS):
            out_ref[n * LAGS + lag] = rows


def lag_kernel(lag_ref, parts_ref, table_ref, out_ref):
    lane = lanes()
    sign = jnp.where(real_lanes(), -1.0, 1.0)
    step = (lane * (lag_ref[0] + 2)) & 3
    along = jnp.where(step == 0, 1.0, 0.0) - jnp.where(step == 2, 1.0, 0.0)
    across = sign * (jnp.where(step == 1, 1.0, 0.0) - jnp.where(step == 3, 1.0, 0.0))
    columns = []
    for first in range(0, PLANE * LAGS, 8):
        bins = transpose_pieces([parts_ref[first + n] for n in range(8)], 2 * BAND)
        value = jnp.concatenate(bins, axis=0)
        swapped = jnp.where(real_lanes(), pltpu.roll(value, WIDE - BAND, 1), pltpu.roll(value, BAND, 1))
        columns.append(value * along + swapped * across)
    lagged = jnp.dot(jnp.concatenate(columns, axis=1), table_ref[...], precision=HI, preferred_element_type=F32)
    for y in range(ROWS):
        for k in range(NBIN):
            out_ref[y, k : k + 1, :] = lagged[k * 8 + y : k * 8 + y + 1]


def later_kernel(traces_ref, taps_ref, table_ref, out_ref, x_ref, h_ref, d_ref, sems):
    copies = [
        pltpu.make_async_copy(traces_ref.at[:, WIN - TAPS :], x_ref, sems.at[0]),
        pltpu.make_async_copy(taps_ref, h_ref, sems.at[1]),
        pltpu.make_async_copy(table_ref, d_ref, sems.at[2]),
    ]
    for copy in copies:
        copy.start()
    for copy in copies:
        copy.wait()
    spectra_kernel(x_ref.at[:, :TAPS], x_ref.at[:, TAPS:], h_ref, d_ref, out_ref)


def later_window(traces, taps, table):
    return pl.pallas_call(
        later_kernel,
        out_shape=shape((CB, WIN), BF16),
        in_specs=[pl.BlockSpec(memory_space=pltpu.HBM)] * 3,
        out_specs=pl.BlockSpec(memory_space=pltpu.VMEM),
        scratch_shapes=[
            pltpu.VMEM((CB, WIN + TAPS), F32),
            pltpu.VMEM((2 * TAPS, TAPS), F32),
            pltpu.VMEM((HALF, WIN), BF16),
            pltpu.SemaphoreType.DMA((3,)),
        ],
        compiler_params=pltpu.CompilerParams(vmem_limit_bytes=VMEM_LIMIT),
    )(*[pltpu.with_memory_space_constraint(value, pltpu.HBM) for value in (traces, taps, table)])


def first_window(history, traces, taps, table):
    return pl.pallas_call(
        spectra_kernel,
        out_shape=shape((CB, WIN), BF16),
        grid=(1,),
        in_specs=[
            pl.BlockSpec((CB, TAPS), lambda n: (0, 0)),
            pl.BlockSpec((CB, WIN), lambda n: (0, 0)),
            pl.BlockSpec((2 * TAPS, TAPS), lambda n: (0, 0)),
            pl.BlockSpec((HALF, WIN), lambda n: (0, 0)),
        ],
        out_specs=pl.BlockSpec((CB, WIN), lambda n: (0, 0)),
        compiler_params=pltpu.CompilerParams(vmem_limit_bytes=VMEM_LIMIT),
    )(history, traces, taps, table)


def row_below(blocks):
    return lax.ppermute(blocks, "row", [(i, i + 1) for i in range(ROWS - 1)])


def middle(lists, owners, slabs, send):
    halves = tuple(shape((n, MEETINGS, CB, CB), BF16) for n in (ROUNDS, PLANE - ROUNDS))
    chosen_low, chosen_high = call(chosen_kernel, halves, lists)
    low_shape = shape((ROUNDS, CB, WIDE), BF16)
    high_shape = shape((PLANE - ROUNDS, CB, WIDE), BF16)
    low, high, low_swapped, high_swapped = call(
        whiten_kernel, (low_shape, high_shape, low_shape, high_shape), slabs
    )
    last, chosen_low, chosen_high = lax.optimization_barrier((high[-ROUNDS:], chosen_low, chosen_high))
    below = send(last)
    sums_shape = shape((ROWS * PLANE, NBIN, WIDE), F32)
    bins = pltpu.VMEM((SPAN_ROWS, CB), BF16)
    blocks = pltpu.VMEM((PLANE, CB, WIDE), BF16)
    sums = call(
        plane_kernel,
        sums_shape,
        owners,
        chosen_high,
        low,
        high,
        low_swapped,
        high_swapped,
        smem=(0,),
        scratch=(bins, blocks, blocks),
    )
    sums = call(
        below_kernel,
        sums_shape,
        owners,
        chosen_low,
        low,
        low_swapped,
        below,
        sums,
        smem=(0,),
        scratch=(bins, pltpu.VMEM(sums_shape.shape, F32)),
    )
    return sums, high


def body(traces, owner_map, pair_codes, pair_count):
    blk = (lax.axis_index("row") * PLANE + lax.axis_index("plane")).astype(jnp.int32).reshape(1)
    lag = lax.axis_index("lag").astype(jnp.int32).reshape(1)
    taps = jnp.asarray(filter_table())
    table = jnp.asarray(transform_table())

    history = lax.ppermute(traces[:, -TAPS:], "lag", [(i, i + 1) for i in range(3)])

    spectra1 = later_window(traces, taps, table)
    lists_shape = shape((PLANE, LIST_ROWS, CB), jnp.int32)
    lists = call(
        list_kernel,
        lists_shape,
        blk,
        pair_count.reshape(1, MEETINGS),
        owner_map.reshape(1, MEETINGS),
        pair_codes,
        smem=(0,),
    )
    lists, history, spectra1 = lax.optimization_barrier((lists, history, spectra1))
    lists = lax.all_to_all(lists, "plane", 0, 0, tiled=True)
    spectra0 = first_window(history, traces, taps, table)
    slabs = call(pack_kernel, shape((PLANE * LAGS, 32, WIDE), BF16), spectra0, spectra1)
    slabs, lists = lax.optimization_barrier((slabs, lists))
    owners = lists[:, 4 * MEETINGS, :MEETINGS]
    slabs = lax.all_to_all(slabs, ("plane", "lag"), 0, 0, tiled=True)
    sums, _ = middle(lists, owners, slabs, row_below)
    parts = lax.all_to_all(sums, ("plane", "lag"), 0, 0, tiled=True)
    table = jnp.asarray(inverse_table())
    lagged = call(lag_kernel, shape((ROWS, NBIN, LANES), F32), lag, parts, table, smem=(0,))
    return jnp.sum(lax.all_to_all(lagged, "row", 0, 0, tiled=True), axis=0, keepdims=True)


def solution(mesh):
    split = Mesh(mesh.devices.reshape(ROWS, PLANE, 4), ("row", "plane", "lag"))
    owned = ("row", "plane")
    return jax.shard_map(
        body,
        mesh=split,
        in_specs=(P(owned, "lag"), P(None, owned), P(None, owned), P(None, owned)),
        out_specs=P(owned, None, "lag"),
        check_vma=False,
    )
```

```python
import math

import jax
import jax.numpy as jnp
import numpy as np
from jax import lax
from jax.experimental import pallas as pl
from jax.experimental.pallas import tpu as pltpu
from jax.sharding import Mesh
from jax.sharding import PartitionSpec as P

CB = 128
WIN = 1024
HALF = 512
NF = 512
TAPS = 128
NBIN = 8
BINW = 80
ROUNDS = 4
MEETINGS = 5
PCAP = 512
WINDOWS = 8
LANES = 256
PLANE = 16
ROWS = 4
LAGS = 4
WIDE = 128
BAND = 8
DATA_ROWS = 32
SLAB_ROWS = 40

BAND_LOW = 0.02
BAND_HIGH = 0.48
WATER = 0.1

F32 = jnp.float32
BF16 = jnp.bfloat16
HI = lax.Precision.HIGHEST
VMEM_LIMIT = 16 * 1024 * 1024


def level_rows(o):
    found = []
    for k in range(NBIN):
        pairs = [
            i
            for i in range(CB)
            for j in range(CB)
            if (o > 0 or i < j) and (CB * o + j - i) // BINW == k
        ]
        if pairs:
            found.append((k, min(pairs) // 16 * 16, max(pairs) // 16 * 16 + 16))
    return tuple(found)


LEVELS = tuple(level_rows(o) for o in range(MEETINGS))
SPANS = tuple((o, k, lo, hi) for o in range(MEETINGS) for k, lo, hi in LEVELS[o])
SPAN_ROWS = sum(hi - lo for _, _, lo, hi in SPANS)


def filter_table():
    k = np.arange(TAPS, dtype=np.float64)
    m = k - (TAPS - 1) / 2.0
    ideal = 2 * BAND_HIGH * np.sinc(2 * BAND_HIGH * m) - 2 * BAND_LOW * np.sinc(2 * BAND_LOW * m)
    taps = ideal * (0.5 - 0.5 * np.cos(2 * np.pi * (k + 0.5) / TAPS))
    lagged = np.arange(TAPS)[None, :] - np.arange(2 * TAPS)[:, None] + TAPS
    inside = (lagged >= 0) & (lagged < TAPS)
    return np.where(inside, taps[np.clip(lagged, 0, TAPS - 1)], 0.0).astype(np.float32)


def column_order():
    column = np.arange(WIN)
    return column // (2 * BAND) * BAND + column % BAND, column // BAND % 2 == 1


def transform_table():
    freq, is_imag = column_order()
    angle = (np.arange(HALF)[:, None] * freq[None, :] % WIN) * (2 * np.pi / WIN)
    return (np.where(is_imag[None, :], -np.sin(angle), np.cos(angle)) / math.sqrt(WIN)).astype(jnp.bfloat16)


def inverse_table():
    freq, is_imag = column_order()
    angle = (freq[:, None] * np.arange(LANES)[None, :] % WIN) * (2 * np.pi / WIN)
    weight = np.where(freq == 0, 1.0, 2.0)[:, None] / (WINDOWS * math.sqrt(WIN))
    return (weight * np.where(is_imag[:, None], -np.sin(angle), np.cos(angle))).astype(np.float32)


def call(kernel, out_shape, *args, smem=(), aliases=None, scratch=()):
    specs = [
        pl.BlockSpec(memory_space=pltpu.SMEM) if n in smem else pl.BlockSpec(memory_space=pltpu.VMEM)
        for n in range(len(args))
    ]
    many = isinstance(out_shape, (tuple, list))
    out_specs = [pl.BlockSpec(memory_space=pltpu.VMEM)] * len(out_shape) if many else pl.BlockSpec(memory_space=pltpu.VMEM)
    return pl.pallas_call(
        kernel,
        out_shape=out_shape,
        in_specs=specs,
        out_specs=out_specs,
        input_output_aliases=aliases or {},
        scratch_shapes=list(scratch),
        compiler_params=pltpu.CompilerParams(vmem_limit_bytes=VMEM_LIMIT),
    )(*args)


def shape(dims, dtype):
    return jax.ShapeDtypeStruct(dims, dtype)


def lanes():
    return lax.broadcasted_iota(jnp.int32, (1, WIDE), 1)


def real_lanes():
    return (lanes() & BAND) == 0


def fold(values):
    for step in (BAND, 2 * BAND, 4 * BAND, 8 * BAND):
        values = values + pltpu.roll(values, step, 1)
    return values


def fold_table(real, imag):
    row = lax.broadcasted_iota(jnp.int32, (WIDE, WIDE), 0)
    column = lax.broadcasted_iota(jnp.int32, (WIDE, WIDE), 1)
    same = ((row ^ column) & (BAND - 1)) == 0
    asked = jnp.where((column & BAND) == 0, real, imag)
    return jnp.where(same, asked, 0.0).astype(BF16)


def swap_table():
    row = lax.broadcasted_iota(jnp.int32, (WIDE, WIDE), 0)
    column = lax.broadcasted_iota(jnp.int32, (WIDE, WIDE), 1)
    value = jnp.where((column & BAND) == 0, -1.0, 1.0)
    return jnp.where(row == (column ^ BAND), value, 0.0).astype(BF16)


def order_table():
    row = lax.broadcasted_iota(jnp.int32, (4 * WIDE, 1), 0)
    goal = ((row >> 5) & 3) * WIDE + (row >> 7) * 32 + (row & 31)
    column = lax.broadcasted_iota(jnp.int32, (4 * WIDE, 4 * WIDE), 1)
    return jnp.where(column == goal, 1.0, 0.0).astype(BF16)


def halves_of(values):
    high = values.astype(BF16)
    return high, (values - high.astype(F32)).astype(BF16)


def transpose_pieces(arrays, width):
    bit = 1
    while bit < len(arrays):
        upper = (lanes() & (bit * width)) != 0
        out = list(arrays)
        for q in range(len(arrays)):
            if q & bit:
                continue
            a, b = arrays[q], arrays[q | bit]
            out[q] = jnp.where(upper, pltpu.roll(b, bit * width, 1), a)
            out[q | bit] = jnp.where(upper, b, pltpu.roll(a, WIDE - bit * width, 1))
        arrays = out
        bit *= 2
    return arrays


def spectra_kernel(hist_ref, x_ref, taps_ref, table_ref, out_ref):
    tiles = [hist_ref[...]] + [x_ref[:, t * TAPS : (t + 1) * TAPS] for t in range(WIN // TAPS)]
    pairs = [jnp.concatenate([tiles[t], tiles[t + 1]], axis=1) for t in range(WIN // TAPS)]
    rows = jnp.dot(jnp.concatenate(pairs, axis=0), taps_ref[...], precision=HI, preferred_element_type=F32)
    rows = rows.astype(BF16)
    filtered = [rows[t * CB : (t + 1) * CB] for t in range(WIN // TAPS)]
    early = jnp.concatenate(filtered[:4], axis=1)
    late = jnp.concatenate(filtered[4:], axis=1)
    column = lax.broadcasted_iota(jnp.int32, (1, WIN), 1)
    turn = jnp.where(column % 2 == 0, 1.0, -1.0).astype(F32)
    first = jnp.dot(early, table_ref[...], preferred_element_type=F32)
    second = jnp.dot(late, table_ref[...], preferred_element_type=F32)
    out_ref[...] = (first + turn * second).astype(BF16)


def list_rows(place_ref, count_ref, owner_ref, codes_ref):
    lane = lanes()
    start = pl.multiple_of(place_ref[1] * WIDE, WIDE)
    codes = codes_ref[:, pl.ds(start, WIDE)]
    exponent = codes >> 8
    value = 1.0 + (codes & (CB - 1)).astype(F32) * (1.0 / CB)
    for bit in range(6):
        value = jnp.where(((exponent >> bit) & 1) == 1, value * 2.0 ** (1 << bit), value)
    value = jnp.where(((codes >> 7) & 1) == 1, -value, value)
    rows = []
    owners = jnp.zeros((1, WIDE), F32)
    for o in range(MEETINGS):
        live = jnp.where(place_ref[0] >= o, count_ref[:, o : o + 1], 0)
        rows.append(jnp.where(lane + start < live, value[o : o + 1], 0.0))
        owner = owner_ref[:, o : o + 1]
        spot = (owner & (PLANE - 1)) * ROWS + (owner >> 4)
        owners = jnp.where(lane == o, spot.astype(F32), owners)
    rows = rows + [owners] + [jnp.zeros((1, WIDE), F32)] * (SLAB_ROWS - DATA_ROWS - MEETINGS - 1)
    return jnp.concatenate(rows, axis=0).astype(BF16)


def pack_kernel(place_ref, count_ref, owner_ref, codes_ref, s0_ref, s1_ref, out_ref):
    lists = list_rows(place_ref, count_ref, owner_ref, codes_ref)
    for c in range(WIN // WIDE):
        cols = slice(c * WIDE, (c + 1) * WIDE)
        pieces = []
        for g in range(4):
            for ref in (s0_ref, s1_ref):
                pieces.append(ref[g * 32 : (g + 1) * 32, cols].astype(F32))
        for e, value in enumerate(transpose_pieces(pieces, 2 * BAND)):
            out_ref[c * 8 + e, :DATA_ROWS, :] = value.astype(BF16)
            out_ref[c * 8 + e, DATA_ROWS:, :] = lists


def whiten_kernel(slab_ref, out_ref, swapped_ref, last_ref):
    order = order_table()
    both = fold_table(1.0, 1.0)
    both = jnp.concatenate([both, both], axis=0)
    swap = swap_table()
    batch = 4
    for first in range(0, PLANE, batch):
        rows = []
        for p in range(first, first + batch):
            rows.append(jnp.concatenate([slab_ref[p * LAGS + n, :DATA_ROWS, :] for n in range(LAGS)], axis=1))
        values = jnp.dot(jnp.concatenate(rows, axis=0), order, preferred_element_type=F32)
        values = jnp.concatenate([values[:, g * WIDE : (g + 1) * WIDE] for g in range(4)], axis=0)
        high, low = halves_of(values * values)
        power = jnp.dot(jnp.concatenate([high, low], axis=1), both, preferred_element_type=F32)
        whitened = (values * lax.rsqrt(power * (1.0 / WINDOWS) + WATER)).astype(BF16)
        turned = jnp.dot(whitened, swap, preferred_element_type=F32).astype(BF16)
        for n in range(batch):
            for g in range(4):
                at = (g * batch + n) * 32
                out_ref[first + n, g * 32 : (g + 1) * 32, :] = whitened[at : at + 32]
                swapped_ref[first + n, g * 32 : (g + 1) * 32, :] = turned[at : at + 32]
                if first == PLANE - ROUNDS:
                    last_ref[n, g * 32 : (g + 1) * 32, :] = whitened[at : at + 32]


def chosen_kernel(slab_ref, out_ref, owner_ref):
    row = lax.broadcasted_iota(jnp.int32, (CB, PCAP), 0).astype(F32)

    def one(p, carry):
        value = jnp.concatenate([slab_ref[p * LAGS + n, DATA_ROWS:, :] for n in range(LAGS)], axis=1).astype(F32)
        owner_ref[pl.ds(p, 1), :] = value[MEETINGS : MEETINGS + 1, :WIDE].astype(jnp.int32)
        odd = jnp.where(value < 0.0, 1.0, 0.0)
        size = jnp.abs(value)
        live = size > 0.0
        exponent = jnp.zeros(value.shape, F32)
        for bit in (5, 4, 3, 2, 1, 0):
            large = size >= 2.0 ** (1 << bit)
            size = jnp.where(large, size * 2.0 ** -(1 << bit), size)
            exponent = jnp.where(large, exponent + 2.0**bit, exponent)
        first = jnp.where(live, 2.0 * exponent + odd, -1.0)
        second = (size - 1.0) * CB
        for o in range(MEETINGS):
            pick_first = jnp.where(row == first[o : o + 1], 1.0, 0.0).astype(BF16)
            pick_second = jnp.where(row == second[o : o + 1], 1.0, 0.0).astype(BF16)
            chosen = lax.dot_general(pick_first, pick_second, (((1,), (1,)), ((), ())), preferred_element_type=F32)
            out_ref[p, o] = chosen.astype(BF16)
        return carry

    lax.fori_loop(0, PLANE, one, 0, unroll=4)


def fill_bins(bins_ref):
    spread = lax.broadcasted_iota(jnp.int32, (CB, CB), 1) - lax.broadcasted_iota(jnp.int32, (CB, CB), 0)
    at = 0
    for o, k, lo, hi in SPANS:
        distance = spread[lo:hi] + CB * o
        inside = (distance >= BINW * k) & (distance < BINW * (k + 1))
        bins_ref[at : at + hi - lo, :] = jnp.where(inside, 1.0, 0.0).astype(BF16)
        at += hi - lo


def meet(out_ref, owner_ref, bins_ref, chosen_ref, at_block, block, partners, p):
    row_id = lax.broadcasted_iota(jnp.int32, (NBIN, WIDE), 0)
    at = 0
    pieces = []
    for o, _, lo, hi in SPANS:
        pieces.append(chosen_ref[at_block, o, lo:hi, :] * bins_ref[at : at + hi - lo, :])
        at += hi - lo
    mixed = jnp.dot(jnp.concatenate(pieces, axis=0), block, preferred_element_type=F32)
    at = 0
    real, imag = [], []
    for o in range(MEETINGS):
        straight = partners[o][0].astype(F32)
        swapped = partners[o][1].astype(F32)
        for k, lo, hi in LEVELS[o]:
            part = mixed[at : at + hi - lo]
            at += hi - lo
            dims = ((hi - lo) // 8, 8, WIDE)
            real.append(jnp.sum((straight[lo:hi] * part).reshape(dims), axis=0))
            imag.append(jnp.sum((swapped[lo:hi] * part).reshape(dims), axis=0))
    at = 0
    for o in range(MEETINGS):
        re = jnp.zeros((NBIN, WIDE), F32)
        im = jnp.zeros((NBIN, WIDE), F32)
        for k, _, _ in LEVELS[o]:
            re = jnp.where(row_id == k, jnp.sum(real[at], axis=0, keepdims=True), re)
            im = jnp.where(row_id == k, jnp.sum(imag[at], axis=0, keepdims=True), im)
            at += 1
        found = jnp.where(real_lanes(), fold(re), fold(im))
        spot = owner_ref[p, o]
        out_ref[spot] = out_ref[spot] + found


def meetings_kernel(
    owner_ref, chosen_ref, group_ref, swapped_ref, below_ref, out_ref, bins_ref, all_ref, turned_ref, total_ref
):
    total_ref[...] = jnp.zeros(total_ref.shape, F32)
    fill_bins(bins_ref)
    swap = swap_table()
    for n in range(ROUNDS):
        all_ref[n] = below_ref[n]
        turned_ref[n] = jnp.dot(below_ref[n], swap, preferred_element_type=F32).astype(BF16)
    all_ref[ROUNDS:] = group_ref[...]
    turned_ref[ROUNDS:] = swapped_ref[...]

    def one(p, carry):
        partners = [(all_ref[p + ROUNDS - o], turned_ref[p + ROUNDS - o]) for o in range(MEETINGS)]
        meet(total_ref, owner_ref, bins_ref, chosen_ref, p, group_ref[p], partners, p)
        return carry

    lax.fori_loop(0, PLANE, one, 0, unroll=4)
    row_id = lax.broadcasted_iota(jnp.int32, (NBIN, WIDE), 0)
    own_piece = (lanes() >> 4) == row_id
    for n in range(PLANE):
        rows = jnp.zeros((NBIN, WIDE), F32)
        for y in range(ROWS):
            value = jnp.where(own_piece, total_ref[n * ROWS + y], 0.0)
            rows = jnp.where(row_id == y, jnp.sum(value, axis=0, keepdims=True), rows)
        for lag in range(LAGS):
            out_ref[n * LAGS + lag] = rows


def lag_kernel(lag_ref, parts_ref, table_ref, out_ref):
    lane = lanes()
    sign = jnp.where(real_lanes(), -1.0, 1.0)
    step = (lane * (lag_ref[0] + 2)) & 3
    along = jnp.where(step == 0, 1.0, 0.0) - jnp.where(step == 2, 1.0, 0.0)
    across = sign * (jnp.where(step == 1, 1.0, 0.0) - jnp.where(step == 3, 1.0, 0.0))
    columns = []
    for first in range(0, PLANE * LAGS, 8):
        bins = transpose_pieces([parts_ref[first + n] for n in range(8)], 2 * BAND)
        value = jnp.concatenate(bins, axis=0)
        swapped = jnp.where(real_lanes(), pltpu.roll(value, WIDE - BAND, 1), pltpu.roll(value, BAND, 1))
        columns.append(value * along + swapped * across)
    lagged = jnp.dot(jnp.concatenate(columns, axis=1), table_ref[...], precision=HI, preferred_element_type=F32)
    for y in range(ROWS):
        for k in range(NBIN):
            out_ref[y, k : k + 1, :] = lagged[k * 8 + y : k * 8 + y + 1]


def later_kernel(traces_ref, taps_ref, table_ref, out_ref, x_ref, h_ref, d_ref, sems):
    copies = [
        pltpu.make_async_copy(traces_ref.at[:, WIN - TAPS :], x_ref, sems.at[0]),
        pltpu.make_async_copy(taps_ref, h_ref, sems.at[1]),
        pltpu.make_async_copy(table_ref, d_ref, sems.at[2]),
    ]
    for copy in copies:
        copy.start()
    for copy in copies:
        copy.wait()
    spectra_kernel(x_ref.at[:, :TAPS], x_ref.at[:, TAPS:], h_ref, d_ref, out_ref)


def later_window(traces, taps, table):
    return pl.pallas_call(
        later_kernel,
        out_shape=shape((CB, WIN), BF16),
        in_specs=[pl.BlockSpec(memory_space=pltpu.HBM)] * 3,
        out_specs=pl.BlockSpec(memory_space=pltpu.VMEM),
        scratch_shapes=[
            pltpu.VMEM((CB, WIN + TAPS), F32),
            pltpu.VMEM((2 * TAPS, TAPS), F32),
            pltpu.VMEM((HALF, WIN), BF16),
            pltpu.SemaphoreType.DMA((3,)),
        ],
        compiler_params=pltpu.CompilerParams(vmem_limit_bytes=VMEM_LIMIT),
    )(*[pltpu.with_memory_space_constraint(value, pltpu.HBM) for value in (traces, taps, table)])


def first_window(history, traces, taps, table):
    return pl.pallas_call(
        spectra_kernel,
        out_shape=shape((CB, WIN), BF16),
        grid=(1,),
        in_specs=[
            pl.BlockSpec((CB, TAPS), lambda n: (0, 0)),
            pl.BlockSpec((CB, WIN), lambda n: (0, 0)),
            pl.BlockSpec((2 * TAPS, TAPS), lambda n: (0, 0)),
            pl.BlockSpec((HALF, WIN), lambda n: (0, 0)),
        ],
        out_specs=pl.BlockSpec((CB, WIN), lambda n: (0, 0)),
        compiler_params=pltpu.CompilerParams(vmem_limit_bytes=VMEM_LIMIT),
    )(history, traces, taps, table)


def row_below(blocks):
    return lax.ppermute(blocks, "row", [(i, i + 1) for i in range(ROWS - 1)])


def middle(slabs, send):
    blocks = (PLANE, CB, WIDE)
    group, swapped, last = call(
        whiten_kernel, (shape(blocks, BF16), shape(blocks, BF16), shape((ROUNDS, CB, WIDE), BF16)), slabs
    )
    below = send(last)
    chosen, owners = call(
        chosen_kernel, (shape((PLANE, MEETINGS, CB, CB), BF16), shape((PLANE, WIDE), jnp.int32)), slabs
    )
    sums_shape = (ROWS * PLANE, NBIN, WIDE)
    more = pltpu.VMEM((PLANE + ROUNDS, CB, WIDE), BF16)
    return call(
        meetings_kernel,
        shape(sums_shape, F32),
        owners,
        chosen,
        group,
        swapped,
        below,
        smem=(0,),
        scratch=(pltpu.VMEM((SPAN_ROWS, CB), BF16), more, more, pltpu.VMEM(sums_shape, F32)),
    )


def body(traces, owner_map, pair_codes, pair_count):
    blk = (lax.axis_index("row") * PLANE + lax.axis_index("plane")).astype(jnp.int32)
    lag = lax.axis_index("lag").astype(jnp.int32)
    taps = jnp.asarray(filter_table())
    table = jnp.asarray(transform_table())

    history = lax.ppermute(traces[:, -TAPS:], "lag", [(i, i + 1) for i in range(3)])

    spectra1 = later_window(traces, taps, table)
    spectra0 = first_window(history, traces, taps, table)
    slabs = call(
        pack_kernel,
        shape((PLANE * LAGS, SLAB_ROWS, WIDE), BF16),
        jnp.stack([blk, lag]),
        pair_count.reshape(1, MEETINGS),
        owner_map.reshape(1, MEETINGS),
        pair_codes,
        spectra0,
        spectra1,
        smem=(0,),
    )
    slabs = lax.all_to_all(slabs, ("plane", "lag"), 0, 0, tiled=True)
    sums = middle(slabs, row_below)
    parts = lax.all_to_all(sums, ("plane", "lag"), 0, 0, tiled=True)
    table = jnp.asarray(inverse_table())
    lagged = call(lag_kernel, shape((ROWS, NBIN, LANES), F32), lag.reshape(1), parts, table, smem=(0,))
    return jnp.sum(lax.all_to_all(lagged, "row", 0, 0, tiled=True), axis=0, keepdims=True)


def solution(mesh):
    split = Mesh(mesh.devices.reshape(ROWS, PLANE, 4), ("row", "plane", "lag"))
    owned = ("row", "plane")
    return jax.shard_map(
        body,
        mesh=split,
        in_specs=(P(owned, "lag"), P(None, owned), P(None, owned), P(None, owned)),
        out_specs=P(owned, None, "lag"),
        check_vma=False,
    )
```

```python
import math

import jax
import jax.numpy as jnp
import numpy as np
from jax import lax
from jax.experimental import pallas as pl
from jax.experimental.pallas import tpu as pltpu
from jax.sharding import Mesh
from jax.sharding import PartitionSpec as P

CB = 128
WIN = 1024
HALF = 512
NF = 512
TAPS = 128
NBIN = 8
BINW = 80
ROUNDS = 4
MEETINGS = 5
PCAP = 512
WINDOWS = 8
LANES = 256
PLANE = 16
ROWS = 4
LAGS = 4
WIDE = 128
BAND = 8
DATA_ROWS = 32
SLAB_ROWS = 40

BAND_LOW = 0.02
BAND_HIGH = 0.48
WATER = 0.1

F32 = jnp.float32
BF16 = jnp.bfloat16
VMEM_LIMIT = 16 * 1024 * 1024


def level_rows(o):
    found = []
    for k in range(NBIN):
        pairs = [
            i
            for i in range(CB)
            for j in range(CB)
            if (o > 0 or i < j) and (CB * o + j - i) // BINW == k
        ]
        if pairs:
            found.append((k, min(pairs) // 16 * 16, max(pairs) // 16 * 16 + 16))
    return tuple(found)


LEVELS = tuple(level_rows(o) for o in range(MEETINGS))
SPANS = tuple((o, k, lo, hi) for o in range(MEETINGS) for k, lo, hi in LEVELS[o])
SPAN_ROWS = sum(hi - lo for _, _, lo, hi in SPANS)


def two_terms(table):
    high = table.astype(jnp.bfloat16)
    low = (table - high.astype(np.float32)).astype(jnp.bfloat16)
    return np.concatenate([high, low], axis=1)


def filter_table():
    k = np.arange(TAPS, dtype=np.float64)
    m = k - (TAPS - 1) / 2.0
    ideal = 2 * BAND_HIGH * np.sinc(2 * BAND_HIGH * m) - 2 * BAND_LOW * np.sinc(2 * BAND_LOW * m)
    taps = ideal * (0.5 - 0.5 * np.cos(2 * np.pi * (k + 0.5) / TAPS))
    lagged = np.arange(TAPS)[None, :] - np.arange(2 * TAPS)[:, None] + TAPS
    inside = (lagged >= 0) & (lagged < TAPS)
    return two_terms(np.where(inside, taps[np.clip(lagged, 0, TAPS - 1)], 0.0).astype(np.float32))


def column_order():
    column = np.arange(WIN)
    return column // (2 * BAND) * BAND + column % BAND, column // BAND % 2 == 1


def transform_table():
    freq, is_imag = column_order()
    angle = (np.arange(HALF)[:, None] * freq[None, :] % WIN) * (2 * np.pi / WIN)
    return (np.where(is_imag[None, :], -np.sin(angle), np.cos(angle)) / math.sqrt(WIN)).astype(jnp.bfloat16)


def inverse_table():
    freq, is_imag = column_order()
    angle = (freq[:, None] * np.arange(LANES)[None, :] % WIN) * (2 * np.pi / WIN)
    weight = np.where(freq == 0, 1.0, 2.0)[:, None] / (WINDOWS * math.sqrt(WIN))
    return two_terms((weight * np.where(is_imag[:, None], -np.sin(angle), np.cos(angle))).astype(np.float32))


def call(kernel, out_shape, *args, smem=(), aliases=None, scratch=()):
    specs = [
        pl.BlockSpec(memory_space=pltpu.SMEM) if n in smem else pl.BlockSpec(memory_space=pltpu.VMEM)
        for n in range(len(args))
    ]
    many = isinstance(out_shape, (tuple, list))
    out_specs = [pl.BlockSpec(memory_space=pltpu.VMEM)] * len(out_shape) if many else pl.BlockSpec(memory_space=pltpu.VMEM)
    return pl.pallas_call(
        kernel,
        out_shape=out_shape,
        in_specs=specs,
        out_specs=out_specs,
        input_output_aliases=aliases or {},
        scratch_shapes=list(scratch),
        compiler_params=pltpu.CompilerParams(vmem_limit_bytes=VMEM_LIMIT),
    )(*args)


def shape(dims, dtype):
    return jax.ShapeDtypeStruct(dims, dtype)


def lanes():
    return lax.broadcasted_iota(jnp.int32, (1, WIDE), 1)


def real_lanes():
    return (lanes() & BAND) == 0


def fold(values):
    for step in (BAND, 2 * BAND, 4 * BAND, 8 * BAND):
        values = values + pltpu.roll(values, step, 1)
    return values


def fold_table(real, imag):
    row = lax.broadcasted_iota(jnp.int32, (WIDE, WIDE), 0)
    column = lax.broadcasted_iota(jnp.int32, (WIDE, WIDE), 1)
    same = ((row ^ column) & (BAND - 1)) == 0
    asked = jnp.where((column & BAND) == 0, real, imag)
    return jnp.where(same, asked, 0.0).astype(BF16)


def swap_table():
    row = lax.broadcasted_iota(jnp.int32, (WIDE, WIDE), 0)
    column = lax.broadcasted_iota(jnp.int32, (WIDE, WIDE), 1)
    value = jnp.where((column & BAND) == 0, -1.0, 1.0)
    return jnp.where(row == (column ^ BAND), value, 0.0).astype(BF16)


def order_table():
    row = lax.broadcasted_iota(jnp.int32, (4 * WIDE, 1), 0)
    goal = ((row >> 5) & 3) * WIDE + (row >> 7) * 32 + (row & 31)
    column = lax.broadcasted_iota(jnp.int32, (4 * WIDE, 4 * WIDE), 1)
    return jnp.where(column == goal, 1.0, 0.0).astype(BF16)


def halves_of(values):
    high = values.astype(BF16)
    return high, (values - high.astype(F32)).astype(BF16)


def split_dot(values, table):
    high, low = halves_of(values)
    count, width = values.shape[0], table.shape[1] // 2
    out = jnp.dot(jnp.concatenate([high, low], axis=0), table, preferred_element_type=F32)
    small = out[count:, width:] + (out[count:, :width] + out[:count, width:])
    return small + out[:count, :width]


def transpose_pieces(arrays, width):
    bit = 1
    while bit < len(arrays):
        upper = (lanes() & (bit * width)) != 0
        out = list(arrays)
        for q in range(len(arrays)):
            if q & bit:
                continue
            a, b = arrays[q], arrays[q | bit]
            out[q] = jnp.where(upper, pltpu.roll(b, bit * width, 1), a)
            out[q | bit] = jnp.where(upper, b, pltpu.roll(a, WIDE - bit * width, 1))
        arrays = out
        bit *= 2
    return arrays


def spectra_kernel(hist_ref, x_ref, taps_ref, table_ref, out_ref, ready=None):
    tiles = [hist_ref[...]] + [x_ref[:, t * TAPS : (t + 1) * TAPS] for t in range(WIN // TAPS)]
    pairs = [jnp.concatenate([tiles[t], tiles[t + 1]], axis=1) for t in range(WIN // TAPS)]
    rows = split_dot(jnp.concatenate(pairs, axis=0), taps_ref[...]).astype(BF16)
    filtered = [rows[t * CB : (t + 1) * CB] for t in range(WIN // TAPS)]
    early = jnp.concatenate(filtered[:4], axis=1)
    late = jnp.concatenate(filtered[4:], axis=1)
    if ready is not None:
        ready()
    column = lax.broadcasted_iota(jnp.int32, (1, WIN), 1)
    turn = jnp.where(column % 2 == 0, 1.0, -1.0).astype(F32)
    first = jnp.dot(early, table_ref[...], preferred_element_type=F32)
    second = jnp.dot(late, table_ref[...], preferred_element_type=F32)
    out_ref[...] = (first + turn * second).astype(BF16)


def pack_table():
    row = lax.broadcasted_iota(jnp.int32, (4 * WIDE, 1), 0)
    goal = ((row >> 4) & 3) * WIDE + ((row >> 6) & 1) * (WIDE // 2) + (row >> 7) * 16 + (row & 15)
    column = lax.broadcasted_iota(jnp.int32, (4 * WIDE, 4 * WIDE), 1)
    return jnp.where(column == goal, 1.0, 0.0).astype(BF16)


def list_rows(place_ref, count_ref, owner_ref, codes_ref):
    lane = lanes()
    start = pl.multiple_of(place_ref[1] * WIDE, WIDE)
    codes = codes_ref[:, pl.ds(start, WIDE)]
    exponent = codes >> 8
    value = 1.0 + (codes & (CB - 1)).astype(F32) * (1.0 / CB)
    for bit in range(6):
        value = jnp.where(((exponent >> bit) & 1) == 1, value * 2.0 ** (1 << bit), value)
    value = jnp.where(((codes >> 7) & 1) == 1, -value, value)
    rows = []
    owners = jnp.zeros((1, WIDE), F32)
    for o in range(MEETINGS):
        live = jnp.where(place_ref[0] >= o, count_ref[:, o : o + 1], 0)
        rows.append(jnp.where(lane + start < live, value[o : o + 1], 0.0))
        owner = owner_ref[:, o : o + 1]
        spot = (owner & (PLANE - 1)) * ROWS + (owner >> 4)
        owners = jnp.where(lane == o, spot.astype(F32), owners)
    rows = rows + [owners] + [jnp.zeros((1, WIDE), F32)] * (SLAB_ROWS - DATA_ROWS - MEETINGS - 1)
    return jnp.concatenate(rows, axis=0).astype(BF16)


def pack_kernel(place_ref, count_ref, owner_ref, codes_ref, s0_ref, s1_ref, out_ref):
    lists = list_rows(place_ref, count_ref, owner_ref, codes_ref)
    order = pack_table()
    for c in range(WIN // WIDE):
        cols = slice(c * WIDE, (c + 1) * WIDE)
        halves = []
        for g in range(0, 4, 2):
            pieces = [ref[n * 32 : (n + 1) * 32, cols] for n in (g, g + 1) for ref in (s0_ref, s1_ref)]
            halves.append(jnp.concatenate(pieces, axis=1))
        mixed = jnp.dot(jnp.concatenate(halves, axis=0), order, preferred_element_type=F32)
        upper = lanes() >= WIDE // 2
        for e in range(4):
            first = mixed[:DATA_ROWS, e * WIDE : (e + 1) * WIDE]
            second = mixed[DATA_ROWS:, e * WIDE : (e + 1) * WIDE]
            low = jnp.where(upper, pltpu.roll(second, WIDE // 2, 1), first)
            high = jnp.where(upper, second, pltpu.roll(first, WIDE // 2, 1))
            for d, value in ((c * 8 + e, low), (c * 8 + e + 4, high)):
                out_ref[d, :DATA_ROWS, :] = value.astype(BF16)
                out_ref[d, DATA_ROWS:, :] = lists


def whiten_kernel(slab_ref, out_ref, swapped_ref, last_ref):
    order = order_table()
    both = fold_table(1.0, 1.0)
    both = jnp.concatenate([both, both], axis=0)
    swap = swap_table()
    batch = 4
    for first in range(0, PLANE, batch):
        rows = []
        for p in range(first, first + batch):
            rows.append(jnp.concatenate([slab_ref[p * LAGS + n, :DATA_ROWS, :] for n in range(LAGS)], axis=1))
        values = jnp.dot(jnp.concatenate(rows, axis=0), order, preferred_element_type=F32)
        values = jnp.concatenate([values[:, g * WIDE : (g + 1) * WIDE] for g in range(4)], axis=0)
        high, low = halves_of(values * values)
        power = jnp.dot(jnp.concatenate([high, low], axis=1), both, preferred_element_type=F32)
        whitened = (values * lax.rsqrt(power * (1.0 / WINDOWS) + WATER)).astype(BF16)
        turned = jnp.dot(whitened, swap, preferred_element_type=F32).astype(BF16)
        for n in range(batch):
            for g in range(4):
                at = (g * batch + n) * 32
                out_ref[first + n, g * 32 : (g + 1) * 32, :] = whitened[at : at + 32]
                swapped_ref[first + n, g * 32 : (g + 1) * 32, :] = turned[at : at + 32]
                if first == PLANE - ROUNDS:
                    last_ref[n, g * 32 : (g + 1) * 32, :] = whitened[at : at + 32]


def chosen_kernel(slab_ref, out_ref, owner_ref):
    row = lax.broadcasted_iota(jnp.int32, (CB, PCAP), 0).astype(F32)

    def one(p, carry):
        value = jnp.concatenate([slab_ref[p * LAGS + n, DATA_ROWS:, :] for n in range(LAGS)], axis=1).astype(F32)
        owner_ref[pl.ds(p, 1), :] = value[MEETINGS : MEETINGS + 1, :WIDE].astype(jnp.int32)
        odd = jnp.where(value < 0.0, 1.0, 0.0)
        size = jnp.abs(value)
        live = size > 0.0
        exponent = jnp.zeros(value.shape, F32)
        for bit in (5, 4, 3, 2, 1, 0):
            large = size >= 2.0 ** (1 << bit)
            size = jnp.where(large, size * 2.0 ** -(1 << bit), size)
            exponent = jnp.where(large, exponent + 2.0**bit, exponent)
        first = jnp.where(live, 2.0 * exponent + odd, -1.0)
        second = (size - 1.0) * CB
        for o in range(MEETINGS):
            pick_first = jnp.where(row == first[o : o + 1], 1.0, 0.0).astype(BF16)
            pick_second = jnp.where(row == second[o : o + 1], 1.0, 0.0).astype(BF16)
            chosen = lax.dot_general(pick_first, pick_second, (((1,), (1,)), ((), ())), preferred_element_type=F32)
            out_ref[p, o] = chosen.astype(BF16)
        return carry

    lax.fori_loop(0, PLANE, one, 0, unroll=16)


def fill_bins(bins_ref):
    spread = lax.broadcasted_iota(jnp.int32, (CB, CB), 1) - lax.broadcasted_iota(jnp.int32, (CB, CB), 0)
    at = 0
    for o, k, lo, hi in SPANS:
        distance = spread[lo:hi] + CB * o
        inside = (distance >= BINW * k) & (distance < BINW * (k + 1))
        bins_ref[at : at + hi - lo, :] = jnp.where(inside, 1.0, 0.0).astype(BF16)
        at += hi - lo


def meet(out_ref, owner_ref, bins_ref, chosen_ref, at_block, block, partners, p):
    row_id = lax.broadcasted_iota(jnp.int32, (NBIN, WIDE), 0)
    at = 0
    pieces = []
    for o, _, lo, hi in SPANS:
        pieces.append(chosen_ref[at_block, o, lo:hi, :] * bins_ref[at : at + hi - lo, :])
        at += hi - lo
    mixed = jnp.dot(jnp.concatenate(pieces, axis=0), block, preferred_element_type=F32)
    at = 0
    real, imag = [], []
    for o in range(MEETINGS):
        straight = partners[o][0].astype(F32)
        swapped = partners[o][1].astype(F32)
        for k, lo, hi in LEVELS[o]:
            part = mixed[at : at + hi - lo]
            at += hi - lo
            dims = ((hi - lo) // 8, 8, WIDE)
            real.append(jnp.sum((straight[lo:hi] * part).reshape(dims), axis=0))
            imag.append(jnp.sum((swapped[lo:hi] * part).reshape(dims), axis=0))
    at = 0
    for o in range(MEETINGS):
        re = jnp.zeros((NBIN, WIDE), F32)
        im = jnp.zeros((NBIN, WIDE), F32)
        for k, _, _ in LEVELS[o]:
            re = jnp.where(row_id == k, jnp.sum(real[at], axis=0, keepdims=True), re)
            im = jnp.where(row_id == k, jnp.sum(imag[at], axis=0, keepdims=True), im)
            at += 1
        found = jnp.where(real_lanes(), fold(re), fold(im))
        spot = owner_ref[p, o]
        out_ref[spot] = out_ref[spot] + found


def meetings_kernel(
    owner_ref, chosen_ref, group_ref, swapped_ref, below_ref, out_ref, bins_ref, all_ref, turned_ref, total_ref
):
    total_ref[...] = jnp.zeros(total_ref.shape, F32)
    fill_bins(bins_ref)
    swap = swap_table()
    for n in range(ROUNDS):
        all_ref[n] = below_ref[n]
        turned_ref[n] = jnp.dot(below_ref[n], swap, preferred_element_type=F32).astype(BF16)
    all_ref[ROUNDS:] = group_ref[...]
    turned_ref[ROUNDS:] = swapped_ref[...]

    def one(p, carry):
        partners = [(all_ref[p + ROUNDS - o], turned_ref[p + ROUNDS - o]) for o in range(MEETINGS)]
        meet(total_ref, owner_ref, bins_ref, chosen_ref, p, group_ref[p], partners, p)
        return carry

    lax.fori_loop(0, PLANE, one, 0, unroll=16)
    row_id = lax.broadcasted_iota(jnp.int32, (NBIN, WIDE), 0)
    own_piece = (lanes() >> 4) == row_id
    for n in range(PLANE):
        rows = jnp.zeros((NBIN, WIDE), F32)
        for y in range(ROWS):
            value = jnp.where(own_piece, total_ref[n * ROWS + y], 0.0)
            rows = jnp.where(row_id == y, jnp.sum(value, axis=0, keepdims=True), rows)
        for lag in range(LAGS):
            out_ref[n * LAGS + lag] = rows


def lag_kernel(lag_ref, parts_ref, table_ref, out_ref):
    lane = lanes()
    sign = jnp.where(real_lanes(), -1.0, 1.0)
    step = (lane * (lag_ref[0] + 2)) & 3
    along = jnp.where(step == 0, 1.0, 0.0) - jnp.where(step == 2, 1.0, 0.0)
    across = sign * (jnp.where(step == 1, 1.0, 0.0) - jnp.where(step == 3, 1.0, 0.0))
    columns = []
    for first in range(0, PLANE * LAGS, 8):
        bins = transpose_pieces([parts_ref[first + n] for n in range(8)], 2 * BAND)
        value = jnp.concatenate(bins, axis=0)
        swapped = jnp.where(real_lanes(), pltpu.roll(value, WIDE - BAND, 1), pltpu.roll(value, BAND, 1))
        columns.append(value * along + swapped * across)
    lagged = split_dot(jnp.concatenate(columns, axis=1), table_ref[...])
    for y in range(ROWS):
        for k in range(NBIN):
            out_ref[y, k : k + 1, :] = lagged[k * 8 + y : k * 8 + y + 1]


def later_kernel(traces_ref, taps_ref, table_ref, out_ref, x_ref, h_ref, d_ref, sems):
    copies = [
        pltpu.make_async_copy(traces_ref.at[:, WIN - TAPS :], x_ref, sems.at[0]),
        pltpu.make_async_copy(taps_ref, h_ref, sems.at[1]),
        pltpu.make_async_copy(table_ref, d_ref, sems.at[2]),
    ]
    for copy in copies:
        copy.start()
    copies[0].wait()
    copies[1].wait()
    spectra_kernel(x_ref.at[:, :TAPS], x_ref.at[:, TAPS:], h_ref, d_ref, out_ref, copies[2].wait)


def later_window(traces, taps, table):
    return pl.pallas_call(
        later_kernel,
        out_shape=shape((CB, WIN), BF16),
        in_specs=[pl.BlockSpec(memory_space=pltpu.HBM)] * 3,
        out_specs=pl.BlockSpec(memory_space=pltpu.VMEM),
        scratch_shapes=[
            pltpu.VMEM((CB, WIN + TAPS), F32),
            pltpu.VMEM((2 * TAPS, 2 * TAPS), BF16),
            pltpu.VMEM((HALF, WIN), BF16),
            pltpu.SemaphoreType.DMA((3,)),
        ],
        compiler_params=pltpu.CompilerParams(vmem_limit_bytes=VMEM_LIMIT),
    )(*[pltpu.with_memory_space_constraint(value, pltpu.HBM) for value in (traces, taps, table)])


def first_window(history, traces, taps, table):
    return pl.pallas_call(
        spectra_kernel,
        out_shape=shape((CB, WIN), BF16),
        grid=(1,),
        in_specs=[
            pl.BlockSpec((CB, TAPS), lambda n: (0, 0)),
            pl.BlockSpec((CB, WIN), lambda n: (0, 0)),
            pl.BlockSpec((2 * TAPS, 2 * TAPS), lambda n: (0, 0)),
            pl.BlockSpec((HALF, WIN), lambda n: (0, 0)),
        ],
        out_specs=pl.BlockSpec((CB, WIN), lambda n: (0, 0)),
        compiler_params=pltpu.CompilerParams(vmem_limit_bytes=VMEM_LIMIT),
    )(history, traces, taps, table)


def row_below(blocks):
    return lax.ppermute(blocks, "row", [(i, i + 1) for i in range(ROWS - 1)])


def middle(slabs, send):
    blocks = (PLANE, CB, WIDE)
    group, swapped, last = call(
        whiten_kernel, (shape(blocks, BF16), shape(blocks, BF16), shape((ROUNDS, CB, WIDE), BF16)), slabs
    )
    below = send(last)
    chosen, owners = call(
        chosen_kernel, (shape((PLANE, MEETINGS, CB, CB), BF16), shape((PLANE, WIDE), jnp.int32)), slabs
    )
    sums_shape = (ROWS * PLANE, NBIN, WIDE)
    more = pltpu.VMEM((PLANE + ROUNDS, CB, WIDE), BF16)
    return call(
        meetings_kernel,
        shape(sums_shape, F32),
        owners,
        chosen,
        group,
        swapped,
        below,
        smem=(0,),
        scratch=(pltpu.VMEM((SPAN_ROWS, CB), BF16), more, more, pltpu.VMEM(sums_shape, F32)),
    )


def body(traces, owner_map, pair_codes, pair_count):
    blk = (lax.axis_index("row") * PLANE + lax.axis_index("plane")).astype(jnp.int32)
    lag = lax.axis_index("lag").astype(jnp.int32)
    taps = jnp.asarray(filter_table())
    table = jnp.asarray(transform_table())

    history = lax.ppermute(traces[:, -TAPS:], "lag", [(i, i + 1) for i in range(3)])

    spectra1 = later_window(traces, taps, table)
    spectra0 = first_window(history, traces, taps, table)
    slabs = call(
        pack_kernel,
        shape((PLANE * LAGS, SLAB_ROWS, WIDE), BF16),
        jnp.stack([blk, lag]),
        pair_count.reshape(1, MEETINGS),
        owner_map.reshape(1, MEETINGS),
        pair_codes,
        spectra0,
        spectra1,
        smem=(0,),
    )
    slabs = lax.all_to_all(slabs, ("plane", "lag"), 0, 0, tiled=True)
    sums = middle(slabs, row_below)
    parts = lax.all_to_all(sums, ("plane", "lag"), 0, 0, tiled=True)
    table = jnp.asarray(inverse_table())
    lagged = call(lag_kernel, shape((ROWS, NBIN, LANES), F32), lag.reshape(1), parts, table, smem=(0,))
    return jnp.sum(lax.all_to_all(lagged, "row", 0, 0, tiled=True), axis=0, keepdims=True)


def solution(mesh):
    split = Mesh(mesh.devices.reshape(ROWS, PLANE, 4), ("row", "plane", "lag"))
    owned = ("row", "plane")
    return jax.shard_map(
        body,
        mesh=split,
        in_specs=(P(owned, "lag"), P(None, owned), P(None, owned), P(None, owned)),
        out_specs=P(owned, None, "lag"),
        check_vma=False,
    )
```

```python
import math

import jax
import jax.numpy as jnp
import numpy as np
from jax import lax
from jax.experimental import pallas as pl
from jax.experimental.pallas import tpu as pltpu
from jax.sharding import Mesh
from jax.sharding import PartitionSpec as P

CB = 128
WIN = 1024
HALF = 512
NF = 512
TAPS = 128
NBIN = 8
BINW = 80
ROUNDS = 4
MEETINGS = 5
PCAP = 512
WINDOWS = 8
LANES = 256
PLANE = 16
ROWS = 4
LAGS = 4
WIDE = 128
BAND = 8
DATA_ROWS = 32
SLAB_ROWS = 40

BAND_LOW = 0.02
BAND_HIGH = 0.48
WATER = 0.1

F32 = jnp.float32
BF16 = jnp.bfloat16
VMEM_LIMIT = 16 * 1024 * 1024


def level_rows(o):
    found = []
    for k in range(NBIN):
        pairs = [
            i
            for i in range(CB)
            for j in range(CB)
            if (o > 0 or i < j) and (CB * o + j - i) // BINW == k
        ]
        if pairs:
            found.append((k, min(pairs) // 16 * 16, max(pairs) // 16 * 16 + 16))
    return tuple(found)


LEVELS = tuple(level_rows(o) for o in range(MEETINGS))
SPANS = tuple((o, k, lo, hi) for o in range(MEETINGS) for k, lo, hi in LEVELS[o])
SPAN_ROWS = sum(hi - lo for _, _, lo, hi in SPANS)


def two_terms(table):
    high = table.astype(jnp.bfloat16)
    low = (table - high.astype(np.float32)).astype(jnp.bfloat16)
    return np.concatenate([high, low], axis=1)


def filter_table():
    k = np.arange(TAPS, dtype=np.float64)
    m = k - (TAPS - 1) / 2.0
    ideal = 2 * BAND_HIGH * np.sinc(2 * BAND_HIGH * m) - 2 * BAND_LOW * np.sinc(2 * BAND_LOW * m)
    taps = ideal * (0.5 - 0.5 * np.cos(2 * np.pi * (k + 0.5) / TAPS))
    lagged = np.arange(TAPS)[None, :] - np.arange(2 * TAPS)[:, None] + TAPS
    inside = (lagged >= 0) & (lagged < TAPS)
    return two_terms(np.where(inside, taps[np.clip(lagged, 0, TAPS - 1)], 0.0).astype(np.float32))


def column_order():
    column = np.arange(WIN)
    return column // (2 * BAND) * BAND + column % BAND, column // BAND % 2 == 1


def transform_table():
    freq, is_imag = column_order()
    angle = (np.arange(HALF)[:, None] * freq[None, :] % WIN) * (2 * np.pi / WIN)
    return (np.where(is_imag[None, :], -np.sin(angle), np.cos(angle)) / math.sqrt(WIN)).astype(jnp.bfloat16)


def inverse_table():
    freq, is_imag = column_order()
    angle = (freq[:, None] * np.arange(LANES)[None, :] % WIN) * (2 * np.pi / WIN)
    weight = np.where(freq == 0, 1.0, 2.0)[:, None] / (WINDOWS * math.sqrt(WIN))
    return two_terms((weight * np.where(is_imag[:, None], -np.sin(angle), np.cos(angle))).astype(np.float32))


def call(kernel, out_shape, *args, smem=(), aliases=None, scratch=()):
    specs = [
        pl.BlockSpec(memory_space=pltpu.SMEM) if n in smem else pl.BlockSpec(memory_space=pltpu.VMEM)
        for n in range(len(args))
    ]
    many = isinstance(out_shape, (tuple, list))
    out_specs = [pl.BlockSpec(memory_space=pltpu.VMEM)] * len(out_shape) if many else pl.BlockSpec(memory_space=pltpu.VMEM)
    return pl.pallas_call(
        kernel,
        out_shape=out_shape,
        in_specs=specs,
        out_specs=out_specs,
        input_output_aliases=aliases or {},
        scratch_shapes=list(scratch),
        compiler_params=pltpu.CompilerParams(vmem_limit_bytes=VMEM_LIMIT),
    )(*args)


def shape(dims, dtype):
    return jax.ShapeDtypeStruct(dims, dtype)


def lanes():
    return lax.broadcasted_iota(jnp.int32, (1, WIDE), 1)


def real_lanes():
    return (lanes() & BAND) == 0


def fold(values):
    for step in (BAND, 2 * BAND, 4 * BAND, 8 * BAND):
        values = values + pltpu.roll(values, step, 1)
    return values


def fold_table(real, imag):
    row = lax.broadcasted_iota(jnp.int32, (WIDE, WIDE), 0)
    column = lax.broadcasted_iota(jnp.int32, (WIDE, WIDE), 1)
    same = ((row ^ column) & (BAND - 1)) == 0
    asked = jnp.where((column & BAND) == 0, real, imag)
    return jnp.where(same, asked, 0.0).astype(BF16)


def swap_table():
    row = lax.broadcasted_iota(jnp.int32, (WIDE, WIDE), 0)
    column = lax.broadcasted_iota(jnp.int32, (WIDE, WIDE), 1)
    value = jnp.where((column & BAND) == 0, -1.0, 1.0)
    return jnp.where(row == (column ^ BAND), value, 0.0).astype(BF16)


def order_table():
    row = lax.broadcasted_iota(jnp.int32, (4 * WIDE, 1), 0)
    goal = ((row >> 5) & 3) * WIDE + (row >> 7) * 32 + (row & 31)
    column = lax.broadcasted_iota(jnp.int32, (4 * WIDE, 4 * WIDE), 1)
    return jnp.where(column == goal, 1.0, 0.0).astype(BF16)


def halves_of(values):
    high = values.astype(BF16)
    return high, (values - high.astype(F32)).astype(BF16)


def split_dot(values, table):
    high, low = halves_of(values)
    count, width = values.shape[0], table.shape[1] // 2
    out = jnp.dot(jnp.concatenate([high, low], axis=0), table, preferred_element_type=F32)
    small = out[count:, width:] + (out[count:, :width] + out[:count, width:])
    return small + out[:count, :width]


def transpose_pieces(arrays, width):
    bit = 1
    while bit < len(arrays):
        upper = (lanes() & (bit * width)) != 0
        out = list(arrays)
        for q in range(len(arrays)):
            if q & bit:
                continue
            a, b = arrays[q], arrays[q | bit]
            out[q] = jnp.where(upper, pltpu.roll(b, bit * width, 1), a)
            out[q | bit] = jnp.where(upper, b, pltpu.roll(a, WIDE - bit * width, 1))
        arrays = out
        bit *= 2
    return arrays


def spectra_kernel(hist_ref, x_ref, taps_ref, table_ref, out_ref, ready=None):
    tiles = [hist_ref[...]] + [x_ref[:, t * TAPS : (t + 1) * TAPS] for t in range(WIN // TAPS)]
    pairs = [jnp.concatenate([tiles[t], tiles[t + 1]], axis=1) for t in range(WIN // TAPS)]
    rows = split_dot(jnp.concatenate(pairs, axis=0), taps_ref[...]).astype(BF16)
    filtered = [rows[t * CB : (t + 1) * CB] for t in range(WIN // TAPS)]
    early = jnp.concatenate(filtered[:4], axis=1)
    late = jnp.concatenate(filtered[4:], axis=1)
    if ready is not None:
        ready()
    column = lax.broadcasted_iota(jnp.int32, (1, WIN), 1)
    turn = jnp.where(column % 2 == 0, 1.0, -1.0).astype(F32)
    first = jnp.dot(early, table_ref[...], preferred_element_type=F32)
    second = jnp.dot(late, table_ref[...], preferred_element_type=F32)
    out_ref[...] = (first + turn * second).astype(BF16)


def pack_table():
    row = lax.broadcasted_iota(jnp.int32, (4 * WIDE, 1), 0)
    goal = ((row >> 4) & 3) * WIDE + ((row >> 6) & 1) * (WIDE // 2) + (row >> 7) * 16 + (row & 15)
    column = lax.broadcasted_iota(jnp.int32, (4 * WIDE, 4 * WIDE), 1)
    return jnp.where(column == goal, 1.0, 0.0).astype(BF16)


def list_rows(place_ref, count_ref, owner_ref, codes_ref):
    lane = lanes()
    start = pl.multiple_of(place_ref[1] * WIDE, WIDE)
    codes = codes_ref[:, pl.ds(start, WIDE)]
    exponent = codes >> 8
    value = 1.0 + (codes & (CB - 1)).astype(F32) * (1.0 / CB)
    for bit in range(6):
        value = jnp.where(((exponent >> bit) & 1) == 1, value * 2.0 ** (1 << bit), value)
    value = jnp.where(((codes >> 7) & 1) == 1, -value, value)
    rows = []
    owners = jnp.zeros((1, WIDE), F32)
    for o in range(MEETINGS):
        live = jnp.where(place_ref[0] >= o, count_ref[:, o : o + 1], 0)
        rows.append(jnp.where(lane + start < live, value[o : o + 1], 0.0))
        owner = owner_ref[:, o : o + 1]
        owners = jnp.where(lane == o, owner.astype(F32), owners)
    rows = rows + [owners] + [jnp.zeros((1, WIDE), F32)] * (SLAB_ROWS - DATA_ROWS - MEETINGS - 1)
    return jnp.concatenate(rows, axis=0).astype(BF16)


def pack_kernel(place_ref, count_ref, owner_ref, codes_ref, s0_ref, s1_ref, out_ref):
    lists = list_rows(place_ref, count_ref, owner_ref, codes_ref)
    order = pack_table()
    for c in range(WIN // WIDE):
        cols = slice(c * WIDE, (c + 1) * WIDE)
        halves = []
        for g in range(0, 4, 2):
            pieces = [ref[n * 32 : (n + 1) * 32, cols] for n in (g, g + 1) for ref in (s0_ref, s1_ref)]
            halves.append(jnp.concatenate(pieces, axis=1))
        mixed = jnp.dot(jnp.concatenate(halves, axis=0), order, preferred_element_type=F32)
        upper = lanes() >= WIDE // 2
        for e in range(4):
            first = mixed[:DATA_ROWS, e * WIDE : (e + 1) * WIDE]
            second = mixed[DATA_ROWS:, e * WIDE : (e + 1) * WIDE]
            low = jnp.where(upper, pltpu.roll(second, WIDE // 2, 1), first)
            high = jnp.where(upper, second, pltpu.roll(first, WIDE // 2, 1))
            for d, value in ((c * 8 + e, low), (c * 8 + e + 4, high)):
                out_ref[d, :DATA_ROWS, :] = value.astype(BF16)
                out_ref[d, DATA_ROWS:, :] = lists


def whiten_kernel(slab_ref, out_ref, swapped_ref, last_ref):
    order = order_table()
    both = fold_table(1.0, 1.0)
    both = jnp.concatenate([both, both], axis=0)
    swap = swap_table()
    batch = 4
    for first in range(0, PLANE, batch):
        rows = []
        for p in range(first, first + batch):
            rows.append(jnp.concatenate([slab_ref[p * LAGS + n, :DATA_ROWS, :] for n in range(LAGS)], axis=1))
        values = jnp.dot(jnp.concatenate(rows, axis=0), order, preferred_element_type=F32)
        values = jnp.concatenate([values[:, g * WIDE : (g + 1) * WIDE] for g in range(4)], axis=0)
        high, low = halves_of(values * values)
        power = jnp.dot(jnp.concatenate([high, low], axis=1), both, preferred_element_type=F32)
        whitened = (values * lax.rsqrt(power * (1.0 / WINDOWS) + WATER)).astype(BF16)
        turned = jnp.dot(whitened, swap, preferred_element_type=F32).astype(BF16)
        for n in range(batch):
            for g in range(4):
                at = (g * batch + n) * 32
                out_ref[first + n, g * 32 : (g + 1) * 32, :] = whitened[at : at + 32]
                swapped_ref[first + n, g * 32 : (g + 1) * 32, :] = turned[at : at + 32]
                if first == PLANE - ROUNDS:
                    last_ref[n, g * 32 : (g + 1) * 32, :] = whitened[at : at + 32]


def chosen_kernel(slab_ref, out_ref, owner_ref):
    row = lax.broadcasted_iota(jnp.int32, (CB, PCAP), 0).astype(F32)

    def one(p, carry):
        value = jnp.concatenate([slab_ref[p * LAGS + n, DATA_ROWS:, :] for n in range(LAGS)], axis=1).astype(F32)
        owner_ref[pl.ds(p, 1), :] = value[MEETINGS : MEETINGS + 1, :WIDE].astype(jnp.int32)
        odd = jnp.where(value < 0.0, 1.0, 0.0)
        size = jnp.abs(value)
        live = size > 0.0
        exponent = jnp.zeros(value.shape, F32)
        for bit in (5, 4, 3, 2, 1, 0):
            large = size >= 2.0 ** (1 << bit)
            size = jnp.where(large, size * 2.0 ** -(1 << bit), size)
            exponent = jnp.where(large, exponent + 2.0**bit, exponent)
        first = jnp.where(live, 2.0 * exponent + odd, -1.0)
        second = (size - 1.0) * CB
        for o in range(MEETINGS):
            pick_first = jnp.where(row == first[o : o + 1], 1.0, 0.0).astype(BF16)
            pick_second = jnp.where(row == second[o : o + 1], 1.0, 0.0).astype(BF16)
            chosen = lax.dot_general(pick_first, pick_second, (((1,), (1,)), ((), ())), preferred_element_type=F32)
            out_ref[p, o] = chosen.astype(BF16)
        return carry

    lax.fori_loop(0, PLANE, one, 0, unroll=16)


def fill_bins(bins_ref):
    spread = lax.broadcasted_iota(jnp.int32, (CB, CB), 1) - lax.broadcasted_iota(jnp.int32, (CB, CB), 0)
    at = 0
    for o, k, lo, hi in SPANS:
        distance = spread[lo:hi] + CB * o
        inside = (distance >= BINW * k) & (distance < BINW * (k + 1))
        bins_ref[at : at + hi - lo, :] = jnp.where(inside, 1.0, 0.0).astype(BF16)
        at += hi - lo


def meet(out_ref, owner_ref, bins_ref, chosen_ref, at_block, block, partners, p):
    row_id = lax.broadcasted_iota(jnp.int32, (NBIN, WIDE), 0)
    at = 0
    pieces = []
    for o, _, lo, hi in SPANS:
        pieces.append(chosen_ref[at_block, o, lo:hi, :] * bins_ref[at : at + hi - lo, :])
        at += hi - lo
    mixed = jnp.dot(jnp.concatenate(pieces, axis=0), block, preferred_element_type=F32)
    at = 0
    real, imag = [], []
    for o in range(MEETINGS):
        straight = partners[o][0].astype(F32)
        swapped = partners[o][1].astype(F32)
        for k, lo, hi in LEVELS[o]:
            part = mixed[at : at + hi - lo]
            at += hi - lo
            dims = ((hi - lo) // 8, 8, WIDE)
            real.append(jnp.sum((straight[lo:hi] * part).reshape(dims), axis=0))
            imag.append(jnp.sum((swapped[lo:hi] * part).reshape(dims), axis=0))
    at = 0
    for o in range(MEETINGS):
        re = jnp.zeros((NBIN, WIDE), F32)
        im = jnp.zeros((NBIN, WIDE), F32)
        for k, _, _ in LEVELS[o]:
            re = jnp.where(row_id == k, jnp.sum(real[at], axis=0, keepdims=True), re)
            im = jnp.where(row_id == k, jnp.sum(imag[at], axis=0, keepdims=True), im)
            at += 1
        found = jnp.where(real_lanes(), fold(re), fold(im))
        spot = owner_ref[p, o]
        out_ref[spot] = out_ref[spot] + found


def meetings_kernel(
    owner_ref, chosen_ref, group_ref, swapped_ref, below_ref, out_ref, bins_ref, all_ref, turned_ref, total_ref
):
    total_ref[...] = jnp.zeros(total_ref.shape, F32)
    fill_bins(bins_ref)
    swap = swap_table()
    for n in range(ROUNDS):
        all_ref[n] = below_ref[n]
        turned_ref[n] = jnp.dot(below_ref[n], swap, preferred_element_type=F32).astype(BF16)
    all_ref[ROUNDS:] = group_ref[...]
    turned_ref[ROUNDS:] = swapped_ref[...]

    def one(p, carry):
        partners = [(all_ref[p + ROUNDS - o], turned_ref[p + ROUNDS - o]) for o in range(MEETINGS)]
        meet(total_ref, owner_ref, bins_ref, chosen_ref, p, group_ref[p], partners, p)
        return carry

    lax.fori_loop(0, PLANE, one, 0, unroll=16)
    row_id = lax.broadcasted_iota(jnp.int32, (NBIN, WIDE), 0)
    own_piece = (lanes() >> 4) == row_id
    for n in range(0, ROWS * PLANE, 2):
        pair = []
        for owner in (n, n + 1):
            value = jnp.where(own_piece, total_ref[owner], 0.0)
            pair.append(jnp.sum(value, axis=0, keepdims=True))
        out_ref[n * LAGS : (n + 2) * LAGS, :] = jnp.where(row_id < LAGS, pair[0], pair[1])


def lag_kernel(lag_ref, parts_ref, table_ref, out_ref, order_ref):
    lane = lanes()
    sign = jnp.where(real_lanes(), -1.0, 1.0)
    step = (lane * (lag_ref[0] + 2)) & 3
    along = jnp.where(step == 0, 1.0, 0.0) - jnp.where(step == 2, 1.0, 0.0)
    across = sign * (jnp.where(step == 1, 1.0, 0.0) - jnp.where(step == 3, 1.0, 0.0))
    pieces = []
    for n in range(8):
        value = parts_ref[pl.ds(n, 8, stride=8), :]
        for y in range(1, ROWS):
            value = value + parts_ref[pl.ds(y * PLANE * LAGS + n, 8, stride=8), :]
        pieces.append(value)
    for k, value in enumerate(transpose_pieces(pieces, 2 * BAND)):
        swapped = jnp.where(real_lanes(), pltpu.roll(value, WIDE - BAND, 1), pltpu.roll(value, BAND, 1))
        order_ref[pl.ds(k, 8, stride=8), :] = value * along + swapped * across
    columns = [order_ref[n * NBIN : (n + 1) * NBIN, :] for n in range(8)]
    out_ref[0] = split_dot(jnp.concatenate(columns, axis=1), table_ref[...])


def later_kernel(traces_ref, taps_ref, table_ref, out_ref, x_ref, h_ref, d_ref, sems):
    copies = [
        pltpu.make_async_copy(traces_ref.at[:, WIN - TAPS :], x_ref, sems.at[0]),
        pltpu.make_async_copy(taps_ref, h_ref, sems.at[1]),
        pltpu.make_async_copy(table_ref, d_ref, sems.at[2]),
    ]
    for copy in copies:
        copy.start()
    copies[0].wait()
    copies[1].wait()
    spectra_kernel(x_ref.at[:, :TAPS], x_ref.at[:, TAPS:], h_ref, d_ref, out_ref, copies[2].wait)


def later_window(traces, taps, table):
    return pl.pallas_call(
        later_kernel,
        out_shape=shape((CB, WIN), BF16),
        in_specs=[pl.BlockSpec(memory_space=pltpu.HBM)] * 3,
        out_specs=pl.BlockSpec(memory_space=pltpu.VMEM),
        scratch_shapes=[
            pltpu.VMEM((CB, WIN + TAPS), F32),
            pltpu.VMEM((2 * TAPS, 2 * TAPS), BF16),
            pltpu.VMEM((HALF, WIN), BF16),
            pltpu.SemaphoreType.DMA((3,)),
        ],
        compiler_params=pltpu.CompilerParams(vmem_limit_bytes=VMEM_LIMIT),
    )(*[pltpu.with_memory_space_constraint(value, pltpu.HBM) for value in (traces, taps, table)])


def first_window(history, traces, taps, table):
    return pl.pallas_call(
        spectra_kernel,
        out_shape=shape((CB, WIN), BF16),
        grid=(1,),
        in_specs=[
            pl.BlockSpec((CB, TAPS), lambda n: (0, 0)),
            pl.BlockSpec((CB, WIN), lambda n: (0, 0)),
            pl.BlockSpec((2 * TAPS, 2 * TAPS), lambda n: (0, 0)),
            pl.BlockSpec((HALF, WIN), lambda n: (0, 0)),
        ],
        out_specs=pl.BlockSpec((CB, WIN), lambda n: (0, 0)),
        compiler_params=pltpu.CompilerParams(vmem_limit_bytes=VMEM_LIMIT),
    )(history, traces, taps, table)


def row_below(blocks):
    return lax.ppermute(blocks, "row", [(i, i + 1) for i in range(ROWS - 1)])


def middle(slabs, send):
    blocks = (PLANE, CB, WIDE)
    group, swapped, last = call(
        whiten_kernel, (shape(blocks, BF16), shape(blocks, BF16), shape((ROUNDS, CB, WIDE), BF16)), slabs
    )
    below = send(last)
    chosen, owners = call(
        chosen_kernel, (shape((PLANE, MEETINGS, CB, CB), BF16), shape((PLANE, WIDE), jnp.int32)), slabs
    )
    sums_shape = (ROWS * PLANE, NBIN, WIDE)
    more = pltpu.VMEM((PLANE + ROUNDS, CB, WIDE), BF16)
    return call(
        meetings_kernel,
        shape((ROWS * PLANE * LAGS, WIDE), F32),
        owners,
        chosen,
        group,
        swapped,
        below,
        smem=(0,),
        scratch=(pltpu.VMEM((SPAN_ROWS, CB), BF16), more, more, pltpu.VMEM(sums_shape, F32)),
    )


def body(traces, owner_map, pair_codes, pair_count):
    blk = (lax.axis_index("row") * PLANE + lax.axis_index("plane")).astype(jnp.int32)
    lag = lax.axis_index("lag").astype(jnp.int32)
    taps = jnp.asarray(filter_table())
    table = jnp.asarray(transform_table())

    history = lax.ppermute(traces[:, -TAPS:], "lag", [(i, i + 1) for i in range(3)])

    spectra1 = later_window(traces, taps, table)
    spectra0 = first_window(history, traces, taps, table)
    slabs = call(
        pack_kernel,
        shape((PLANE * LAGS, SLAB_ROWS, WIDE), BF16),
        jnp.stack([blk, lag]),
        pair_count.reshape(1, MEETINGS),
        owner_map.reshape(1, MEETINGS),
        pair_codes,
        spectra0,
        spectra1,
        smem=(0,),
    )
    slabs = lax.all_to_all(slabs, ("plane", "lag"), 0, 0, tiled=True)
    sums = middle(slabs, row_below)
    parts = lax.all_to_all(sums, ("row", "plane", "lag"), 0, 0, tiled=True)
    return call(
        lag_kernel,
        shape((1, NBIN, LANES), F32),
        lag.reshape(1),
        parts,
        jnp.asarray(inverse_table()),
        smem=(0,),
        scratch=(pltpu.VMEM((8 * NBIN, WIDE), F32),),
    )


def solution(mesh):
    split = Mesh(mesh.devices.reshape(ROWS, PLANE, 4), ("row", "plane", "lag"))
    owned = ("row", "plane")
    return jax.shard_map(
        body,
        mesh=split,
        in_specs=(P(owned, "lag"), P(None, owned), P(None, owned), P(None, owned)),
        out_specs=P(owned, None, "lag"),
        check_vma=False,
    )
```

```python
import math

import jax
import jax.numpy as jnp
import numpy as np
from jax import lax
from jax.experimental import pallas as pl
from jax.experimental.pallas import tpu as pltpu
from jax.sharding import Mesh
from jax.sharding import PartitionSpec as P

CB = 128
WIN = 1024
HALF = 512
NF = 512
TAPS = 128
NBIN = 8
BINW = 80
ROUNDS = 4
MEETINGS = 5
PCAP = 512
WINDOWS = 8
LANES = 256
PLANE = 16
ROWS = 4
LAGS = 4
WIDE = 128
BAND = 8
DATA_ROWS = 32
SLAB_ROWS = 40

BAND_LOW = 0.02
BAND_HIGH = 0.48
WATER = 0.1

F32 = jnp.float32
BF16 = jnp.bfloat16
VMEM_LIMIT = 16 * 1024 * 1024


def level_rows(o):
    found = []
    for k in range(NBIN):
        pairs = [
            i
            for i in range(CB)
            for j in range(CB)
            if (o > 0 or i < j) and (CB * o + j - i) // BINW == k
        ]
        if pairs:
            found.append((k, min(pairs) // 16 * 16, max(pairs) // 16 * 16 + 16))
    return tuple(found)


LEVELS = tuple(level_rows(o) for o in range(MEETINGS))
SPANS = tuple((o, k, lo, hi) for o in range(MEETINGS) for k, lo, hi in LEVELS[o])
SPAN_ROWS = sum(hi - lo for _, _, lo, hi in SPANS)


def two_terms(table):
    high = table.astype(jnp.bfloat16)
    low = (table - high.astype(np.float32)).astype(jnp.bfloat16)
    return np.concatenate([high, low], axis=1)


def filter_table():
    k = np.arange(TAPS, dtype=np.float64)
    m = k - (TAPS - 1) / 2.0
    ideal = 2 * BAND_HIGH * np.sinc(2 * BAND_HIGH * m) - 2 * BAND_LOW * np.sinc(2 * BAND_LOW * m)
    taps = ideal * (0.5 - 0.5 * np.cos(2 * np.pi * (k + 0.5) / TAPS))
    lagged = np.arange(TAPS)[None, :] - np.arange(2 * TAPS)[:, None] + TAPS
    inside = (lagged >= 0) & (lagged < TAPS)
    return two_terms(np.where(inside, taps[np.clip(lagged, 0, TAPS - 1)], 0.0).astype(np.float32))


def column_order():
    column = np.arange(WIN)
    return column // (2 * BAND) * BAND + column % BAND, column // BAND % 2 == 1


def transform_table():
    freq, is_imag = column_order()
    angle = (np.arange(HALF)[:, None] * freq[None, :] % WIN) * (2 * np.pi / WIN)
    return (np.where(is_imag[None, :], -np.sin(angle), np.cos(angle)) / math.sqrt(WIN)).astype(jnp.bfloat16)


def inverse_table():
    freq, is_imag = column_order()
    angle = (freq[:, None] * np.arange(LANES)[None, :] % WIN) * (2 * np.pi / WIN)
    weight = np.where(freq == 0, 1.0, 2.0)[:, None] / (WINDOWS * math.sqrt(WIN))
    return two_terms((weight * np.where(is_imag[:, None], -np.sin(angle), np.cos(angle))).astype(np.float32))


def call(kernel, out_shape, *args, smem=(), aliases=None, scratch=()):
    specs = [
        pl.BlockSpec(memory_space=pltpu.SMEM) if n in smem else pl.BlockSpec(memory_space=pltpu.VMEM)
        for n in range(len(args))
    ]
    many = isinstance(out_shape, (tuple, list))
    out_specs = [pl.BlockSpec(memory_space=pltpu.VMEM)] * len(out_shape) if many else pl.BlockSpec(memory_space=pltpu.VMEM)
    return pl.pallas_call(
        kernel,
        out_shape=out_shape,
        in_specs=specs,
        out_specs=out_specs,
        input_output_aliases=aliases or {},
        scratch_shapes=list(scratch),
        compiler_params=pltpu.CompilerParams(vmem_limit_bytes=VMEM_LIMIT),
    )(*args)


def shape(dims, dtype):
    return jax.ShapeDtypeStruct(dims, dtype)


def lanes():
    return lax.broadcasted_iota(jnp.int32, (1, WIDE), 1)


def real_lanes():
    return (lanes() & BAND) == 0


def fold(values):
    for step in (BAND, 2 * BAND, 4 * BAND, 8 * BAND):
        values = values + pltpu.roll(values, step, 1)
    return values


def fold_table(real, imag):
    row = lax.broadcasted_iota(jnp.int32, (WIDE, WIDE), 0)
    column = lax.broadcasted_iota(jnp.int32, (WIDE, WIDE), 1)
    same = ((row ^ column) & (BAND - 1)) == 0
    asked = jnp.where((column & BAND) == 0, real, imag)
    return jnp.where(same, asked, 0.0).astype(BF16)


def swap_table():
    row = lax.broadcasted_iota(jnp.int32, (WIDE, WIDE), 0)
    column = lax.broadcasted_iota(jnp.int32, (WIDE, WIDE), 1)
    value = jnp.where((column & BAND) == 0, -1.0, 1.0)
    return jnp.where(row == (column ^ BAND), value, 0.0).astype(BF16)


def order_table():
    row = lax.broadcasted_iota(jnp.int32, (4 * WIDE, 1), 0)
    goal = ((row >> 5) & 3) * WIDE + (row >> 7) * 32 + (row & 31)
    column = lax.broadcasted_iota(jnp.int32, (4 * WIDE, 4 * WIDE), 1)
    return jnp.where(column == goal, 1.0, 0.0).astype(BF16)


def halves_of(values):
    high = values.astype(BF16)
    return high, (values - high.astype(F32)).astype(BF16)


def split_dot(values, table):
    high, low = halves_of(values)
    count, width = values.shape[0], table.shape[1] // 2
    out = jnp.dot(jnp.concatenate([high, low], axis=0), table, preferred_element_type=F32)
    small = out[count:, width:] + (out[count:, :width] + out[:count, width:])
    return small + out[:count, :width]


def transpose_pieces(arrays, width):
    bit = 1
    while bit < len(arrays):
        upper = (lanes() & (bit * width)) != 0
        out = list(arrays)
        for q in range(len(arrays)):
            if q & bit:
                continue
            a, b = arrays[q], arrays[q | bit]
            out[q] = jnp.where(upper, pltpu.roll(b, bit * width, 1), a)
            out[q | bit] = jnp.where(upper, b, pltpu.roll(a, WIDE - bit * width, 1))
        arrays = out
        bit *= 2
    return arrays


def turns():
    column = lax.broadcasted_iota(jnp.int32, (1, WIN), 1)
    return jnp.where(column % 2 == 0, 1.0, -1.0).astype(F32)


def early_kernel(
    place_ref, traces_ref, taps_ref, table_ref, counts_in, owners_in, codes_in,
    s1_ref, part_ref, head_ref, taps_out, table_out, lists_ref,
    x_ref, h_ref, d_ref, count_ref, owner_ref, codes_ref, sems,
):
    late = WIN - TAPS
    copies = [
        pltpu.make_async_copy(traces_ref.at[:, late:], x_ref.at[:, late:], sems.at[0]),
        pltpu.make_async_copy(taps_ref, h_ref, sems.at[1]),
        pltpu.make_async_copy(table_ref, d_ref, sems.at[2]),
        pltpu.make_async_copy(traces_ref.at[:, :late], x_ref.at[:, :late], sems.at[3]),
        pltpu.make_async_copy(counts_in, count_ref, sems.at[4]),
        pltpu.make_async_copy(owners_in, owner_ref, sems.at[5]),
        pltpu.make_async_copy(codes_in, codes_ref, sems.at[6]),
    ]
    for copy in copies:
        copy.start()

    def filtered(first, last):
        pairs = [x_ref[:, (t - 1) * TAPS : (t + 1) * TAPS] for t in range(first, last)]
        rows = split_dot(jnp.concatenate(pairs, axis=0), h_ref[...]).astype(BF16)
        return [rows[n * CB : (n + 1) * CB] for n in range(last - first)]

    copies[0].wait()
    copies[1].wait()
    tiles = filtered(8, 16)
    copies[2].wait()
    first = jnp.dot(jnp.concatenate(tiles[:4], axis=1), d_ref[...], preferred_element_type=F32)
    second = jnp.dot(jnp.concatenate(tiles[4:], axis=1), d_ref[...], preferred_element_type=F32)
    s1_ref[...] = (first + turns() * second).astype(BF16)
    copies[3].wait()
    tiles = filtered(1, 8)
    first = jnp.dot(jnp.concatenate(tiles[:3], axis=1), d_ref[TAPS:, :], preferred_element_type=F32)
    second = jnp.dot(jnp.concatenate(tiles[3:], axis=1), d_ref[...], preferred_element_type=F32)
    part_ref[...] = first + turns() * second
    head_ref[...] = x_ref[:, :TAPS]
    taps_out[...] = h_ref[...]
    table_out[...] = d_ref[:TAPS, :]
    for copy in copies[4:]:
        copy.wait()
    lists_ref[...] = list_rows(place_ref, count_ref, owner_ref, codes_ref)


def pack_table():
    row = lax.broadcasted_iota(jnp.int32, (4 * WIDE, 1), 0)
    goal = ((row >> 4) & 3) * WIDE + ((row >> 6) & 1) * (WIDE // 2) + (row >> 7) * 16 + (row & 15)
    column = lax.broadcasted_iota(jnp.int32, (4 * WIDE, 4 * WIDE), 1)
    return jnp.where(column == goal, 1.0, 0.0).astype(BF16)


def list_rows(place_ref, count_ref, owner_ref, codes_ref):
    lane = lanes()
    start = pl.multiple_of(place_ref[1] * WIDE, WIDE)
    codes = codes_ref[:, pl.ds(start, WIDE)]
    exponent = codes >> 8
    value = 1.0 + (codes & (CB - 1)).astype(F32) * (1.0 / CB)
    for bit in range(6):
        value = jnp.where(((exponent >> bit) & 1) == 1, value * 2.0 ** (1 << bit), value)
    value = jnp.where(((codes >> 7) & 1) == 1, -value, value)
    rows = []
    owners = jnp.zeros((1, WIDE), F32)
    for o in range(MEETINGS):
        live = jnp.where(place_ref[0] >= o, count_ref[:, o : o + 1], 0)
        rows.append(jnp.where(lane + start < live, value[o : o + 1], 0.0))
        owner = owner_ref[:, o : o + 1]
        owners = jnp.where(lane == o, owner.astype(F32), owners)
    rows = rows + [owners] + [jnp.zeros((1, WIDE), F32)] * (SLAB_ROWS - DATA_ROWS - MEETINGS - 1)
    return jnp.concatenate(rows, axis=0).astype(BF16)


def pack_kernel(
    lists_ref, hist_ref, head_ref, taps_ref, table_ref, part_ref, s1_ref, out_ref
):
    rows = split_dot(jnp.concatenate([hist_ref[...], head_ref[...]], axis=1), taps_ref[...]).astype(BF16)
    s0 = (part_ref[...] + jnp.dot(rows, table_ref[...], preferred_element_type=F32)).astype(BF16)
    s1 = s1_ref[...]
    lists = lists_ref[...]
    order = pack_table()
    for c in range(WIN // WIDE):
        cols = slice(c * WIDE, (c + 1) * WIDE)
        halves = []
        for g in range(0, 4, 2):
            pieces = [value[n * 32 : (n + 1) * 32, cols] for n in (g, g + 1) for value in (s0, s1)]
            halves.append(jnp.concatenate(pieces, axis=1))
        mixed = jnp.dot(jnp.concatenate(halves, axis=0), order, preferred_element_type=F32)
        upper = lanes() >= WIDE // 2
        for e in range(4):
            first = mixed[:DATA_ROWS, e * WIDE : (e + 1) * WIDE]
            second = mixed[DATA_ROWS:, e * WIDE : (e + 1) * WIDE]
            low = jnp.where(upper, pltpu.roll(second, WIDE // 2, 1), first)
            high = jnp.where(upper, second, pltpu.roll(first, WIDE // 2, 1))
            for d, value in ((c * 8 + e, low), (c * 8 + e + 4, high)):
                out_ref[d, :DATA_ROWS, :] = value.astype(BF16)
                out_ref[d, DATA_ROWS:, :] = lists


def whiten_kernel(slab_ref, out_ref, swapped_ref, last_ref):
    order = order_table()
    both = fold_table(1.0, 1.0)
    both = jnp.concatenate([both, both], axis=0)
    swap = swap_table()
    batch = 4
    for first in range(0, PLANE, batch):
        rows = []
        for p in range(first, first + batch):
            rows.append(jnp.concatenate([slab_ref[p * LAGS + n, :DATA_ROWS, :] for n in range(LAGS)], axis=1))
        values = jnp.dot(jnp.concatenate(rows, axis=0), order, preferred_element_type=F32)
        values = jnp.concatenate([values[:, g * WIDE : (g + 1) * WIDE] for g in range(4)], axis=0)
        high, low = halves_of(values * values)
        power = jnp.dot(jnp.concatenate([high, low], axis=1), both, preferred_element_type=F32)
        whitened = (values * lax.rsqrt(power * (1.0 / WINDOWS) + WATER)).astype(BF16)
        turned = jnp.dot(whitened, swap, preferred_element_type=F32).astype(BF16)
        for n in range(batch):
            for g in range(4):
                at = (g * batch + n) * 32
                out_ref[first + n, g * 32 : (g + 1) * 32, :] = whitened[at : at + 32]
                swapped_ref[first + n, g * 32 : (g + 1) * 32, :] = turned[at : at + 32]
                if first == PLANE - ROUNDS:
                    last_ref[n, g * 32 : (g + 1) * 32, :] = whitened[at : at + 32]


def chosen_kernel(slab_ref, out_ref, owner_ref):
    row = lax.broadcasted_iota(jnp.int32, (CB, PCAP), 0).astype(F32)

    def one(p, carry):
        value = jnp.concatenate([slab_ref[p * LAGS + n, DATA_ROWS:, :] for n in range(LAGS)], axis=1).astype(F32)
        owner_ref[pl.ds(p, 1), :] = value[MEETINGS : MEETINGS + 1, :WIDE].astype(jnp.int32)
        odd = jnp.where(value < 0.0, 1.0, 0.0)
        size = jnp.abs(value)
        live = size > 0.0
        exponent = jnp.zeros(value.shape, F32)
        for bit in (5, 4, 3, 2, 1, 0):
            large = size >= 2.0 ** (1 << bit)
            size = jnp.where(large, size * 2.0 ** -(1 << bit), size)
            exponent = jnp.where(large, exponent + 2.0**bit, exponent)
        first = jnp.where(live, 2.0 * exponent + odd, -1.0)
        second = (size - 1.0) * CB
        for o in range(MEETINGS):
            pick_first = jnp.where(row == first[o : o + 1], 1.0, 0.0).astype(BF16)
            pick_second = jnp.where(row == second[o : o + 1], 1.0, 0.0).astype(BF16)
            chosen = lax.dot_general(pick_first, pick_second, (((1,), (1,)), ((), ())), preferred_element_type=F32)
            out_ref[p, o] = chosen.astype(BF16)
        return carry

    lax.fori_loop(0, PLANE, one, 0, unroll=16)


def fill_bins(bins_ref):
    spread = lax.broadcasted_iota(jnp.int32, (CB, CB), 1) - lax.broadcasted_iota(jnp.int32, (CB, CB), 0)
    at = 0
    for o, k, lo, hi in SPANS:
        distance = spread[lo:hi] + CB * o
        inside = (distance >= BINW * k) & (distance < BINW * (k + 1))
        bins_ref[at : at + hi - lo, :] = jnp.where(inside, 1.0, 0.0).astype(BF16)
        at += hi - lo


def meet(out_ref, owner_ref, bins_ref, chosen_ref, at_block, block, partners, p):
    row_id = lax.broadcasted_iota(jnp.int32, (NBIN, WIDE), 0)
    at = 0
    pieces = []
    for o, _, lo, hi in SPANS:
        pieces.append(chosen_ref[at_block, o, lo:hi, :] * bins_ref[at : at + hi - lo, :])
        at += hi - lo
    mixed = jnp.dot(jnp.concatenate(pieces, axis=0), block, preferred_element_type=F32)
    at = 0
    real, imag = [], []
    for o in range(MEETINGS):
        straight = partners[o][0].astype(F32)
        swapped = partners[o][1].astype(F32)
        for k, lo, hi in LEVELS[o]:
            part = mixed[at : at + hi - lo]
            at += hi - lo
            dims = ((hi - lo) // 8, 8, WIDE)
            real.append(jnp.sum((straight[lo:hi] * part).reshape(dims), axis=0))
            imag.append(jnp.sum((swapped[lo:hi] * part).reshape(dims), axis=0))
    at = 0
    for o in range(MEETINGS):
        re = jnp.zeros((NBIN, WIDE), F32)
        im = jnp.zeros((NBIN, WIDE), F32)
        for k, _, _ in LEVELS[o]:
            re = jnp.where(row_id == k, jnp.sum(real[at], axis=0, keepdims=True), re)
            im = jnp.where(row_id == k, jnp.sum(imag[at], axis=0, keepdims=True), im)
            at += 1
        found = jnp.where(real_lanes(), fold(re), fold(im))
        spot = owner_ref[p, o]
        out_ref[spot] = out_ref[spot] + found


def meetings_kernel(
    owner_ref, chosen_ref, group_ref, swapped_ref, below_ref, out_ref, bins_ref, all_ref, turned_ref, total_ref
):
    total_ref[...] = jnp.zeros(total_ref.shape, F32)
    fill_bins(bins_ref)
    swap = swap_table()
    for n in range(ROUNDS):
        all_ref[n] = below_ref[n]
        turned_ref[n] = jnp.dot(below_ref[n], swap, preferred_element_type=F32).astype(BF16)
    all_ref[ROUNDS:] = group_ref[...]
    turned_ref[ROUNDS:] = swapped_ref[...]

    def one(p, carry):
        partners = [(all_ref[p + ROUNDS - o], turned_ref[p + ROUNDS - o]) for o in range(MEETINGS)]
        meet(total_ref, owner_ref, bins_ref, chosen_ref, p, group_ref[p], partners, p)
        return carry

    lax.fori_loop(0, PLANE, one, 0, unroll=16)
    row_id = lax.broadcasted_iota(jnp.int32, (NBIN, WIDE), 0)
    own_piece = (lanes() >> 4) == row_id
    for n in range(0, ROWS * PLANE, 2):
        pair = []
        for owner in (n, n + 1):
            value = jnp.where(own_piece, total_ref[owner], 0.0)
            pair.append(jnp.sum(value, axis=0, keepdims=True))
        out_ref[n * LAGS : (n + 2) * LAGS, :] = jnp.where(row_id < LAGS, pair[0], pair[1])


def lag_kernel(lag_ref, parts_ref, table_ref, out_ref, order_ref):
    lane = lanes()
    sign = jnp.where(real_lanes(), -1.0, 1.0)
    step = (lane * (lag_ref[0] + 2)) & 3
    along = jnp.where(step == 0, 1.0, 0.0) - jnp.where(step == 2, 1.0, 0.0)
    across = sign * (jnp.where(step == 1, 1.0, 0.0) - jnp.where(step == 3, 1.0, 0.0))
    pieces = []
    for n in range(8):
        value = parts_ref[pl.ds(n, 8, stride=8), :]
        for y in range(1, ROWS):
            value = value + parts_ref[pl.ds(y * PLANE * LAGS + n, 8, stride=8), :]
        pieces.append(value)
    for k, value in enumerate(transpose_pieces(pieces, 2 * BAND)):
        swapped = jnp.where(real_lanes(), pltpu.roll(value, WIDE - BAND, 1), pltpu.roll(value, BAND, 1))
        order_ref[pl.ds(k, 8, stride=8), :] = value * along + swapped * across
    columns = [order_ref[n * NBIN : (n + 1) * NBIN, :] for n in range(8)]
    out_ref[0] = split_dot(jnp.concatenate(columns, axis=1), table_ref[...])


def early_part(place, *inputs):
    operands = [pltpu.with_memory_space_constraint(value, pltpu.HBM) for value in inputs]
    return pl.pallas_call(
        early_kernel,
        out_shape=(
            shape((CB, WIN), BF16),
            shape((CB, WIN), F32),
            shape((CB, TAPS), F32),
            shape((2 * TAPS, 2 * TAPS), BF16),
            shape((TAPS, WIN), BF16),
            shape((SLAB_ROWS - DATA_ROWS, WIDE), BF16),
        ),
        in_specs=[pl.BlockSpec(memory_space=pltpu.SMEM)] + [pl.BlockSpec(memory_space=pltpu.HBM)] * 6,
        out_specs=[pl.BlockSpec(memory_space=pltpu.VMEM)] * 6,
        scratch_shapes=[
            pltpu.VMEM((CB, 2 * WIN), F32),
            pltpu.VMEM((2 * TAPS, 2 * TAPS), BF16),
            pltpu.VMEM((HALF, WIN), BF16),
            pltpu.VMEM((1, MEETINGS), jnp.int32),
            pltpu.VMEM((1, MEETINGS), jnp.int32),
            pltpu.VMEM((MEETINGS, PCAP), jnp.int32),
            pltpu.SemaphoreType.DMA((7,)),
        ],
        compiler_params=pltpu.CompilerParams(vmem_limit_bytes=VMEM_LIMIT),
    )(place, *operands)


def row_below(blocks):
    return lax.ppermute(blocks, "row", [(i, i + 1) for i in range(ROWS - 1)])


def middle(slabs, send):
    blocks = (PLANE, CB, WIDE)
    group, swapped, last = call(
        whiten_kernel, (shape(blocks, BF16), shape(blocks, BF16), shape((ROUNDS, CB, WIDE), BF16)), slabs
    )
    below = send(last)
    chosen, owners = call(
        chosen_kernel, (shape((PLANE, MEETINGS, CB, CB), BF16), shape((PLANE, WIDE), jnp.int32)), slabs
    )
    sums_shape = (ROWS * PLANE, NBIN, WIDE)
    more = pltpu.VMEM((PLANE + ROUNDS, CB, WIDE), BF16)
    return call(
        meetings_kernel,
        shape((ROWS * PLANE * LAGS, WIDE), F32),
        owners,
        chosen,
        group,
        swapped,
        below,
        smem=(0,),
        scratch=(pltpu.VMEM((SPAN_ROWS, CB), BF16), more, more, pltpu.VMEM(sums_shape, F32)),
    )


def body(traces, owner_map, pair_codes, pair_count):
    blk = (lax.axis_index("row") * PLANE + lax.axis_index("plane")).astype(jnp.int32)
    lag = lax.axis_index("lag").astype(jnp.int32)
    taps = jnp.asarray(filter_table())
    table = jnp.asarray(transform_table())

    history = lax.ppermute(traces[:, -TAPS:], "lag", [(i, i + 1) for i in range(3)])

    spectra1, part, head, taps, table, lists = early_part(
        jnp.stack([blk, lag]),
        traces,
        taps,
        table,
        pair_count.reshape(1, MEETINGS),
        owner_map.reshape(1, MEETINGS),
        pair_codes,
    )
    slabs = call(
        pack_kernel,
        shape((PLANE * LAGS, SLAB_ROWS, WIDE), BF16),
        lists,
        history,
        head,
        taps,
        table,
        part,
        spectra1,
    )
    slabs = lax.all_to_all(slabs, ("plane", "lag"), 0, 0, tiled=True)
    sums = middle(slabs, row_below)
    parts = lax.all_to_all(sums, ("row", "plane", "lag"), 0, 0, tiled=True)
    return call(
        lag_kernel,
        shape((1, NBIN, LANES), F32),
        lag.reshape(1),
        parts,
        jnp.asarray(inverse_table()),
        smem=(0,),
        scratch=(pltpu.VMEM((8 * NBIN, WIDE), F32),),
    )


def solution(mesh):
    split = Mesh(mesh.devices.reshape(ROWS, PLANE, 4), ("row", "plane", "lag"))
    owned = ("row", "plane")
    return jax.shard_map(
        body,
        mesh=split,
        in_specs=(P(owned, "lag"), P(None, owned), P(None, owned), P(None, owned)),
        out_specs=P(owned, None, "lag"),
        check_vma=False,
    )
```

```python
import math

import jax
import jax.numpy as jnp
import numpy as np
from jax import lax
from jax.experimental import pallas as pl
from jax.experimental.pallas import tpu as pltpu
from jax.sharding import Mesh
from jax.sharding import PartitionSpec as P

CB = 128
WIN = 1024
HALF = 512
NF = 512
TAPS = 128
NBIN = 8
BINW = 80
ROUNDS = 4
MEETINGS = 5
PCAP = 512
WINDOWS = 8
LANES = 256
PLANE = 16
ROWS = 4
LAGS = 4
WIDE = 128
BAND = 8
DATA_ROWS = 32
SLAB_ROWS = 40

BAND_LOW = 0.02
BAND_HIGH = 0.48
WATER = 0.1

F32 = jnp.float32
BF16 = jnp.bfloat16
VMEM_LIMIT = 16 * 1024 * 1024


def level_rows(o):
    found = []
    for k in range(NBIN):
        pairs = [
            i
            for i in range(CB)
            for j in range(CB)
            if (o > 0 or i < j) and (CB * o + j - i) // BINW == k
        ]
        if pairs:
            found.append((k, min(pairs) // 16 * 16, max(pairs) // 16 * 16 + 16))
    return tuple(found)


LEVELS = tuple(level_rows(o) for o in range(MEETINGS))
SPANS = tuple((o, k, lo, hi) for o in range(MEETINGS) for k, lo, hi in LEVELS[o])
SPAN_ROWS = sum(hi - lo for _, _, lo, hi in SPANS)


def two_terms(table):
    high = table.astype(jnp.bfloat16)
    low = (table - high.astype(np.float32)).astype(jnp.bfloat16)
    return np.concatenate([high, low], axis=1)


def filter_table():
    k = np.arange(TAPS, dtype=np.float64)
    m = k - (TAPS - 1) / 2.0
    ideal = 2 * BAND_HIGH * np.sinc(2 * BAND_HIGH * m) - 2 * BAND_LOW * np.sinc(2 * BAND_LOW * m)
    taps = ideal * (0.5 - 0.5 * np.cos(2 * np.pi * (k + 0.5) / TAPS))
    lagged = np.arange(TAPS)[None, :] - np.arange(2 * TAPS)[:, None] + TAPS
    inside = (lagged >= 0) & (lagged < TAPS)
    return two_terms(np.where(inside, taps[np.clip(lagged, 0, TAPS - 1)], 0.0).astype(np.float32))


def column_order():
    column = np.arange(WIN)
    return column // (2 * BAND) * BAND + column % BAND, column // BAND % 2 == 1


def transform_table():
    freq, is_imag = column_order()
    angle = (np.arange(HALF)[:, None] * freq[None, :] % WIN) * (2 * np.pi / WIN)
    return (np.where(is_imag[None, :], -np.sin(angle), np.cos(angle)) / math.sqrt(WIN)).astype(jnp.bfloat16)


def inverse_table():
    freq, is_imag = column_order()
    angle = (freq[:, None] * np.arange(LANES)[None, :] % WIN) * (2 * np.pi / WIN)
    weight = np.where(freq == 0, 1.0, 2.0)[:, None] / (WINDOWS * math.sqrt(WIN))
    return two_terms((weight * np.where(is_imag[:, None], -np.sin(angle), np.cos(angle))).astype(np.float32))


def call(kernel, out_shape, *args, smem=(), aliases=None, scratch=()):
    specs = [
        pl.BlockSpec(memory_space=pltpu.SMEM) if n in smem else pl.BlockSpec(memory_space=pltpu.VMEM)
        for n in range(len(args))
    ]
    many = isinstance(out_shape, (tuple, list))
    out_specs = [pl.BlockSpec(memory_space=pltpu.VMEM)] * len(out_shape) if many else pl.BlockSpec(memory_space=pltpu.VMEM)
    return pl.pallas_call(
        kernel,
        out_shape=out_shape,
        in_specs=specs,
        out_specs=out_specs,
        input_output_aliases=aliases or {},
        scratch_shapes=list(scratch),
        compiler_params=pltpu.CompilerParams(vmem_limit_bytes=VMEM_LIMIT),
    )(*args)


def shape(dims, dtype):
    return jax.ShapeDtypeStruct(dims, dtype)


def lanes():
    return lax.broadcasted_iota(jnp.int32, (1, WIDE), 1)


def real_lanes():
    return (lanes() & BAND) == 0


def fold(values):
    for step in (BAND, 2 * BAND, 4 * BAND, 8 * BAND):
        values = values + pltpu.roll(values, step, 1)
    return values


def fold_table(real, imag):
    row = lax.broadcasted_iota(jnp.int32, (WIDE, WIDE), 0)
    column = lax.broadcasted_iota(jnp.int32, (WIDE, WIDE), 1)
    same = ((row ^ column) & (BAND - 1)) == 0
    asked = jnp.where((column & BAND) == 0, real, imag)
    return jnp.where(same, asked, 0.0).astype(BF16)


def swap_table():
    row = lax.broadcasted_iota(jnp.int32, (WIDE, WIDE), 0)
    column = lax.broadcasted_iota(jnp.int32, (WIDE, WIDE), 1)
    value = jnp.where((column & BAND) == 0, -1.0, 1.0)
    return jnp.where(row == (column ^ BAND), value, 0.0).astype(BF16)


def order_table():
    row = lax.broadcasted_iota(jnp.int32, (4 * WIDE, 1), 0)
    goal = ((row >> 5) & 3) * WIDE + (row >> 7) * 32 + (row & 31)
    column = lax.broadcasted_iota(jnp.int32, (4 * WIDE, 4 * WIDE), 1)
    return jnp.where(column == goal, 1.0, 0.0).astype(BF16)


def halves_of(values):
    high = values.astype(BF16)
    return high, (values - high.astype(F32)).astype(BF16)


def split_dot(values, table):
    high, low = halves_of(values)
    count, width = values.shape[0], table.shape[1] // 2
    out = jnp.dot(jnp.concatenate([high, low], axis=0), table, preferred_element_type=F32)
    small = out[count:, width:] + (out[count:, :width] + out[:count, width:])
    return small + out[:count, :width]


def transpose_pieces(arrays, width):
    bit = 1
    while bit < len(arrays):
        upper = (lanes() & (bit * width)) != 0
        out = list(arrays)
        for q in range(len(arrays)):
            if q & bit:
                continue
            a, b = arrays[q], arrays[q | bit]
            out[q] = jnp.where(upper, pltpu.roll(b, bit * width, 1), a)
            out[q | bit] = jnp.where(upper, b, pltpu.roll(a, WIDE - bit * width, 1))
        arrays = out
        bit *= 2
    return arrays


def turns():
    column = lax.broadcasted_iota(jnp.int32, (1, WIN), 1)
    return jnp.where(column % 2 == 0, 1.0, -1.0).astype(F32)


def early_kernel(
    place_ref, traces_ref, taps_ref, table_ref, counts_in, owners_in, codes_in,
    s1_ref, part_ref, head_ref, taps_out, table_out, lists_ref,
    x_ref, h_ref, d_ref, count_ref, owner_ref, codes_ref, sems,
):
    late = WIN - TAPS
    copies = [
        pltpu.make_async_copy(traces_ref.at[:, late:], x_ref.at[:, late:], sems.at[0]),
        pltpu.make_async_copy(taps_ref, h_ref, sems.at[1]),
        pltpu.make_async_copy(table_ref, d_ref, sems.at[2]),
        pltpu.make_async_copy(traces_ref.at[:, :late], x_ref.at[:, :late], sems.at[3]),
        pltpu.make_async_copy(counts_in, count_ref, sems.at[4]),
        pltpu.make_async_copy(owners_in, owner_ref, sems.at[5]),
        pltpu.make_async_copy(codes_in, codes_ref, sems.at[6]),
    ]
    for copy in copies:
        copy.start()

    def filtered(first, last):
        pairs = [x_ref[:, (t - 1) * TAPS : (t + 1) * TAPS] for t in range(first, last)]
        rows = split_dot(jnp.concatenate(pairs, axis=0), h_ref[...]).astype(BF16)
        return [rows[n * CB : (n + 1) * CB] for n in range(last - first)]

    copies[0].wait()
    copies[1].wait()
    tiles = filtered(8, 16)
    copies[3].wait()
    tiles = [jnp.zeros((CB, TAPS), BF16)] + filtered(1, 8) + tiles
    copies[2].wait()
    rows = [jnp.concatenate(tiles[n : n + 4], axis=1) for n in (0, 4, 8, 12)]
    first = jnp.dot(jnp.concatenate(rows[0::2], axis=0), d_ref[...], preferred_element_type=F32)
    second = jnp.dot(jnp.concatenate(rows[1::2], axis=0), d_ref[...], preferred_element_type=F32)
    both = first + turns() * second
    part_ref[...] = both[:CB]
    s1_ref[...] = both[CB:].astype(BF16)
    head_ref[...] = x_ref[:, :TAPS]
    taps_out[...] = h_ref[...]
    table_out[...] = d_ref[:TAPS, :]
    for copy in copies[4:]:
        copy.wait()
    lists_ref[...] = list_rows(place_ref, count_ref, owner_ref, codes_ref)


def pack_table():
    row = lax.broadcasted_iota(jnp.int32, (4 * WIDE, 1), 0)
    goal = ((row >> 4) & 3) * WIDE + ((row >> 6) & 1) * (WIDE // 2) + (row >> 7) * 16 + (row & 15)
    column = lax.broadcasted_iota(jnp.int32, (4 * WIDE, 4 * WIDE), 1)
    return jnp.where(column == goal, 1.0, 0.0).astype(BF16)


def list_rows(place_ref, count_ref, owner_ref, codes_ref):
    lane = lanes()
    start = pl.multiple_of(place_ref[1] * WIDE, WIDE)
    codes = codes_ref[:, pl.ds(start, WIDE)]
    exponent = codes >> 8
    value = 1.0 + (codes & (CB - 1)).astype(F32) * (1.0 / CB)
    for bit in range(6):
        value = jnp.where(((exponent >> bit) & 1) == 1, value * 2.0 ** (1 << bit), value)
    value = jnp.where(((codes >> 7) & 1) == 1, -value, value)
    rows = []
    owners = jnp.zeros((1, WIDE), F32)
    for o in range(MEETINGS):
        live = jnp.where(place_ref[0] >= o, count_ref[:, o : o + 1], 0)
        rows.append(jnp.where(lane + start < live, value[o : o + 1], 0.0))
        owner = owner_ref[:, o : o + 1]
        owners = jnp.where(lane == o, owner.astype(F32), owners)
    rows = rows + [owners] + [jnp.zeros((1, WIDE), F32)] * (SLAB_ROWS - DATA_ROWS - MEETINGS - 1)
    return jnp.concatenate(rows, axis=0).astype(BF16)


def pack_kernel(
    lists_ref, hist_ref, head_ref, taps_ref, table_ref, part_ref, s1_ref, out_ref
):
    rows = split_dot(jnp.concatenate([hist_ref[...], head_ref[...]], axis=1), taps_ref[...]).astype(BF16)
    s0 = (part_ref[...] + jnp.dot(rows, table_ref[...], preferred_element_type=F32)).astype(BF16)
    s1 = s1_ref[...]
    lists = lists_ref[...]
    order = pack_table()
    for c in range(WIN // WIDE):
        cols = slice(c * WIDE, (c + 1) * WIDE)
        halves = []
        for g in range(0, 4, 2):
            pieces = [value[n * 32 : (n + 1) * 32, cols] for n in (g, g + 1) for value in (s0, s1)]
            halves.append(jnp.concatenate(pieces, axis=1))
        mixed = jnp.dot(jnp.concatenate(halves, axis=0), order, preferred_element_type=F32)
        upper = lanes() >= WIDE // 2
        for e in range(4):
            first = mixed[:DATA_ROWS, e * WIDE : (e + 1) * WIDE]
            second = mixed[DATA_ROWS:, e * WIDE : (e + 1) * WIDE]
            low = jnp.where(upper, pltpu.roll(second, WIDE // 2, 1), first)
            high = jnp.where(upper, second, pltpu.roll(first, WIDE // 2, 1))
            for d, value in ((c * 8 + e, low), (c * 8 + e + 4, high)):
                out_ref[d, :DATA_ROWS, :] = value.astype(BF16)
                out_ref[d, DATA_ROWS:, :] = lists


def whiten_kernel(slab_ref, out_ref, swapped_ref, last_ref):
    order = order_table()
    both = fold_table(1.0, 1.0)
    both = jnp.concatenate([both, both], axis=0)
    swap = swap_table()
    batch = 4
    for first in range(0, PLANE, batch):
        rows = []
        for p in range(first, first + batch):
            rows.append(jnp.concatenate([slab_ref[p * LAGS + n, :DATA_ROWS, :] for n in range(LAGS)], axis=1))
        values = jnp.dot(jnp.concatenate(rows, axis=0), order, preferred_element_type=F32)
        values = jnp.concatenate([values[:, g * WIDE : (g + 1) * WIDE] for g in range(4)], axis=0)
        high, low = halves_of(values * values)
        power = jnp.dot(jnp.concatenate([high, low], axis=1), both, preferred_element_type=F32)
        whitened = (values * lax.rsqrt(power * (1.0 / WINDOWS) + WATER)).astype(BF16)
        turned = jnp.dot(whitened, swap, preferred_element_type=F32).astype(BF16)
        for n in range(batch):
            for g in range(4):
                at = (g * batch + n) * 32
                out_ref[first + n, g * 32 : (g + 1) * 32, :] = whitened[at : at + 32]
                swapped_ref[first + n, g * 32 : (g + 1) * 32, :] = turned[at : at + 32]
                if first == PLANE - ROUNDS:
                    last_ref[n, g * 32 : (g + 1) * 32, :] = whitened[at : at + 32]


def chosen_kernel(slab_ref, out_ref, owner_ref):
    row = lax.broadcasted_iota(jnp.int32, (CB, PCAP), 0).astype(F32)

    def one(p, carry):
        value = jnp.concatenate([slab_ref[p * LAGS + n, DATA_ROWS:, :] for n in range(LAGS)], axis=1).astype(F32)
        owner_ref[pl.ds(p, 1), :] = value[MEETINGS : MEETINGS + 1, :WIDE].astype(jnp.int32)
        odd = jnp.where(value < 0.0, 1.0, 0.0)
        size = jnp.abs(value)
        live = size > 0.0
        exponent = jnp.zeros(value.shape, F32)
        for bit in (5, 4, 3, 2, 1, 0):
            large = size >= 2.0 ** (1 << bit)
            size = jnp.where(large, size * 2.0 ** -(1 << bit), size)
            exponent = jnp.where(large, exponent + 2.0**bit, exponent)
        first = jnp.where(live, 2.0 * exponent + odd, -1.0)
        second = (size - 1.0) * CB
        for o in range(MEETINGS):
            pick_first = jnp.where(row == first[o : o + 1], 1.0, 0.0).astype(BF16)
            pick_second = jnp.where(row == second[o : o + 1], 1.0, 0.0).astype(BF16)
            chosen = lax.dot_general(pick_first, pick_second, (((1,), (1,)), ((), ())), preferred_element_type=F32)
            out_ref[p, o] = chosen.astype(BF16)
        return carry

    lax.fori_loop(0, PLANE, one, 0, unroll=16)


def fill_bins(bins_ref):
    spread = lax.broadcasted_iota(jnp.int32, (CB, CB), 1) - lax.broadcasted_iota(jnp.int32, (CB, CB), 0)
    at = 0
    for o, k, lo, hi in SPANS:
        distance = spread[lo:hi] + CB * o
        inside = (distance >= BINW * k) & (distance < BINW * (k + 1))
        bins_ref[at : at + hi - lo, :] = jnp.where(inside, 1.0, 0.0).astype(BF16)
        at += hi - lo


def meet(out_ref, owner_ref, bins_ref, chosen_ref, at_block, block, partners, p):
    row_id = lax.broadcasted_iota(jnp.int32, (NBIN, WIDE), 0)
    at = 0
    pieces = []
    for o, _, lo, hi in SPANS:
        pieces.append(chosen_ref[at_block, o, lo:hi, :] * bins_ref[at : at + hi - lo, :])
        at += hi - lo
    mixed = jnp.dot(jnp.concatenate(pieces, axis=0), block, preferred_element_type=F32)
    at = 0
    real, imag = [], []
    for o in range(MEETINGS):
        straight = partners[o][0].astype(F32)
        swapped = partners[o][1].astype(F32)
        for k, lo, hi in LEVELS[o]:
            part = mixed[at : at + hi - lo]
            at += hi - lo
            dims = ((hi - lo) // 8, 8, WIDE)
            real.append(jnp.sum((straight[lo:hi] * part).reshape(dims), axis=0))
            imag.append(jnp.sum((swapped[lo:hi] * part).reshape(dims), axis=0))
    at = 0
    for o in range(MEETINGS):
        re = jnp.zeros((NBIN, WIDE), F32)
        im = jnp.zeros((NBIN, WIDE), F32)
        for k, _, _ in LEVELS[o]:
            re = jnp.where(row_id == k, jnp.sum(real[at], axis=0, keepdims=True), re)
            im = jnp.where(row_id == k, jnp.sum(imag[at], axis=0, keepdims=True), im)
            at += 1
        found = jnp.where(real_lanes(), fold(re), fold(im))
        spot = owner_ref[p, o]
        out_ref[spot] = out_ref[spot] + found


def meetings_kernel(
    owner_ref, chosen_ref, group_ref, swapped_ref, below_ref, out_ref, bins_ref, all_ref, turned_ref, total_ref
):
    total_ref[...] = jnp.zeros(total_ref.shape, F32)
    fill_bins(bins_ref)
    swap = swap_table()
    for n in range(ROUNDS):
        all_ref[n] = below_ref[n]
        turned_ref[n] = jnp.dot(below_ref[n], swap, preferred_element_type=F32).astype(BF16)
    all_ref[ROUNDS:] = group_ref[...]
    turned_ref[ROUNDS:] = swapped_ref[...]

    def one(p, carry):
        partners = [(all_ref[p + ROUNDS - o], turned_ref[p + ROUNDS - o]) for o in range(MEETINGS)]
        meet(total_ref, owner_ref, bins_ref, chosen_ref, p, group_ref[p], partners, p)
        return carry

    lax.fori_loop(0, PLANE, one, 0, unroll=16)
    row_id = lax.broadcasted_iota(jnp.int32, (NBIN, WIDE), 0)
    own_piece = (lanes() >> 4) == row_id
    for n in range(0, ROWS * PLANE, 2):
        pair = []
        for owner in (n, n + 1):
            value = jnp.where(own_piece, total_ref[owner], 0.0)
            pair.append(jnp.sum(value, axis=0, keepdims=True))
        out_ref[n * LAGS : (n + 2) * LAGS, :] = jnp.where(row_id < LAGS, pair[0], pair[1])


def lag_kernel(lag_ref, parts_ref, table_ref, out_ref, order_ref):
    lane = lanes()
    sign = jnp.where(real_lanes(), -1.0, 1.0)
    step = (lane * (lag_ref[0] + 2)) & 3
    along = jnp.where(step == 0, 1.0, 0.0) - jnp.where(step == 2, 1.0, 0.0)
    across = sign * (jnp.where(step == 1, 1.0, 0.0) - jnp.where(step == 3, 1.0, 0.0))
    pieces = []
    for n in range(8):
        value = parts_ref[pl.ds(n, 8, stride=8), :]
        for y in range(1, ROWS):
            value = value + parts_ref[pl.ds(y * PLANE * LAGS + n, 8, stride=8), :]
        pieces.append(value)
    for k, value in enumerate(transpose_pieces(pieces, 2 * BAND)):
        swapped = jnp.where(real_lanes(), pltpu.roll(value, WIDE - BAND, 1), pltpu.roll(value, BAND, 1))
        order_ref[pl.ds(k, 8, stride=8), :] = value * along + swapped * across
    columns = [order_ref[n * NBIN : (n + 1) * NBIN, :] for n in range(8)]
    out_ref[0] = split_dot(jnp.concatenate(columns, axis=1), table_ref[...])


def early_part(place, *inputs):
    operands = [pltpu.with_memory_space_constraint(value, pltpu.HBM) for value in inputs]
    return pl.pallas_call(
        early_kernel,
        out_shape=(
            shape((CB, WIN), BF16),
            shape((CB, WIN), F32),
            shape((CB, TAPS), F32),
            shape((2 * TAPS, 2 * TAPS), BF16),
            shape((TAPS, WIN), BF16),
            shape((SLAB_ROWS - DATA_ROWS, WIDE), BF16),
        ),
        in_specs=[pl.BlockSpec(memory_space=pltpu.SMEM)] + [pl.BlockSpec(memory_space=pltpu.HBM)] * 6,
        out_specs=[pl.BlockSpec(memory_space=pltpu.VMEM)] * 6,
        scratch_shapes=[
            pltpu.VMEM((CB, 2 * WIN), F32),
            pltpu.VMEM((2 * TAPS, 2 * TAPS), BF16),
            pltpu.VMEM((HALF, WIN), BF16),
            pltpu.VMEM((1, MEETINGS), jnp.int32),
            pltpu.VMEM((1, MEETINGS), jnp.int32),
            pltpu.VMEM((MEETINGS, PCAP), jnp.int32),
            pltpu.SemaphoreType.DMA((7,)),
        ],
        compiler_params=pltpu.CompilerParams(vmem_limit_bytes=VMEM_LIMIT),
    )(place, *operands)


def row_below(blocks):
    return lax.ppermute(blocks, "row", [(i, i + 1) for i in range(ROWS - 1)])


def middle(slabs, send):
    blocks = (PLANE, CB, WIDE)
    group, swapped, last = call(
        whiten_kernel, (shape(blocks, BF16), shape(blocks, BF16), shape((ROUNDS, CB, WIDE), BF16)), slabs
    )
    below = send(last)
    chosen, owners = call(
        chosen_kernel, (shape((PLANE, MEETINGS, CB, CB), BF16), shape((PLANE, WIDE), jnp.int32)), slabs
    )
    sums_shape = (ROWS * PLANE, NBIN, WIDE)
    more = pltpu.VMEM((PLANE + ROUNDS, CB, WIDE), BF16)
    return call(
        meetings_kernel,
        shape((ROWS * PLANE * LAGS, WIDE), F32),
        owners,
        chosen,
        group,
        swapped,
        below,
        smem=(0,),
        scratch=(pltpu.VMEM((SPAN_ROWS, CB), BF16), more, more, pltpu.VMEM(sums_shape, F32)),
    )


def body(traces, owner_map, pair_codes, pair_count):
    blk = (lax.axis_index("row") * PLANE + lax.axis_index("plane")).astype(jnp.int32)
    lag = lax.axis_index("lag").astype(jnp.int32)
    taps = jnp.asarray(filter_table())
    table = jnp.asarray(transform_table())

    history = lax.ppermute(traces[:, -TAPS:], "lag", [(i, i + 1) for i in range(3)])

    spectra1, part, head, taps, table, lists = early_part(
        jnp.stack([blk, lag]),
        traces,
        taps,
        table,
        pair_count.reshape(1, MEETINGS),
        owner_map.reshape(1, MEETINGS),
        pair_codes,
    )
    slabs = call(
        pack_kernel,
        shape((PLANE * LAGS, SLAB_ROWS, WIDE), BF16),
        lists,
        history,
        head,
        taps,
        table,
        part,
        spectra1,
    )
    slabs = lax.all_to_all(slabs, ("plane", "lag"), 0, 0, tiled=True)
    sums = middle(slabs, row_below)
    parts = lax.all_to_all(sums, ("row", "plane", "lag"), 0, 0, tiled=True)
    return call(
        lag_kernel,
        shape((1, NBIN, LANES), F32),
        lag.reshape(1),
        parts,
        jnp.asarray(inverse_table()),
        smem=(0,),
        scratch=(pltpu.VMEM((8 * NBIN, WIDE), F32),),
    )


def solution(mesh):
    split = Mesh(mesh.devices.reshape(ROWS, PLANE, 4), ("row", "plane", "lag"))
    owned = ("row", "plane")
    return jax.shard_map(
        body,
        mesh=split,
        in_specs=(P(owned, "lag"), P(None, owned), P(None, owned), P(None, owned)),
        out_specs=P(owned, None, "lag"),
        check_vma=False,
    )
```

```python
import math

import jax
import jax.numpy as jnp
import numpy as np
from jax import lax
from jax.experimental import pallas as pl
from jax.experimental.pallas import tpu as pltpu
from jax.sharding import Mesh
from jax.sharding import PartitionSpec as P

CB = 128
WIN = 1024
HALF = 512
NF = 512
TAPS = 128
NBIN = 8
BINW = 80
ROUNDS = 4
MEETINGS = 5
PCAP = 512
WINDOWS = 8
LANES = 256
PLANE = 16
ROWS = 4
LAGS = 4
WIDE = 128
BAND = 8
DATA_ROWS = 32
SLAB_ROWS = 40

BAND_LOW = 0.02
BAND_HIGH = 0.48
WATER = 0.1

F32 = jnp.float32
BF16 = jnp.bfloat16
VMEM_LIMIT = 16 * 1024 * 1024


def level_rows(o):
    found = []
    for k in range(NBIN):
        pairs = [
            i
            for i in range(CB)
            for j in range(CB)
            if (o > 0 or i < j) and (CB * o + j - i) // BINW == k
        ]
        if pairs:
            found.append((k, min(pairs) // 16 * 16, max(pairs) // 16 * 16 + 16))
    return tuple(found)


LEVELS = tuple(level_rows(o) for o in range(MEETINGS))
SPANS = tuple((o, k, lo, hi) for o in range(MEETINGS) for k, lo, hi in LEVELS[o])
SPAN_ROWS = sum(hi - lo for _, _, lo, hi in SPANS)


def two_terms(table):
    high = table.astype(jnp.bfloat16)
    low = (table - high.astype(np.float32)).astype(jnp.bfloat16)
    return np.concatenate([high, low], axis=1)


def filter_table():
    k = np.arange(TAPS, dtype=np.float64)
    m = k - (TAPS - 1) / 2.0
    ideal = 2 * BAND_HIGH * np.sinc(2 * BAND_HIGH * m) - 2 * BAND_LOW * np.sinc(2 * BAND_LOW * m)
    taps = ideal * (0.5 - 0.5 * np.cos(2 * np.pi * (k + 0.5) / TAPS))
    lagged = np.arange(TAPS)[None, :] - np.arange(2 * TAPS)[:, None] + TAPS
    inside = (lagged >= 0) & (lagged < TAPS)
    return two_terms(np.where(inside, taps[np.clip(lagged, 0, TAPS - 1)], 0.0).astype(np.float32))


def column_order():
    column = np.arange(WIN)
    return column // (2 * BAND) * BAND + column % BAND, column // BAND % 2 == 1


def transform_table():
    freq, is_imag = column_order()
    angle = (np.arange(HALF)[:, None] * freq[None, :] % WIN) * (2 * np.pi / WIN)
    return (np.where(is_imag[None, :], -np.sin(angle), np.cos(angle)) / math.sqrt(WIN)).astype(jnp.bfloat16)


def inverse_table():
    freq, is_imag = column_order()
    angle = (freq[:, None] * np.arange(LANES)[None, :] % WIN) * (2 * np.pi / WIN)
    weight = np.where(freq == 0, 1.0, 2.0)[:, None] / (WINDOWS * math.sqrt(WIN))
    return two_terms((weight * np.where(is_imag[:, None], -np.sin(angle), np.cos(angle))).astype(np.float32))


def call(kernel, out_shape, *args, smem=(), aliases=None, scratch=()):
    specs = [
        pl.BlockSpec(memory_space=pltpu.SMEM) if n in smem else pl.BlockSpec(memory_space=pltpu.VMEM)
        for n in range(len(args))
    ]
    many = isinstance(out_shape, (tuple, list))
    out_specs = [pl.BlockSpec(memory_space=pltpu.VMEM)] * len(out_shape) if many else pl.BlockSpec(memory_space=pltpu.VMEM)
    return pl.pallas_call(
        kernel,
        out_shape=out_shape,
        in_specs=specs,
        out_specs=out_specs,
        input_output_aliases=aliases or {},
        scratch_shapes=list(scratch),
        compiler_params=pltpu.CompilerParams(vmem_limit_bytes=VMEM_LIMIT),
    )(*args)


def shape(dims, dtype):
    return jax.ShapeDtypeStruct(dims, dtype)


def lanes():
    return lax.broadcasted_iota(jnp.int32, (1, WIDE), 1)


def real_lanes():
    return (lanes() & BAND) == 0


def fold(values):
    for step in (BAND, 2 * BAND, 4 * BAND, 8 * BAND):
        values = values + pltpu.roll(values, step, 1)
    return values


def fold_table(real, imag):
    row = lax.broadcasted_iota(jnp.int32, (WIDE, WIDE), 0)
    column = lax.broadcasted_iota(jnp.int32, (WIDE, WIDE), 1)
    same = ((row ^ column) & (BAND - 1)) == 0
    asked = jnp.where((column & BAND) == 0, real, imag)
    return jnp.where(same, asked, 0.0).astype(BF16)


def swap_table():
    row = lax.broadcasted_iota(jnp.int32, (WIDE, WIDE), 0)
    column = lax.broadcasted_iota(jnp.int32, (WIDE, WIDE), 1)
    value = jnp.where((column & BAND) == 0, -1.0, 1.0)
    return jnp.where(row == (column ^ BAND), value, 0.0).astype(BF16)


def order_table():
    row = lax.broadcasted_iota(jnp.int32, (4 * WIDE, 1), 0)
    goal = ((row >> 5) & 3) * WIDE + (row >> 7) * 32 + (row & 31)
    column = lax.broadcasted_iota(jnp.int32, (4 * WIDE, 4 * WIDE), 1)
    return jnp.where(column == goal, 1.0, 0.0).astype(BF16)


def halves_of(values):
    high = values.astype(BF16)
    return high, (values - high.astype(F32)).astype(BF16)


def split_dot(values, table):
    high, low = halves_of(values)
    count, width = values.shape[0], table.shape[1] // 2
    out = jnp.dot(jnp.concatenate([high, low], axis=0), table, preferred_element_type=F32)
    small = out[count:, width:] + (out[count:, :width] + out[:count, width:])
    return small + out[:count, :width]


def transpose_pieces(arrays, width):
    bit = 1
    while bit < len(arrays):
        upper = (lanes() & (bit * width)) != 0
        out = list(arrays)
        for q in range(len(arrays)):
            if q & bit:
                continue
            a, b = arrays[q], arrays[q | bit]
            out[q] = jnp.where(upper, pltpu.roll(b, bit * width, 1), a)
            out[q | bit] = jnp.where(upper, b, pltpu.roll(a, WIDE - bit * width, 1))
        arrays = out
        bit *= 2
    return arrays


def turns():
    column = lax.broadcasted_iota(jnp.int32, (1, WIN), 1)
    return jnp.where(column % 2 == 0, 1.0, -1.0).astype(F32)


def early_kernel(
    place_ref, traces_ref, taps_ref, table_ref, counts_in, owners_in, codes_in,
    s1_ref, part_ref, head_ref, taps_out, table_out, lists_ref,
    x_ref, h_ref, d_ref, count_ref, owner_ref, codes_ref, sems,
):
    late = WIN - TAPS
    copies = [
        pltpu.make_async_copy(traces_ref.at[:, late:], x_ref.at[:, late:], sems.at[0]),
        pltpu.make_async_copy(taps_ref, h_ref, sems.at[1]),
        pltpu.make_async_copy(table_ref, d_ref, sems.at[2]),
        pltpu.make_async_copy(traces_ref.at[:, :late], x_ref.at[:, :late], sems.at[3]),
        pltpu.make_async_copy(counts_in, count_ref, sems.at[4]),
        pltpu.make_async_copy(owners_in, owner_ref, sems.at[5]),
        pltpu.make_async_copy(codes_in, codes_ref, sems.at[6]),
    ]
    for copy in copies:
        copy.start()

    def filtered(first, last):
        pairs = [x_ref[:, (t - 1) * TAPS : (t + 1) * TAPS] for t in range(first, last)]
        rows = split_dot(jnp.concatenate(pairs, axis=0), h_ref[...]).astype(BF16)
        return [rows[n * CB : (n + 1) * CB] for n in range(last - first)]

    copies[0].wait()
    copies[1].wait()
    tiles = filtered(8, 16)
    copies[3].wait()
    tiles = [jnp.zeros((CB, TAPS), BF16)] + filtered(1, 8) + tiles
    copies[2].wait()
    rows = [jnp.concatenate(tiles[n : n + 4], axis=1) for n in (0, 4, 8, 12)]
    first = jnp.dot(jnp.concatenate(rows[0::2], axis=0), d_ref[...], preferred_element_type=F32)
    second = jnp.dot(jnp.concatenate(rows[1::2], axis=0), d_ref[...], preferred_element_type=F32)
    both = first + turns() * second
    part_ref[...] = both[:CB]
    s1_ref[...] = both[CB:].astype(BF16)
    head_ref[...] = x_ref[:, :TAPS]
    taps_out[...] = h_ref[...]
    table_out[...] = d_ref[:TAPS, :]
    for copy in copies[4:]:
        copy.wait()
    lists_ref[...] = list_rows(place_ref, count_ref, owner_ref, codes_ref)


def pack_table():
    row = lax.broadcasted_iota(jnp.int32, (4 * WIDE, 1), 0)
    goal = ((row >> 4) & 3) * WIDE + ((row >> 6) & 1) * (WIDE // 2) + (row >> 7) * 16 + (row & 15)
    column = lax.broadcasted_iota(jnp.int32, (4 * WIDE, 4 * WIDE), 1)
    return jnp.where(column == goal, 1.0, 0.0).astype(BF16)


def list_rows(place_ref, count_ref, owner_ref, codes_ref):
    lane = lanes()
    start = pl.multiple_of(place_ref[1] * WIDE, WIDE)
    codes = codes_ref[:, pl.ds(start, WIDE)]
    exponent = codes >> 8
    value = 1.0 + (codes & (CB - 1)).astype(F32) * (1.0 / CB)
    for bit in range(6):
        value = jnp.where(((exponent >> bit) & 1) == 1, value * 2.0 ** (1 << bit), value)
    value = jnp.where(((codes >> 7) & 1) == 1, -value, value)
    rows = []
    owners = jnp.zeros((1, WIDE), F32)
    for o in range(MEETINGS):
        live = jnp.where(place_ref[0] >= o, count_ref[:, o : o + 1], 0)
        rows.append(jnp.where(lane + start < live, value[o : o + 1], 0.0))
        owner = owner_ref[:, o : o + 1]
        owners = jnp.where(lane == o, owner.astype(F32), owners)
    rows = rows + [owners] + [jnp.zeros((1, WIDE), F32)] * (SLAB_ROWS - DATA_ROWS - MEETINGS - 1)
    return jnp.concatenate(rows, axis=0).astype(BF16)


def pack_kernel(
    lists_ref, hist_ref, head_ref, taps_ref, table_ref, part_ref, s1_ref, out_ref
):
    rows = split_dot(jnp.concatenate([hist_ref[...], head_ref[...]], axis=1), taps_ref[...]).astype(BF16)
    s0 = (part_ref[...] + jnp.dot(rows, table_ref[...], preferred_element_type=F32)).astype(BF16)
    s1 = s1_ref[...]
    lists = lists_ref[...]
    order = pack_table()
    for c in range(WIN // WIDE):
        cols = slice(c * WIDE, (c + 1) * WIDE)
        halves = []
        for g in range(0, 4, 2):
            pieces = [value[n * 32 : (n + 1) * 32, cols] for n in (g, g + 1) for value in (s0, s1)]
            halves.append(jnp.concatenate(pieces, axis=1))
        mixed = jnp.dot(jnp.concatenate(halves, axis=0), order, preferred_element_type=F32)
        upper = lanes() >= WIDE // 2
        for e in range(4):
            first = mixed[:DATA_ROWS, e * WIDE : (e + 1) * WIDE]
            second = mixed[DATA_ROWS:, e * WIDE : (e + 1) * WIDE]
            low = jnp.where(upper, pltpu.roll(second, WIDE // 2, 1), first)
            high = jnp.where(upper, second, pltpu.roll(first, WIDE // 2, 1))
            for d, value in ((c * 8 + e, low), (c * 8 + e + 4, high)):
                out_ref[d, :DATA_ROWS, :] = value.astype(BF16)
                out_ref[d, DATA_ROWS:, :] = lists


def tables_kernel(place_ref, order_ref, both_ref, swap_ref, bins_ref):
    order_ref[...] = order_table()
    both = fold_table(1.0, 1.0)
    both_ref[...] = jnp.concatenate([both, both], axis=0)
    swap_ref[...] = swap_table()
    fill_bins(bins_ref)


def whiten_kernel(slab_ref, order_ref, both_ref, swap_ref, out_ref, swapped_ref, last_ref):
    order, both, swap = order_ref[...], both_ref[...], swap_ref[...]
    batch = 4
    for first in range(0, PLANE, batch):
        rows = []
        for p in range(first, first + batch):
            rows.append(jnp.concatenate([slab_ref[p * LAGS + n, :DATA_ROWS, :] for n in range(LAGS)], axis=1))
        values = jnp.dot(jnp.concatenate(rows, axis=0), order, preferred_element_type=F32)
        values = jnp.concatenate([values[:, g * WIDE : (g + 1) * WIDE] for g in range(4)], axis=0)
        high, low = halves_of(values * values)
        power = jnp.dot(jnp.concatenate([high, low], axis=1), both, preferred_element_type=F32)
        whitened = (values * lax.rsqrt(power * (1.0 / WINDOWS) + WATER)).astype(BF16)
        turned = jnp.dot(whitened, swap, preferred_element_type=F32).astype(BF16)
        for n in range(batch):
            for g in range(4):
                at = (g * batch + n) * 32
                out_ref[first + n, g * 32 : (g + 1) * 32, :] = whitened[at : at + 32]
                swapped_ref[first + n, g * 32 : (g + 1) * 32, :] = turned[at : at + 32]
                if first == PLANE - ROUNDS:
                    last_ref[n, g * 32 : (g + 1) * 32, :] = whitened[at : at + 32]


def chosen_kernel(slab_ref, out_ref, owner_ref):
    row = lax.broadcasted_iota(jnp.int32, (CB, PCAP), 0).astype(F32)

    def one(p, carry):
        value = jnp.concatenate([slab_ref[p * LAGS + n, DATA_ROWS:, :] for n in range(LAGS)], axis=1).astype(F32)
        owner_ref[pl.ds(p, 1), :] = value[MEETINGS : MEETINGS + 1, :WIDE].astype(jnp.int32)
        odd = jnp.where(value < 0.0, 1.0, 0.0)
        size = jnp.abs(value)
        live = size > 0.0
        exponent = jnp.zeros(value.shape, F32)
        for bit in (5, 4, 3, 2, 1, 0):
            large = size >= 2.0 ** (1 << bit)
            size = jnp.where(large, size * 2.0 ** -(1 << bit), size)
            exponent = jnp.where(large, exponent + 2.0**bit, exponent)
        first = jnp.where(live, 2.0 * exponent + odd, -1.0)
        second = (size - 1.0) * CB
        for o in range(MEETINGS):
            pick_first = jnp.where(row == first[o : o + 1], 1.0, 0.0).astype(BF16)
            pick_second = jnp.where(row == second[o : o + 1], 1.0, 0.0).astype(BF16)
            chosen = lax.dot_general(pick_first, pick_second, (((1,), (1,)), ((), ())), preferred_element_type=F32)
            out_ref[p, o] = chosen.astype(BF16)
        return carry

    lax.fori_loop(0, PLANE, one, 0, unroll=16)


def fill_bins(bins_ref):
    spread = lax.broadcasted_iota(jnp.int32, (CB, CB), 1) - lax.broadcasted_iota(jnp.int32, (CB, CB), 0)
    at = 0
    for o, k, lo, hi in SPANS:
        distance = spread[lo:hi] + CB * o
        inside = (distance >= BINW * k) & (distance < BINW * (k + 1))
        bins_ref[at : at + hi - lo, :] = jnp.where(inside, 1.0, 0.0).astype(BF16)
        at += hi - lo


def meet(out_ref, owner_ref, bins_ref, chosen_ref, at_block, block, partners, p):
    row_id = lax.broadcasted_iota(jnp.int32, (NBIN, WIDE), 0)
    at = 0
    pieces = []
    for o, _, lo, hi in SPANS:
        pieces.append(chosen_ref[at_block, o, lo:hi, :] * bins_ref[at : at + hi - lo, :])
        at += hi - lo
    mixed = jnp.dot(jnp.concatenate(pieces, axis=0), block, preferred_element_type=F32)
    at = 0
    real, imag = [], []
    for o in range(MEETINGS):
        straight = partners[o][0].astype(F32)
        swapped = partners[o][1].astype(F32)
        for k, lo, hi in LEVELS[o]:
            part = mixed[at : at + hi - lo]
            at += hi - lo
            dims = ((hi - lo) // 8, 8, WIDE)
            real.append(jnp.sum((straight[lo:hi] * part).reshape(dims), axis=0))
            imag.append(jnp.sum((swapped[lo:hi] * part).reshape(dims), axis=0))
    at = 0
    for o in range(MEETINGS):
        re = jnp.zeros((NBIN, WIDE), F32)
        im = jnp.zeros((NBIN, WIDE), F32)
        for k, _, _ in LEVELS[o]:
            re = jnp.where(row_id == k, jnp.sum(real[at], axis=0, keepdims=True), re)
            im = jnp.where(row_id == k, jnp.sum(imag[at], axis=0, keepdims=True), im)
            at += 1
        found = jnp.where(real_lanes(), fold(re), fold(im))
        spot = owner_ref[p, o]
        out_ref[spot] = out_ref[spot] + found


def meetings_kernel(
    owner_ref, chosen_ref, group_ref, swapped_ref, below_ref, bins_ref, swap_ref, out_ref, all_ref, turned_ref, total_ref
):
    total_ref[...] = jnp.zeros(total_ref.shape, F32)
    swap = swap_ref[...]
    for n in range(ROUNDS):
        all_ref[n] = below_ref[n]
        turned_ref[n] = jnp.dot(below_ref[n], swap, preferred_element_type=F32).astype(BF16)
    all_ref[ROUNDS:] = group_ref[...]
    turned_ref[ROUNDS:] = swapped_ref[...]

    def one(p, carry):
        partners = [(all_ref[p + ROUNDS - o], turned_ref[p + ROUNDS - o]) for o in range(MEETINGS)]
        meet(total_ref, owner_ref, bins_ref, chosen_ref, p, group_ref[p], partners, p)
        return carry

    lax.fori_loop(0, PLANE, one, 0, unroll=16)
    row_id = lax.broadcasted_iota(jnp.int32, (NBIN, WIDE), 0)
    own_piece = (lanes() >> 4) == row_id
    for n in range(0, ROWS * PLANE, 2):
        pair = []
        for owner in (n, n + 1):
            value = jnp.where(own_piece, total_ref[owner], 0.0)
            pair.append(jnp.sum(value, axis=0, keepdims=True))
        out_ref[n * LAGS : (n + 2) * LAGS, :] = jnp.where(row_id < LAGS, pair[0], pair[1])


def lag_kernel(lag_ref, parts_ref, table_ref, out_ref, order_ref):
    lane = lanes()
    sign = jnp.where(real_lanes(), -1.0, 1.0)
    step = (lane * (lag_ref[0] + 2)) & 3
    along = jnp.where(step == 0, 1.0, 0.0) - jnp.where(step == 2, 1.0, 0.0)
    across = sign * (jnp.where(step == 1, 1.0, 0.0) - jnp.where(step == 3, 1.0, 0.0))
    pieces = []
    for n in range(8):
        value = parts_ref[pl.ds(n, 8, stride=8), :]
        for y in range(1, ROWS):
            value = value + parts_ref[pl.ds(y * PLANE * LAGS + n, 8, stride=8), :]
        pieces.append(value)
    for k, value in enumerate(transpose_pieces(pieces, 2 * BAND)):
        swapped = jnp.where(real_lanes(), pltpu.roll(value, WIDE - BAND, 1), pltpu.roll(value, BAND, 1))
        order_ref[pl.ds(k, 8, stride=8), :] = value * along + swapped * across
    columns = [order_ref[n * NBIN : (n + 1) * NBIN, :] for n in range(8)]
    out_ref[0] = split_dot(jnp.concatenate(columns, axis=1), table_ref[...])


def early_part(place, *inputs):
    operands = [pltpu.with_memory_space_constraint(value, pltpu.HBM) for value in inputs]
    return pl.pallas_call(
        early_kernel,
        out_shape=(
            shape((CB, WIN), BF16),
            shape((CB, WIN), F32),
            shape((CB, TAPS), F32),
            shape((2 * TAPS, 2 * TAPS), BF16),
            shape((TAPS, WIN), BF16),
            shape((SLAB_ROWS - DATA_ROWS, WIDE), BF16),
        ),
        in_specs=[pl.BlockSpec(memory_space=pltpu.SMEM)] + [pl.BlockSpec(memory_space=pltpu.HBM)] * 6,
        out_specs=[pl.BlockSpec(memory_space=pltpu.VMEM)] * 6,
        scratch_shapes=[
            pltpu.VMEM((CB, 2 * WIN), F32),
            pltpu.VMEM((2 * TAPS, 2 * TAPS), BF16),
            pltpu.VMEM((HALF, WIN), BF16),
            pltpu.VMEM((1, MEETINGS), jnp.int32),
            pltpu.VMEM((1, MEETINGS), jnp.int32),
            pltpu.VMEM((MEETINGS, PCAP), jnp.int32),
            pltpu.SemaphoreType.DMA((7,)),
        ],
        compiler_params=pltpu.CompilerParams(vmem_limit_bytes=VMEM_LIMIT),
    )(place, *operands)


def row_below(blocks):
    return lax.ppermute(blocks, "row", [(i, i + 1) for i in range(ROWS - 1)])


def middle(slabs, send, order, both, swap, bins):
    blocks = (PLANE, CB, WIDE)
    group, swapped, last = call(
        whiten_kernel, (shape(blocks, BF16), shape(blocks, BF16), shape((ROUNDS, CB, WIDE), BF16)), slabs, order, both, swap
    )
    below = send(last)
    chosen, owners = call(
        chosen_kernel, (shape((PLANE, MEETINGS, CB, CB), BF16), shape((PLANE, WIDE), jnp.int32)), slabs
    )
    sums_shape = (ROWS * PLANE, NBIN, WIDE)
    more = pltpu.VMEM((PLANE + ROUNDS, CB, WIDE), BF16)
    return call(
        meetings_kernel,
        shape((ROWS * PLANE * LAGS, WIDE), F32),
        owners,
        chosen,
        group,
        swapped,
        below,
        bins,
        swap,
        smem=(0,),
        scratch=(more, more, pltpu.VMEM(sums_shape, F32)),
    )


def body(traces, owner_map, pair_codes, pair_count):
    blk = (lax.axis_index("row") * PLANE + lax.axis_index("plane")).astype(jnp.int32)
    lag = lax.axis_index("lag").astype(jnp.int32)
    taps = jnp.asarray(filter_table())
    table = jnp.asarray(transform_table())

    history = lax.ppermute(traces[:, -TAPS:], "lag", [(i, i + 1) for i in range(3)])

    spectra1, part, head, taps, table, lists = early_part(
        jnp.stack([blk, lag]),
        traces,
        taps,
        table,
        pair_count.reshape(1, MEETINGS),
        owner_map.reshape(1, MEETINGS),
        pair_codes,
    )
    slabs = call(
        pack_kernel,
        shape((PLANE * LAGS, SLAB_ROWS, WIDE), BF16),
        lists,
        history,
        head,
        taps,
        table,
        part,
        spectra1,
    )
    slabs, place = lax.optimization_barrier((slabs, lag.reshape(1)))
    table_shapes = ((4 * WIDE, 4 * WIDE), (2 * WIDE, WIDE), (WIDE, WIDE), (SPAN_ROWS, CB))
    tables = call(tables_kernel, tuple(shape(dims, BF16) for dims in table_shapes), place, smem=(0,))
    slabs = lax.all_to_all(slabs, ("plane", "lag"), 0, 0, tiled=True)
    slabs, *tables = lax.optimization_barrier((slabs, *tables))
    sums = middle(slabs, row_below, *tables)
    parts = lax.all_to_all(sums, ("row", "plane", "lag"), 0, 0, tiled=True)
    return call(
        lag_kernel,
        shape((1, NBIN, LANES), F32),
        lag.reshape(1),
        parts,
        jnp.asarray(inverse_table()),
        smem=(0,),
        scratch=(pltpu.VMEM((8 * NBIN, WIDE), F32),),
    )


def solution(mesh):
    split = Mesh(mesh.devices.reshape(ROWS, PLANE, 4), ("row", "plane", "lag"))
    owned = ("row", "plane")
    return jax.shard_map(
        body,
        mesh=split,
        in_specs=(P(owned, "lag"), P(None, owned), P(None, owned), P(None, owned)),
        out_specs=P(owned, None, "lag"),
        check_vma=False,
    )
```

```python
import math

import jax
import jax.numpy as jnp
import numpy as np
from jax import lax
from jax.experimental import pallas as pl
from jax.experimental.pallas import tpu as pltpu
from jax.sharding import Mesh
from jax.sharding import PartitionSpec as P

CB = 128
WIN = 1024
HALF = 512
NF = 512
TAPS = 128
NBIN = 8
BINW = 80
ROUNDS = 4
MEETINGS = 5
PCAP = 512
WINDOWS = 8
LANES = 256
PLANE = 16
ROWS = 4
LAGS = 4
WIDE = 128
BAND = 8
DATA_ROWS = 32
SLAB_ROWS = 40

BAND_LOW = 0.02
BAND_HIGH = 0.48
WATER = 0.1

F32 = jnp.float32
BF16 = jnp.bfloat16
VMEM_LIMIT = 16 * 1024 * 1024


def level_rows(o):
    found = []
    for k in range(NBIN):
        pairs = [
            i
            for i in range(CB)
            for j in range(CB)
            if (o > 0 or i < j) and (CB * o + j - i) // BINW == k
        ]
        if pairs:
            found.append((k, min(pairs) // 16 * 16, max(pairs) // 16 * 16 + 16))
    return tuple(found)


LEVELS = tuple(level_rows(o) for o in range(MEETINGS))
SPANS = tuple((o, k, lo, hi) for o in range(MEETINGS) for k, lo, hi in LEVELS[o])
SPAN_ROWS = sum(hi - lo for _, _, lo, hi in SPANS)


def two_terms(table):
    high = table.astype(jnp.bfloat16)
    low = (table - high.astype(np.float32)).astype(jnp.bfloat16)
    return np.concatenate([high, low], axis=1)


def filter_table():
    k = np.arange(TAPS, dtype=np.float64)
    m = k - (TAPS - 1) / 2.0
    ideal = 2 * BAND_HIGH * np.sinc(2 * BAND_HIGH * m) - 2 * BAND_LOW * np.sinc(2 * BAND_LOW * m)
    taps = ideal * (0.5 - 0.5 * np.cos(2 * np.pi * (k + 0.5) / TAPS))
    lagged = np.arange(TAPS)[None, :] - np.arange(2 * TAPS)[:, None] + TAPS
    inside = (lagged >= 0) & (lagged < TAPS)
    return two_terms(np.where(inside, taps[np.clip(lagged, 0, TAPS - 1)], 0.0).astype(np.float32))


def column_order():
    column = np.arange(WIN)
    return column // (2 * BAND) * BAND + column % BAND, column // BAND % 2 == 1


def transform_table():
    freq, is_imag = column_order()
    angle = (np.arange(HALF)[:, None] * freq[None, :] % WIN) * (2 * np.pi / WIN)
    return (np.where(is_imag[None, :], -np.sin(angle), np.cos(angle)) / math.sqrt(WIN)).astype(jnp.bfloat16)


def inverse_table():
    freq, is_imag = column_order()
    angle = (freq[:, None] * np.arange(LANES)[None, :] % WIN) * (2 * np.pi / WIN)
    weight = np.where(freq == 0, 1.0, 2.0)[:, None] / (WINDOWS * math.sqrt(WIN))
    return two_terms((weight * np.where(is_imag[:, None], -np.sin(angle), np.cos(angle))).astype(np.float32))


def call(kernel, out_shape, *args, smem=(), aliases=None, scratch=()):
    specs = [
        pl.BlockSpec(memory_space=pltpu.SMEM) if n in smem else pl.BlockSpec(memory_space=pltpu.VMEM)
        for n in range(len(args))
    ]
    many = isinstance(out_shape, (tuple, list))
    out_specs = [pl.BlockSpec(memory_space=pltpu.VMEM)] * len(out_shape) if many else pl.BlockSpec(memory_space=pltpu.VMEM)
    return pl.pallas_call(
        kernel,
        out_shape=out_shape,
        in_specs=specs,
        out_specs=out_specs,
        input_output_aliases=aliases or {},
        scratch_shapes=list(scratch),
        compiler_params=pltpu.CompilerParams(vmem_limit_bytes=VMEM_LIMIT),
    )(*args)


def shape(dims, dtype):
    return jax.ShapeDtypeStruct(dims, dtype)


def lanes():
    return lax.broadcasted_iota(jnp.int32, (1, WIDE), 1)


def real_lanes():
    return (lanes() & BAND) == 0


def fold(values):
    for step in (BAND, 2 * BAND, 4 * BAND, 8 * BAND):
        values = values + pltpu.roll(values, step, 1)
    return values


def fold_table(real, imag):
    row = lax.broadcasted_iota(jnp.int32, (WIDE, WIDE), 0)
    column = lax.broadcasted_iota(jnp.int32, (WIDE, WIDE), 1)
    same = ((row ^ column) & (BAND - 1)) == 0
    asked = jnp.where((column & BAND) == 0, real, imag)
    return jnp.where(same, asked, 0.0).astype(BF16)


def swap_table():
    row = lax.broadcasted_iota(jnp.int32, (WIDE, WIDE), 0)
    column = lax.broadcasted_iota(jnp.int32, (WIDE, WIDE), 1)
    value = jnp.where((column & BAND) == 0, -1.0, 1.0)
    return jnp.where(row == (column ^ BAND), value, 0.0).astype(BF16)


def order_table():
    row = lax.broadcasted_iota(jnp.int32, (4 * WIDE, 1), 0)
    goal = ((row >> 5) & 3) * WIDE + (row >> 7) * 32 + (row & 31)
    column = lax.broadcasted_iota(jnp.int32, (4 * WIDE, 4 * WIDE), 1)
    return jnp.where(column == goal, 1.0, 0.0).astype(BF16)


def halves_of(values):
    high = values.astype(BF16)
    return high, (values - high.astype(F32)).astype(BF16)


def split_dot(values, table):
    high, low = halves_of(values)
    count, width = values.shape[0], table.shape[1] // 2
    out = jnp.dot(jnp.concatenate([high, low], axis=0), table, preferred_element_type=F32)
    small = out[count:, width:] + (out[count:, :width] + out[:count, width:])
    return small + out[:count, :width]


def transpose_pieces(arrays, width):
    bit = 1
    while bit < len(arrays):
        upper = (lanes() & (bit * width)) != 0
        out = list(arrays)
        for q in range(len(arrays)):
            if q & bit:
                continue
            a, b = arrays[q], arrays[q | bit]
            out[q] = jnp.where(upper, pltpu.roll(b, bit * width, 1), a)
            out[q | bit] = jnp.where(upper, b, pltpu.roll(a, WIDE - bit * width, 1))
        arrays = out
        bit *= 2
    return arrays


def turns():
    column = lax.broadcasted_iota(jnp.int32, (1, WIN), 1)
    return jnp.where(column % 2 == 0, 1.0, -1.0).astype(F32)


def early_kernel(
    place_ref, traces_ref, taps_ref, table_ref, counts_in, owners_in, codes_in,
    s1_ref, part_ref, head_ref, taps_out, table_out, lists_ref, order_ref,
    x_ref, h_ref, d_ref, count_ref, owner_ref, codes_ref, sems,
):
    late = WIN - TAPS
    copies = [
        pltpu.make_async_copy(traces_ref.at[:, late:], x_ref.at[:, late:], sems.at[0]),
        pltpu.make_async_copy(taps_ref, h_ref, sems.at[1]),
        pltpu.make_async_copy(table_ref, d_ref, sems.at[2]),
        pltpu.make_async_copy(traces_ref.at[:, :late], x_ref.at[:, :late], sems.at[3]),
        pltpu.make_async_copy(counts_in, count_ref, sems.at[4]),
        pltpu.make_async_copy(owners_in, owner_ref, sems.at[5]),
        pltpu.make_async_copy(codes_in, codes_ref, sems.at[6]),
    ]
    for copy in copies:
        copy.start()
    order_ref[...] = pack_table()

    def filtered(first, last):
        pairs = [x_ref[:, (t - 1) * TAPS : (t + 1) * TAPS] for t in range(first, last)]
        rows = split_dot(jnp.concatenate(pairs, axis=0), h_ref[...]).astype(BF16)
        return [rows[n * CB : (n + 1) * CB] for n in range(last - first)]

    copies[0].wait()
    copies[1].wait()
    tiles = filtered(8, 16)
    copies[3].wait()
    tiles = [jnp.zeros((CB, TAPS), BF16)] + filtered(1, 8) + tiles
    copies[2].wait()
    rows = [jnp.concatenate(tiles[n : n + 4], axis=1) for n in (0, 4, 8, 12)]
    first = jnp.dot(jnp.concatenate(rows[0::2], axis=0), d_ref[...], preferred_element_type=F32)
    second = jnp.dot(jnp.concatenate(rows[1::2], axis=0), d_ref[...], preferred_element_type=F32)
    both = first + turns() * second
    part_ref[...] = both[:CB]
    s1_ref[...] = both[CB:].astype(BF16)
    head_ref[...] = x_ref[:, :TAPS]
    taps_out[...] = h_ref[...]
    table_out[...] = d_ref[:TAPS, :]
    for copy in copies[4:]:
        copy.wait()
    lists_ref[...] = list_rows(place_ref, count_ref, owner_ref, codes_ref)


def pack_table():
    row = lax.broadcasted_iota(jnp.int32, (4 * WIDE, 1), 0)
    goal = ((row >> 4) & 3) * WIDE + ((row >> 6) & 1) * (WIDE // 2) + (row >> 7) * 16 + (row & 15)
    column = lax.broadcasted_iota(jnp.int32, (4 * WIDE, 4 * WIDE), 1)
    return jnp.where(column == goal, 1.0, 0.0).astype(BF16)


def list_rows(place_ref, count_ref, owner_ref, codes_ref):
    lane = lanes()
    start = pl.multiple_of(place_ref[1] * WIDE, WIDE)
    codes = codes_ref[:, pl.ds(start, WIDE)]
    exponent = codes >> 8
    value = 1.0 + (codes & (CB - 1)).astype(F32) * (1.0 / CB)
    for bit in range(6):
        value = jnp.where(((exponent >> bit) & 1) == 1, value * 2.0 ** (1 << bit), value)
    value = jnp.where(((codes >> 7) & 1) == 1, -value, value)
    rows = []
    owners = jnp.zeros((1, WIDE), F32)
    for o in range(MEETINGS):
        live = jnp.where(place_ref[0] >= o, count_ref[:, o : o + 1], 0)
        rows.append(jnp.where(lane + start < live, value[o : o + 1], 0.0))
        owner = owner_ref[:, o : o + 1]
        owners = jnp.where(lane == o, owner.astype(F32), owners)
    rows = rows + [owners] + [jnp.zeros((1, WIDE), F32)] * (SLAB_ROWS - DATA_ROWS - MEETINGS - 1)
    return jnp.concatenate(rows, axis=0).astype(BF16)


def pack_kernel(
    lists_ref, order_ref, hist_ref, head_ref, taps_ref, table_ref, part_ref, s1_ref, out_ref
):
    rows = split_dot(jnp.concatenate([hist_ref[...], head_ref[...]], axis=1), taps_ref[...]).astype(BF16)
    s0 = (part_ref[...] + jnp.dot(rows, table_ref[...], preferred_element_type=F32)).astype(BF16)
    s1 = s1_ref[...]
    lists = lists_ref[...]
    order = order_ref[...]
    for c in range(WIN // WIDE):
        cols = slice(c * WIDE, (c + 1) * WIDE)
        halves = []
        for g in range(0, 4, 2):
            pieces = [value[n * 32 : (n + 1) * 32, cols] for n in (g, g + 1) for value in (s0, s1)]
            halves.append(jnp.concatenate(pieces, axis=1))
        mixed = jnp.dot(jnp.concatenate(halves, axis=0), order, preferred_element_type=F32)
        upper = lanes() >= WIDE // 2
        for e in range(4):
            first = mixed[:DATA_ROWS, e * WIDE : (e + 1) * WIDE]
            second = mixed[DATA_ROWS:, e * WIDE : (e + 1) * WIDE]
            low = jnp.where(upper, pltpu.roll(second, WIDE // 2, 1), first)
            high = jnp.where(upper, second, pltpu.roll(first, WIDE // 2, 1))
            for d, value in ((c * 8 + e, low), (c * 8 + e + 4, high)):
                out_ref[d, :DATA_ROWS, :] = value.astype(BF16)
                out_ref[d, DATA_ROWS:, :] = lists


def whiten_kernel(slab_ref, out_ref, swapped_ref, last_ref):
    order = order_table()
    both = fold_table(1.0, 1.0)
    both = jnp.concatenate([both, both], axis=0)
    swap = swap_table()
    batch = 4
    for first in range(0, PLANE, batch):
        rows = []
        for p in range(first, first + batch):
            rows.append(jnp.concatenate([slab_ref[p * LAGS + n, :DATA_ROWS, :] for n in range(LAGS)], axis=1))
        values = jnp.dot(jnp.concatenate(rows, axis=0), order, preferred_element_type=F32)
        values = jnp.concatenate([values[:, g * WIDE : (g + 1) * WIDE] for g in range(4)], axis=0)
        high, low = halves_of(values * values)
        power = jnp.dot(jnp.concatenate([high, low], axis=1), both, preferred_element_type=F32)
        whitened = (values * lax.rsqrt(power * (1.0 / WINDOWS) + WATER)).astype(BF16)
        turned = jnp.dot(whitened, swap, preferred_element_type=F32).astype(BF16)
        for n in range(batch):
            for g in range(4):
                at = (g * batch + n) * 32
                out_ref[first + n, g * 32 : (g + 1) * 32, :] = whitened[at : at + 32]
                swapped_ref[first + n, g * 32 : (g + 1) * 32, :] = turned[at : at + 32]
                if first == PLANE - ROUNDS:
                    last_ref[n, g * 32 : (g + 1) * 32, :] = whitened[at : at + 32]


def chosen_kernel(slab_ref, out_ref, owner_ref):
    row = lax.broadcasted_iota(jnp.int32, (CB, PCAP), 0).astype(F32)

    def one(p, carry):
        value = jnp.concatenate([slab_ref[p * LAGS + n, DATA_ROWS:, :] for n in range(LAGS)], axis=1).astype(F32)
        owner_ref[pl.ds(p, 1), :] = value[MEETINGS : MEETINGS + 1, :WIDE].astype(jnp.int32)
        odd = jnp.where(value < 0.0, 1.0, 0.0)
        size = jnp.abs(value)
        live = size > 0.0
        exponent = jnp.zeros(value.shape, F32)
        for bit in (5, 4, 3, 2, 1, 0):
            large = size >= 2.0 ** (1 << bit)
            size = jnp.where(large, size * 2.0 ** -(1 << bit), size)
            exponent = jnp.where(large, exponent + 2.0**bit, exponent)
        first = jnp.where(live, 2.0 * exponent + odd, -1.0)
        second = (size - 1.0) * CB
        for o in range(MEETINGS):
            pick_first = jnp.where(row == first[o : o + 1], 1.0, 0.0).astype(BF16)
            pick_second = jnp.where(row == second[o : o + 1], 1.0, 0.0).astype(BF16)
            chosen = lax.dot_general(pick_first, pick_second, (((1,), (1,)), ((), ())), preferred_element_type=F32)
            out_ref[p, o] = chosen.astype(BF16)
        return carry

    lax.fori_loop(0, PLANE, one, 0, unroll=16)


def fill_bins(bins_ref):
    spread = lax.broadcasted_iota(jnp.int32, (CB, CB), 1) - lax.broadcasted_iota(jnp.int32, (CB, CB), 0)
    at = 0
    for o, k, lo, hi in SPANS:
        distance = spread[lo:hi] + CB * o
        inside = (distance >= BINW * k) & (distance < BINW * (k + 1))
        bins_ref[at : at + hi - lo, :] = jnp.where(inside, 1.0, 0.0).astype(BF16)
        at += hi - lo


def meet(out_ref, owner_ref, bins_ref, chosen_ref, at_block, block, partners, p):
    row_id = lax.broadcasted_iota(jnp.int32, (NBIN, WIDE), 0)
    at = 0
    pieces = []
    for o, _, lo, hi in SPANS:
        pieces.append(chosen_ref[at_block, o, lo:hi, :] * bins_ref[at : at + hi - lo, :])
        at += hi - lo
    mixed = jnp.dot(jnp.concatenate(pieces, axis=0), block, preferred_element_type=F32)
    at = 0
    real, imag = [], []
    for o in range(MEETINGS):
        straight = partners[o][0].astype(F32)
        swapped = partners[o][1].astype(F32)
        for k, lo, hi in LEVELS[o]:
            part = mixed[at : at + hi - lo]
            at += hi - lo
            dims = ((hi - lo) // 8, 8, WIDE)
            real.append(jnp.sum((straight[lo:hi] * part).reshape(dims), axis=0))
            imag.append(jnp.sum((swapped[lo:hi] * part).reshape(dims), axis=0))
    at = 0
    for o in range(MEETINGS):
        re = jnp.zeros((NBIN, WIDE), F32)
        im = jnp.zeros((NBIN, WIDE), F32)
        for k, _, _ in LEVELS[o]:
            re = jnp.where(row_id == k, jnp.sum(real[at], axis=0, keepdims=True), re)
            im = jnp.where(row_id == k, jnp.sum(imag[at], axis=0, keepdims=True), im)
            at += 1
        found = jnp.where(real_lanes(), fold(re), fold(im))
        spot = owner_ref[p, o]
        out_ref[spot] = out_ref[spot] + found


def meetings_kernel(
    owner_ref, chosen_ref, group_ref, swapped_ref, below_ref, out_ref, bins_ref, all_ref, turned_ref, total_ref
):
    total_ref[...] = jnp.zeros(total_ref.shape, F32)
    fill_bins(bins_ref)
    swap = swap_table()
    for n in range(ROUNDS):
        all_ref[n] = below_ref[n]
        turned_ref[n] = jnp.dot(below_ref[n], swap, preferred_element_type=F32).astype(BF16)
    all_ref[ROUNDS:] = group_ref[...]
    turned_ref[ROUNDS:] = swapped_ref[...]

    def one(p, carry):
        partners = [(all_ref[p + ROUNDS - o], turned_ref[p + ROUNDS - o]) for o in range(MEETINGS)]
        meet(total_ref, owner_ref, bins_ref, chosen_ref, p, group_ref[p], partners, p)
        return carry

    lax.fori_loop(0, PLANE, one, 0, unroll=16)
    row_id = lax.broadcasted_iota(jnp.int32, (NBIN, WIDE), 0)
    own_piece = (lanes() >> 4) == row_id
    for n in range(0, ROWS * PLANE, 2):
        pair = []
        for owner in (n, n + 1):
            value = jnp.where(own_piece, total_ref[owner], 0.0)
            pair.append(jnp.sum(value, axis=0, keepdims=True))
        out_ref[n * LAGS : (n + 2) * LAGS, :] = jnp.where(row_id < LAGS, pair[0], pair[1])


def lag_kernel(lag_ref, parts_ref, table_ref, out_ref, order_ref):
    lane = lanes()
    sign = jnp.where(real_lanes(), -1.0, 1.0)
    step = (lane * (lag_ref[0] + 2)) & 3
    along = jnp.where(step == 0, 1.0, 0.0) - jnp.where(step == 2, 1.0, 0.0)
    across = sign * (jnp.where(step == 1, 1.0, 0.0) - jnp.where(step == 3, 1.0, 0.0))
    pieces = []
    for n in range(8):
        value = parts_ref[pl.ds(n, 8, stride=8), :]
        for y in range(1, ROWS):
            value = value + parts_ref[pl.ds(y * PLANE * LAGS + n, 8, stride=8), :]
        pieces.append(value)
    for k, value in enumerate(transpose_pieces(pieces, 2 * BAND)):
        swapped = jnp.where(real_lanes(), pltpu.roll(value, WIDE - BAND, 1), pltpu.roll(value, BAND, 1))
        order_ref[pl.ds(k, 8, stride=8), :] = value * along + swapped * across
    columns = [order_ref[n * NBIN : (n + 1) * NBIN, :] for n in range(8)]
    out_ref[0] = split_dot(jnp.concatenate(columns, axis=1), table_ref[...])


def early_part(place, *inputs):
    operands = [pltpu.with_memory_space_constraint(value, pltpu.HBM) for value in inputs]
    return pl.pallas_call(
        early_kernel,
        out_shape=(
            shape((CB, WIN), BF16),
            shape((CB, WIN), F32),
            shape((CB, TAPS), F32),
            shape((2 * TAPS, 2 * TAPS), BF16),
            shape((TAPS, WIN), BF16),
            shape((SLAB_ROWS - DATA_ROWS, WIDE), BF16),
            shape((4 * WIDE, 4 * WIDE), BF16),
        ),
        in_specs=[pl.BlockSpec(memory_space=pltpu.SMEM)] + [pl.BlockSpec(memory_space=pltpu.HBM)] * 6,
        out_specs=[pl.BlockSpec(memory_space=pltpu.VMEM)] * 7,
        scratch_shapes=[
            pltpu.VMEM((CB, 2 * WIN), F32),
            pltpu.VMEM((2 * TAPS, 2 * TAPS), BF16),
            pltpu.VMEM((HALF, WIN), BF16),
            pltpu.VMEM((1, MEETINGS), jnp.int32),
            pltpu.VMEM((1, MEETINGS), jnp.int32),
            pltpu.VMEM((MEETINGS, PCAP), jnp.int32),
            pltpu.SemaphoreType.DMA((7,)),
        ],
        compiler_params=pltpu.CompilerParams(vmem_limit_bytes=VMEM_LIMIT),
    )(place, *operands)


def row_below(blocks):
    return lax.ppermute(blocks, "row", [(i, i + 1) for i in range(ROWS - 1)])


def middle(slabs, send):
    blocks = (PLANE, CB, WIDE)
    group, swapped, last = call(
        whiten_kernel, (shape(blocks, BF16), shape(blocks, BF16), shape((ROUNDS, CB, WIDE), BF16)), slabs
    )
    below = send(last)
    chosen, owners = call(
        chosen_kernel, (shape((PLANE, MEETINGS, CB, CB), BF16), shape((PLANE, WIDE), jnp.int32)), slabs
    )
    sums_shape = (ROWS * PLANE, NBIN, WIDE)
    more = pltpu.VMEM((PLANE + ROUNDS, CB, WIDE), BF16)
    return call(
        meetings_kernel,
        shape((ROWS * PLANE * LAGS, WIDE), F32),
        owners,
        chosen,
        group,
        swapped,
        below,
        smem=(0,),
        scratch=(pltpu.VMEM((SPAN_ROWS, CB), BF16), more, more, pltpu.VMEM(sums_shape, F32)),
    )


def body(traces, owner_map, pair_codes, pair_count):
    blk = (lax.axis_index("row") * PLANE + lax.axis_index("plane")).astype(jnp.int32)
    lag = lax.axis_index("lag").astype(jnp.int32)
    taps = jnp.asarray(filter_table())
    table = jnp.asarray(transform_table())

    history = lax.ppermute(traces[:, -TAPS:], "lag", [(i, i + 1) for i in range(3)])

    spectra1, part, head, taps, table, lists, order = early_part(
        jnp.stack([blk, lag]),
        traces,
        taps,
        table,
        pair_count.reshape(1, MEETINGS),
        owner_map.reshape(1, MEETINGS),
        pair_codes,
    )
    slabs = call(
        pack_kernel,
        shape((PLANE * LAGS, SLAB_ROWS, WIDE), BF16),
        lists,
        order,
        history,
        head,
        taps,
        table,
        part,
        spectra1,
    )
    slabs = lax.all_to_all(slabs, ("plane", "lag"), 0, 0, tiled=True)
    sums = middle(slabs, row_below)
    parts = lax.all_to_all(sums, ("row", "plane", "lag"), 0, 0, tiled=True)
    return call(
        lag_kernel,
        shape((1, NBIN, LANES), F32),
        lag.reshape(1),
        parts,
        jnp.asarray(inverse_table()),
        smem=(0,),
        scratch=(pltpu.VMEM((8 * NBIN, WIDE), F32),),
    )


def solution(mesh):
    split = Mesh(mesh.devices.reshape(ROWS, PLANE, 4), ("row", "plane", "lag"))
    owned = ("row", "plane")
    return jax.shard_map(
        body,
        mesh=split,
        in_specs=(P(owned, "lag"), P(None, owned), P(None, owned), P(None, owned)),
        out_specs=P(owned, None, "lag"),
        check_vma=False,
    )
```

```python
import math

import jax
import jax.numpy as jnp
import numpy as np
from jax import lax
from jax.experimental import pallas as pl
from jax.experimental.pallas import tpu as pltpu
from jax.sharding import Mesh
from jax.sharding import PartitionSpec as P

CB = 128
WIN = 1024
HALF = 512
NF = 512
TAPS = 128
NBIN = 8
BINW = 80
ROUNDS = 4
MEETINGS = 5
PCAP = 512
WINDOWS = 8
LANES = 256
PLANE = 16
ROWS = 4
LAGS = 4
WIDE = 128
BAND = 8
DATA_ROWS = 32
SLAB_ROWS = 40

BAND_LOW = 0.02
BAND_HIGH = 0.48
WATER = 0.1

F32 = jnp.float32
BF16 = jnp.bfloat16
VMEM_LIMIT = 16 * 1024 * 1024


def level_rows(o):
    found = []
    for k in range(NBIN):
        pairs = [
            i
            for i in range(CB)
            for j in range(CB)
            if (o > 0 or i < j) and (CB * o + j - i) // BINW == k
        ]
        if pairs:
            found.append((k, min(pairs) // 16 * 16, max(pairs) // 16 * 16 + 16))
    return tuple(found)


LEVELS = tuple(level_rows(o) for o in range(MEETINGS))
SPANS = tuple((o, k, lo, hi) for o in range(MEETINGS) for k, lo, hi in LEVELS[o])
SPAN_ROWS = sum(hi - lo for _, _, lo, hi in SPANS)


def two_terms(table):
    high = table.astype(jnp.bfloat16)
    low = (table - high.astype(np.float32)).astype(jnp.bfloat16)
    return np.concatenate([high, low], axis=1)


def filter_table():
    k = np.arange(TAPS, dtype=np.float64)
    m = k - (TAPS - 1) / 2.0
    ideal = 2 * BAND_HIGH * np.sinc(2 * BAND_HIGH * m) - 2 * BAND_LOW * np.sinc(2 * BAND_LOW * m)
    taps = ideal * (0.5 - 0.5 * np.cos(2 * np.pi * (k + 0.5) / TAPS))
    lagged = np.arange(TAPS)[None, :] - np.arange(2 * TAPS)[:, None] + TAPS
    inside = (lagged >= 0) & (lagged < TAPS)
    return two_terms(np.where(inside, taps[np.clip(lagged, 0, TAPS - 1)], 0.0).astype(np.float32))


def column_order():
    column = np.arange(WIN)
    return column // (2 * BAND) * BAND + column % BAND, column // BAND % 2 == 1


def transform_table():
    freq, is_imag = column_order()
    angle = (np.arange(HALF)[:, None] * freq[None, :] % WIN) * (2 * np.pi / WIN)
    return (np.where(is_imag[None, :], -np.sin(angle), np.cos(angle)) / math.sqrt(WIN)).astype(jnp.bfloat16)


def inverse_table():
    freq, is_imag = column_order()
    angle = (freq[:, None] * np.arange(LANES)[None, :] % WIN) * (2 * np.pi / WIN)
    weight = np.where(freq == 0, 1.0, 2.0)[:, None] / (WINDOWS * math.sqrt(WIN))
    return two_terms((weight * np.where(is_imag[:, None], -np.sin(angle), np.cos(angle))).astype(np.float32))


def call(kernel, out_shape, *args, smem=(), aliases=None, scratch=()):
    specs = [
        pl.BlockSpec(memory_space=pltpu.SMEM) if n in smem else pl.BlockSpec(memory_space=pltpu.VMEM)
        for n in range(len(args))
    ]
    many = isinstance(out_shape, (tuple, list))
    out_specs = [pl.BlockSpec(memory_space=pltpu.VMEM)] * len(out_shape) if many else pl.BlockSpec(memory_space=pltpu.VMEM)
    return pl.pallas_call(
        kernel,
        out_shape=out_shape,
        in_specs=specs,
        out_specs=out_specs,
        input_output_aliases=aliases or {},
        scratch_shapes=list(scratch),
        compiler_params=pltpu.CompilerParams(vmem_limit_bytes=VMEM_LIMIT),
    )(*args)


def shape(dims, dtype):
    return jax.ShapeDtypeStruct(dims, dtype)


def lanes():
    return lax.broadcasted_iota(jnp.int32, (1, WIDE), 1)


def real_lanes():
    return (lanes() & BAND) == 0


def fold(values):
    for step in (BAND, 2 * BAND, 4 * BAND, 8 * BAND):
        values = values + pltpu.roll(values, step, 1)
    return values


def fold_table(real, imag):
    row = lax.broadcasted_iota(jnp.int32, (WIDE, WIDE), 0)
    column = lax.broadcasted_iota(jnp.int32, (WIDE, WIDE), 1)
    same = ((row ^ column) & (BAND - 1)) == 0
    asked = jnp.where((column & BAND) == 0, real, imag)
    return jnp.where(same, asked, 0.0).astype(BF16)


def swap_table():
    row = lax.broadcasted_iota(jnp.int32, (WIDE, WIDE), 0)
    column = lax.broadcasted_iota(jnp.int32, (WIDE, WIDE), 1)
    value = jnp.where((column & BAND) == 0, -1.0, 1.0)
    return jnp.where(row == (column ^ BAND), value, 0.0).astype(BF16)


def order_table():
    row = lax.broadcasted_iota(jnp.int32, (4 * WIDE, 1), 0)
    goal = ((row >> 5) & 3) * WIDE + (row >> 7) * 32 + (row & 31)
    column = lax.broadcasted_iota(jnp.int32, (4 * WIDE, 4 * WIDE), 1)
    return jnp.where(column == goal, 1.0, 0.0).astype(BF16)


def halves_of(values):
    high = values.astype(BF16)
    return high, (values - high.astype(F32)).astype(BF16)


def split_dot(values, table):
    high, low = halves_of(values)
    count, width = values.shape[0], table.shape[1] // 2
    out = jnp.dot(jnp.concatenate([high, low], axis=0), table, preferred_element_type=F32)
    small = out[count:, width:] + (out[count:, :width] + out[:count, width:])
    return small + out[:count, :width]


def transpose_pieces(arrays, width):
    bit = 1
    while bit < len(arrays):
        upper = (lanes() & (bit * width)) != 0
        out = list(arrays)
        for q in range(len(arrays)):
            if q & bit:
                continue
            a, b = arrays[q], arrays[q | bit]
            out[q] = jnp.where(upper, pltpu.roll(b, bit * width, 1), a)
            out[q | bit] = jnp.where(upper, b, pltpu.roll(a, WIDE - bit * width, 1))
        arrays = out
        bit *= 2
    return arrays


def turns():
    column = lax.broadcasted_iota(jnp.int32, (1, WIN), 1)
    return jnp.where(column % 2 == 0, 1.0, -1.0).astype(F32)


def early_kernel(
    place_ref, traces_ref, taps_ref, table_ref, counts_in, owners_in, codes_in,
    s1_ref, part_ref, head_ref, taps_out, table_out, lists_ref, order_ref, bins_out,
    x_ref, h_ref, d_ref, count_ref, owner_ref, codes_ref, sems,
):
    late = WIN - TAPS
    copies = [
        pltpu.make_async_copy(traces_ref.at[:, late:], x_ref.at[:, late:], sems.at[0]),
        pltpu.make_async_copy(taps_ref, h_ref, sems.at[1]),
        pltpu.make_async_copy(table_ref, d_ref, sems.at[2]),
        pltpu.make_async_copy(traces_ref.at[:, :late], x_ref.at[:, :late], sems.at[3]),
        pltpu.make_async_copy(counts_in, count_ref, sems.at[4]),
        pltpu.make_async_copy(owners_in, owner_ref, sems.at[5]),
        pltpu.make_async_copy(codes_in, codes_ref, sems.at[6]),
    ]
    for copy in copies:
        copy.start()
    order_ref[...] = pack_table()
    fill_bins(bins_out)

    def filtered(first, last):
        pairs = [x_ref[:, (t - 1) * TAPS : (t + 1) * TAPS] for t in range(first, last)]
        rows = split_dot(jnp.concatenate(pairs, axis=0), h_ref[...]).astype(BF16)
        return [rows[n * CB : (n + 1) * CB] for n in range(last - first)]

    copies[0].wait()
    copies[1].wait()
    tiles = filtered(8, 16)
    copies[3].wait()
    tiles = [jnp.zeros((CB, TAPS), BF16)] + filtered(1, 8) + tiles
    copies[2].wait()
    rows = [jnp.concatenate(tiles[n : n + 4], axis=1) for n in (0, 4, 8, 12)]
    first = jnp.dot(jnp.concatenate(rows[0::2], axis=0), d_ref[...], preferred_element_type=F32)
    second = jnp.dot(jnp.concatenate(rows[1::2], axis=0), d_ref[...], preferred_element_type=F32)
    both = first + turns() * second
    part_ref[...] = both[:CB]
    s1_ref[...] = both[CB:].astype(BF16)
    head_ref[...] = x_ref[:, :TAPS]
    taps_out[...] = h_ref[...]
    table_out[...] = d_ref[:TAPS, :]
    for copy in copies[4:]:
        copy.wait()
    lists_ref[...] = list_rows(place_ref, count_ref, owner_ref, codes_ref)


def pack_table():
    row = lax.broadcasted_iota(jnp.int32, (4 * WIDE, 1), 0)
    goal = ((row >> 4) & 3) * WIDE + ((row >> 6) & 1) * (WIDE // 2) + (row >> 7) * 16 + (row & 15)
    column = lax.broadcasted_iota(jnp.int32, (4 * WIDE, 4 * WIDE), 1)
    return jnp.where(column == goal, 1.0, 0.0).astype(BF16)


def list_rows(place_ref, count_ref, owner_ref, codes_ref):
    lane = lanes()
    start = pl.multiple_of(place_ref[1] * WIDE, WIDE)
    codes = codes_ref[:, pl.ds(start, WIDE)]
    exponent = codes >> 8
    value = 1.0 + (codes & (CB - 1)).astype(F32) * (1.0 / CB)
    for bit in range(6):
        value = jnp.where(((exponent >> bit) & 1) == 1, value * 2.0 ** (1 << bit), value)
    value = jnp.where(((codes >> 7) & 1) == 1, -value, value)
    rows = []
    owners = jnp.zeros((1, WIDE), F32)
    for o in range(MEETINGS):
        live = jnp.where(place_ref[0] >= o, count_ref[:, o : o + 1], 0)
        rows.append(jnp.where(lane + start < live, value[o : o + 1], 0.0))
        owner = owner_ref[:, o : o + 1]
        owners = jnp.where(lane == o, owner.astype(F32), owners)
    rows = rows + [owners] + [jnp.zeros((1, WIDE), F32)] * (SLAB_ROWS - DATA_ROWS - MEETINGS - 1)
    return jnp.concatenate(rows, axis=0).astype(BF16)


def pack_kernel(
    lists_ref, order_ref, hist_ref, head_ref, taps_ref, table_ref, part_ref, s1_ref, out_ref
):
    rows = split_dot(jnp.concatenate([hist_ref[...], head_ref[...]], axis=1), taps_ref[...]).astype(BF16)
    s0 = (part_ref[...] + jnp.dot(rows, table_ref[...], preferred_element_type=F32)).astype(BF16)
    s1 = s1_ref[...]
    lists = lists_ref[...]
    order = order_ref[...]
    for c in range(WIN // WIDE):
        cols = slice(c * WIDE, (c + 1) * WIDE)
        halves = []
        for g in range(0, 4, 2):
            pieces = [value[n * 32 : (n + 1) * 32, cols] for n in (g, g + 1) for value in (s0, s1)]
            halves.append(jnp.concatenate(pieces, axis=1))
        mixed = jnp.dot(jnp.concatenate(halves, axis=0), order, preferred_element_type=F32)
        upper = lanes() >= WIDE // 2
        for e in range(4):
            first = mixed[:DATA_ROWS, e * WIDE : (e + 1) * WIDE]
            second = mixed[DATA_ROWS:, e * WIDE : (e + 1) * WIDE]
            low = jnp.where(upper, pltpu.roll(second, WIDE // 2, 1), first)
            high = jnp.where(upper, second, pltpu.roll(first, WIDE // 2, 1))
            for d, value in ((c * 8 + e, low), (c * 8 + e + 4, high)):
                out_ref[d, :DATA_ROWS, :] = value.astype(BF16)
                out_ref[d, DATA_ROWS:, :] = lists


def whiten_kernel(slab_ref, out_ref, swapped_ref, last_ref):
    order = order_table()
    both = fold_table(1.0, 1.0)
    both = jnp.concatenate([both, both], axis=0)
    swap = swap_table()
    batch = 4
    for first in range(0, PLANE, batch):
        rows = []
        for p in range(first, first + batch):
            rows.append(jnp.concatenate([slab_ref[p * LAGS + n, :DATA_ROWS, :] for n in range(LAGS)], axis=1))
        values = jnp.dot(jnp.concatenate(rows, axis=0), order, preferred_element_type=F32)
        values = jnp.concatenate([values[:, g * WIDE : (g + 1) * WIDE] for g in range(4)], axis=0)
        high, low = halves_of(values * values)
        power = jnp.dot(jnp.concatenate([high, low], axis=1), both, preferred_element_type=F32)
        whitened = (values * lax.rsqrt(power * (1.0 / WINDOWS) + WATER)).astype(BF16)
        turned = jnp.dot(whitened, swap, preferred_element_type=F32).astype(BF16)
        for n in range(batch):
            for g in range(4):
                at = (g * batch + n) * 32
                out_ref[first + n, g * 32 : (g + 1) * 32, :] = whitened[at : at + 32]
                swapped_ref[first + n, g * 32 : (g + 1) * 32, :] = turned[at : at + 32]
                if first == PLANE - ROUNDS:
                    last_ref[n, g * 32 : (g + 1) * 32, :] = whitened[at : at + 32]


def chosen_kernel(slab_ref, out_ref, owner_ref):
    row = lax.broadcasted_iota(jnp.int32, (CB, PCAP), 0).astype(F32)

    def one(p, carry):
        value = jnp.concatenate([slab_ref[p * LAGS + n, DATA_ROWS:, :] for n in range(LAGS)], axis=1).astype(F32)
        owner_ref[pl.ds(p, 1), :] = value[MEETINGS : MEETINGS + 1, :WIDE].astype(jnp.int32)
        odd = jnp.where(value < 0.0, 1.0, 0.0)
        size = jnp.abs(value)
        live = size > 0.0
        exponent = jnp.zeros(value.shape, F32)
        for bit in (5, 4, 3, 2, 1, 0):
            large = size >= 2.0 ** (1 << bit)
            size = jnp.where(large, size * 2.0 ** -(1 << bit), size)
            exponent = jnp.where(large, exponent + 2.0**bit, exponent)
        first = jnp.where(live, 2.0 * exponent + odd, -1.0)
        second = (size - 1.0) * CB
        for o in range(MEETINGS):
            pick_first = jnp.where(row == first[o : o + 1], 1.0, 0.0).astype(BF16)
            pick_second = jnp.where(row == second[o : o + 1], 1.0, 0.0).astype(BF16)
            chosen = lax.dot_general(pick_first, pick_second, (((1,), (1,)), ((), ())), preferred_element_type=F32)
            out_ref[p, o] = chosen.astype(BF16)
        return carry

    lax.fori_loop(0, PLANE, one, 0, unroll=16)


def fill_bins(bins_ref):
    spread = lax.broadcasted_iota(jnp.int32, (CB, CB), 1) - lax.broadcasted_iota(jnp.int32, (CB, CB), 0)
    at = 0
    for o, k, lo, hi in SPANS:
        distance = spread[lo:hi] + CB * o
        inside = (distance >= BINW * k) & (distance < BINW * (k + 1))
        bins_ref[at : at + hi - lo, :] = jnp.where(inside, 1.0, 0.0).astype(BF16)
        at += hi - lo


def meet(out_ref, owner_ref, bins_ref, chosen_ref, at_block, block, partners, p):
    row_id = lax.broadcasted_iota(jnp.int32, (NBIN, WIDE), 0)
    at = 0
    pieces = []
    for o, _, lo, hi in SPANS:
        pieces.append(chosen_ref[at_block, o, lo:hi, :] * bins_ref[at : at + hi - lo, :])
        at += hi - lo
    mixed = jnp.dot(jnp.concatenate(pieces, axis=0), block, preferred_element_type=F32)
    at = 0
    real, imag = [], []
    for o in range(MEETINGS):
        straight = partners[o][0].astype(F32)
        swapped = partners[o][1].astype(F32)
        for k, lo, hi in LEVELS[o]:
            part = mixed[at : at + hi - lo]
            at += hi - lo
            dims = ((hi - lo) // 8, 8, WIDE)
            real.append(jnp.sum((straight[lo:hi] * part).reshape(dims), axis=0))
            imag.append(jnp.sum((swapped[lo:hi] * part).reshape(dims), axis=0))
    at = 0
    for o in range(MEETINGS):
        re = jnp.zeros((NBIN, WIDE), F32)
        im = jnp.zeros((NBIN, WIDE), F32)
        for k, _, _ in LEVELS[o]:
            re = jnp.where(row_id == k, jnp.sum(real[at], axis=0, keepdims=True), re)
            im = jnp.where(row_id == k, jnp.sum(imag[at], axis=0, keepdims=True), im)
            at += 1
        found = jnp.where(real_lanes(), fold(re), fold(im))
        spot = owner_ref[p, o]
        out_ref[spot] = out_ref[spot] + found


def meetings_kernel(
    owner_ref, chosen_ref, group_ref, swapped_ref, below_ref, bins_ref, out_ref, all_ref, turned_ref, total_ref
):
    total_ref[...] = jnp.zeros(total_ref.shape, F32)
    swap = swap_table()
    for n in range(ROUNDS):
        all_ref[n] = below_ref[n]
        turned_ref[n] = jnp.dot(below_ref[n], swap, preferred_element_type=F32).astype(BF16)
    all_ref[ROUNDS:] = group_ref[...]
    turned_ref[ROUNDS:] = swapped_ref[...]

    def one(p, carry):
        partners = [(all_ref[p + ROUNDS - o], turned_ref[p + ROUNDS - o]) for o in range(MEETINGS)]
        meet(total_ref, owner_ref, bins_ref, chosen_ref, p, group_ref[p], partners, p)
        return carry

    lax.fori_loop(0, PLANE, one, 0, unroll=16)
    row_id = lax.broadcasted_iota(jnp.int32, (NBIN, WIDE), 0)
    own_piece = (lanes() >> 4) == row_id
    for n in range(0, ROWS * PLANE, 2):
        pair = []
        for owner in (n, n + 1):
            value = jnp.where(own_piece, total_ref[owner], 0.0)
            pair.append(jnp.sum(value, axis=0, keepdims=True))
        out_ref[n * LAGS : (n + 2) * LAGS, :] = jnp.where(row_id < LAGS, pair[0], pair[1])


def lag_kernel(lag_ref, parts_ref, table_ref, out_ref, order_ref):
    lane = lanes()
    sign = jnp.where(real_lanes(), -1.0, 1.0)
    step = (lane * (lag_ref[0] + 2)) & 3
    along = jnp.where(step == 0, 1.0, 0.0) - jnp.where(step == 2, 1.0, 0.0)
    across = sign * (jnp.where(step == 1, 1.0, 0.0) - jnp.where(step == 3, 1.0, 0.0))
    pieces = []
    for n in range(8):
        value = parts_ref[pl.ds(n, 8, stride=8), :]
        for y in range(1, ROWS):
            value = value + parts_ref[pl.ds(y * PLANE * LAGS + n, 8, stride=8), :]
        pieces.append(value)
    for k, value in enumerate(transpose_pieces(pieces, 2 * BAND)):
        swapped = jnp.where(real_lanes(), pltpu.roll(value, WIDE - BAND, 1), pltpu.roll(value, BAND, 1))
        order_ref[pl.ds(k, 8, stride=8), :] = value * along + swapped * across
    columns = [order_ref[n * NBIN : (n + 1) * NBIN, :] for n in range(8)]
    out_ref[0] = split_dot(jnp.concatenate(columns, axis=1), table_ref[...])


def early_part(place, *inputs):
    operands = [pltpu.with_memory_space_constraint(value, pltpu.HBM) for value in inputs]
    return pl.pallas_call(
        early_kernel,
        out_shape=(
            shape((CB, WIN), BF16),
            shape((CB, WIN), F32),
            shape((CB, TAPS), F32),
            shape((2 * TAPS, 2 * TAPS), BF16),
            shape((TAPS, WIN), BF16),
            shape((SLAB_ROWS - DATA_ROWS, WIDE), BF16),
            shape((4 * WIDE, 4 * WIDE), BF16),
            shape((SPAN_ROWS, CB), BF16),
        ),
        in_specs=[pl.BlockSpec(memory_space=pltpu.SMEM)] + [pl.BlockSpec(memory_space=pltpu.HBM)] * 6,
        out_specs=[pl.BlockSpec(memory_space=pltpu.VMEM)] * 8,
        scratch_shapes=[
            pltpu.VMEM((CB, 2 * WIN), F32),
            pltpu.VMEM((2 * TAPS, 2 * TAPS), BF16),
            pltpu.VMEM((HALF, WIN), BF16),
            pltpu.VMEM((1, MEETINGS), jnp.int32),
            pltpu.VMEM((1, MEETINGS), jnp.int32),
            pltpu.VMEM((MEETINGS, PCAP), jnp.int32),
            pltpu.SemaphoreType.DMA((7,)),
        ],
        compiler_params=pltpu.CompilerParams(vmem_limit_bytes=VMEM_LIMIT),
    )(place, *operands)


def row_below(blocks):
    return lax.ppermute(blocks, "row", [(i, i + 1) for i in range(ROWS - 1)])


def middle(slabs, send, bins):
    blocks = (PLANE, CB, WIDE)
    group, swapped, last = call(
        whiten_kernel, (shape(blocks, BF16), shape(blocks, BF16), shape((ROUNDS, CB, WIDE), BF16)), slabs
    )
    below = send(last)
    chosen, owners = call(
        chosen_kernel, (shape((PLANE, MEETINGS, CB, CB), BF16), shape((PLANE, WIDE), jnp.int32)), slabs
    )
    sums_shape = (ROWS * PLANE, NBIN, WIDE)
    more = pltpu.VMEM((PLANE + ROUNDS, CB, WIDE), BF16)
    return call(
        meetings_kernel,
        shape((ROWS * PLANE * LAGS, WIDE), F32),
        owners,
        chosen,
        group,
        swapped,
        below,
        bins,
        smem=(0,),
        scratch=(more, more, pltpu.VMEM(sums_shape, F32)),
    )


def body(traces, owner_map, pair_codes, pair_count):
    blk = (lax.axis_index("row") * PLANE + lax.axis_index("plane")).astype(jnp.int32)
    lag = lax.axis_index("lag").astype(jnp.int32)
    taps = jnp.asarray(filter_table())
    table = jnp.asarray(transform_table())

    history = lax.ppermute(traces[:, -TAPS:], "lag", [(i, i + 1) for i in range(3)])

    spectra1, part, head, taps, table, lists, order, bins = early_part(
        jnp.stack([blk, lag]),
        traces,
        taps,
        table,
        pair_count.reshape(1, MEETINGS),
        owner_map.reshape(1, MEETINGS),
        pair_codes,
    )
    slabs = call(
        pack_kernel,
        shape((PLANE * LAGS, SLAB_ROWS, WIDE), BF16),
        lists,
        order,
        history,
        head,
        taps,
        table,
        part,
        spectra1,
    )
    slabs = lax.all_to_all(slabs, ("plane", "lag"), 0, 0, tiled=True)
    sums = middle(slabs, row_below, bins)
    parts = lax.all_to_all(sums, ("row", "plane", "lag"), 0, 0, tiled=True)
    return call(
        lag_kernel,
        shape((1, NBIN, LANES), F32),
        lag.reshape(1),
        parts,
        jnp.asarray(inverse_table()),
        smem=(0,),
        scratch=(pltpu.VMEM((8 * NBIN, WIDE), F32),),
    )


def solution(mesh):
    split = Mesh(mesh.devices.reshape(ROWS, PLANE, 4), ("row", "plane", "lag"))
    owned = ("row", "plane")
    return jax.shard_map(
        body,
        mesh=split,
        in_specs=(P(owned, "lag"), P(None, owned), P(None, owned), P(None, owned)),
        out_specs=P(owned, None, "lag"),
        check_vma=False,
    )
```
